32 devices in a mesh: dp: 8 (over y, x, core), tensor: 4 (over z).
Axes of the slice: x: 2, y: 2, z: 4, core: 2. Of those that a mesh axis runs over, the one named last changes fastest.
Arguments:
- hidden: bfloat16 [8, 1280, 1120], P('dp', 'tensor'), may hold values from -6 to 6
- segment_ids: int32 [8, 1280], P('dp'), may hold values from 0 to 15, as said below
- lengths: int32 [8], P('dp'), may hold values from 640 to 1280, as said below
- norm1_gain: float32 [1120], replicated, may hold values from 0.25 to 1.75
- norm1_shift: float32 [1120], replicated, may hold values from -4 to 4
- qkv_weight: bfloat16 [3, 1120, 1120], P(None, None, 'tensor'), may hold values from -0.1875 to 0.1875
- qv_bias: float32 [2, 1120], P(None, 'tensor'), may hold values from -4 to 4
- out_weight: bfloat16 [1120, 1120], P('tensor'), may hold values from -1 to 1
- out_bias: float32 [1120], replicated, may hold values from -4 to 4
- norm2_gain: float32 [1120], replicated, may hold values from 0.25 to 1.75
- norm2_shift: float32 [1120], replicated, may hold values from -4 to 4
- up_weight: bfloat16 [1120, 4480], P(None, 'tensor'), may hold values from -0.1875 to 0.1875
- up_bias: float32 [4480], P('tensor'), may hold values from -4 to 4
- down_weight: bfloat16 [4480, 1120], P('tensor'), may hold values from -0.125 to 0.125
- down_bias: float32 [1120], replicated, may hold values from -4 to 4
- cotangent: bfloat16 [8, 1280, 1120], P('dp', 'tensor'), may hold values from -6 to 6
Outputs:
- output: bfloat16 [8, 1280, 1120], P('dp', 'tensor')
- input_grad: bfloat16 [8, 1280, 1120], P('dp', 'tensor')
- norm1_gain_grad: float32 [1120], replicated
- norm1_shift_grad: float32 [1120], replicated
- qkv_weight_grad: float32 [3, 1120, 1120], P(None, None, 'tensor')
- qv_bias_grad: float32 [2, 1120], P(None, 'tensor')
- out_weight_grad: float32 [1120, 1120], P('tensor')
- out_bias_grad: float32 [1120], replicated
- norm2_gain_grad: float32 [1120], replicated
- norm2_shift_grad: float32 [1120], replicated
- up_weight_grad: float32 [1120, 4480], P(None, 'tensor')
- up_bias_grad: float32 [4480], P('tensor')
- down_weight_grad: float32 [4480, 1120], P('tensor')
- down_bias_grad: float32 [1120], replicated
The draws below stay inside these ranges and needn't reach their ends.
Inputs may be any that keep to these rules, and one draw needn't show every extreme that they name: `segment_ids`: along each row the ids start at 0 and never fall; a cell is a run of equal ids. `lengths`: some row is full and some row holds 640 live tokens.
All inputs are finite; a program needn't handle non-finite values.
Results may differ from the reference program's by a relative error of at most 0.012.
Values may be sent and summed in bfloat16 or wider, within the bound.
A program may use at most 256 MiB of HBM per device.

```python
import jax
import jax.numpy as jnp
from jax import lax

D = 1120
HEADS = 20
HEAD = 56
FF = 4480
SEQ = 1280
ROWS = 8


def draw_segment_ids(key, part):
    starts = jax.random.randint(key, (ROWS, SEQ), 0, max(SEQ // 5, 2)) == 0
    places = jnp.arange(SEQ, dtype=jnp.int32)
    regular = places % (SEQ // 16) == 0
    starts = starts.at[0].set(starts[0] | regular)
    starts = starts.at[:, 0].set(True)
    ids = jnp.cumsum(starts.astype(jnp.int32), axis=1).astype(jnp.int32) - 1
    return jnp.minimum(ids, 15).astype(jnp.int32)


def draw_lengths(key, part):
    counts = jax.random.randint(key, (ROWS,), SEQ // 2, SEQ + 1)
    counts = counts.at[0].set(SEQ)
    counts = counts.at[ROWS - 1].set(SEQ // 2)
    return counts.astype(jnp.int32)


def block_scale(key, dims, shards, smallest, high):
    loudness, own = 1.0, jax.random.fold_in(key, 6)
    for position, blocks in shards:
        steps = jnp.exp(jax.random.uniform(jax.random.fold_in(own, position), (blocks,), jnp.float32, smallest / len(shards), high / len(shards)))
        loudness = loudness * jnp.repeat(steps, dims[position] // blocks).reshape([-1 if axis == position else 1 for axis in range(len(dims))])
    return loudness


def centred(stream_key, extent, scale, limit, shards=(), kind=jnp.bfloat16):
    drawn = scale * jax.random.normal(stream_key, extent, jnp.float32)
    if shards:
        drawn = drawn * block_scale(stream_key, extent, shards, -0.22, 0.18)
    return jnp.clip(drawn, -limit, limit).astype(kind)


def setup_inputs(seed: int = 0) -> dict:
    key_of = jax.random.split(jax.random.key(seed), 17)
    return {
        "hidden": centred(key_of[0], (ROWS, SEQ, D), 1.0, 6.0, ((0, 8), (1, 4))),
        "segment_ids": draw_segment_ids(jax.random.fold_in(key_of[16], 71), 0),
        "lengths": draw_lengths(jax.random.fold_in(key_of[16], 71), 0),
        "norm1_gain": jnp.clip(1.0 + 0.15 * jax.random.normal(key_of[3], (D,), jnp.float32), 0.25, 1.75),
        "norm1_shift": centred(key_of[4], (D,), 0.3, 4.0, (), jnp.float32),
        "qkv_weight": centred(key_of[5], (3, D, D), D ** -0.5, 0.1875, ((2, 4),)),
        "qv_bias": centred(key_of[6], (2, D), 0.3, 4.0, ((1, 4),), jnp.float32),
        "out_weight": centred(key_of[7], (D, D), (D // 32) ** -0.5, 1.0, ((0, 4),)),
        "out_bias": centred(key_of[8], (D,), 0.3, 4.0, (), jnp.float32),
        "norm2_gain": jnp.clip(1.0 + 0.15 * jax.random.normal(key_of[9], (D,), jnp.float32), 0.25, 1.75),
        "norm2_shift": centred(key_of[10], (D,), 0.3, 4.0, (), jnp.float32),
        "up_weight": centred(key_of[11], (D, FF), D ** -0.5, 0.1875, ((1, 4),)),
        "up_bias": centred(key_of[12], (FF,), 0.3, 4.0, ((0, 4),), jnp.float32),
        "down_weight": centred(key_of[13], (FF, D), (FF // 2) ** -0.5, 0.125, ((0, 4),)),
        "down_bias": centred(key_of[14], (D,), 0.3, 4.0, (), jnp.float32),
        "cotangent": centred(key_of[15], (ROWS, SEQ, D), 1.0, 6.0, ((0, 8), (1, 4))),
    }


HIGH = lax.Precision.HIGHEST
EPS = 1e-05

@jax.custom_vjp
def low(v):
    return lax.optimization_barrier(v.astype(jnp.bfloat16)).astype(jnp.float32)

@jax.custom_vjp
def low_back(v):
    return v

def low_keep(v):
    return (low(v), None)

def low_pass(kept, grad):
    return (grad,)

def back_keep(v):
    return (v, None)

def back_low(kept, grad):
    return (low(grad),)
low.defvjp(low_keep, low_pass)
low_back.defvjp(back_keep, back_low)

def norm_rows(values, gain, shift):
    center = values - lax.optimization_barrier(jnp.mean(values, axis=-1, keepdims=True))
    spread = lax.optimization_barrier(jnp.mean(center * center, axis=-1, keepdims=True))
    return center * lax.rsqrt(spread + EPS) * gain + shift

def row_mask(segment, length):
    places = jnp.arange(segment.shape[0], dtype=jnp.int32)
    earlier = places[None, :] <= places[:, None]
    live = places < length
    same = (segment[:, None] == segment[None, :]) & live[:, None] & live[None, :]
    return earlier & (same | (places[:, None] == places[None, :]))

def reference(hidden, segment_ids, lengths, norm1_gain, norm1_shift, qkv_weight, qv_bias, out_weight, out_bias, norm2_gain, norm2_shift, up_weight, up_bias, down_weight, down_bias, cotangent):
    scale = HEAD ** (-0.5)

    def attend_row(pieces):
        query_row, key_row, value_row, segment, length = pieces
        scores = jnp.einsum('qhe,khe->hqk', query_row, key_row, precision=HIGH) * scale
        scores = jnp.where(row_mask(segment, length)[None], low_back(scores), -1e+30)
        probs = low(jax.nn.softmax(scores, axis=-1))
        return jnp.einsum('hqk,khe->qhe', probs, value_row, precision=HIGH)

    def forward(resid, gain1, shift1, w_qkv, b_qv, w_out, b_out, gain2, shift2, w_up, b_up, w_down, b_down):
        normed1 = low(norm_rows(resid, gain1, shift1))
        project = jnp.einsum('rtd,cde->crte', normed1, w_qkv, precision=HIGH)
        query = low_back(low(project[0] + b_qv[0])).reshape(ROWS, SEQ, HEADS, HEAD)
        keys = low_back(low(project[1])).reshape(ROWS, SEQ, HEADS, HEAD)
        values = low_back(low(project[2] + b_qv[1])).reshape(ROWS, SEQ, HEADS, HEAD)
        mixed = lax.map(jax.checkpoint(attend_row), (query, keys, values, segment_ids, lengths))
        attended = low_back(low(mixed.reshape(ROWS, SEQ, D)))
        branch = low_back(jnp.einsum('rte,ed->rtd', attended, w_out, precision=HIGH))
        mid = resid + branch + b_out
        normed2 = low(norm_rows(mid, gain2, shift2))
        inner = low_back(jnp.einsum('rtd,df->rtf', normed2, w_up, precision=HIGH) + b_up)
        active = low(jax.nn.gelu(inner))
        branch2 = low_back(jnp.einsum('rtf,fd->rtd', active, w_down, precision=HIGH))
        return mid + branch2 + b_down
    floats = tuple((item.astype(jnp.float32) for item in (hidden, norm1_gain, norm1_shift, qkv_weight, qv_bias, out_weight, out_bias, norm2_gain, norm2_shift, up_weight, up_bias, down_weight, down_bias)))
    output, pullback = jax.vjp(forward, *floats)
    grads = pullback(cotangent.astype(jnp.float32))
    return (output.astype(jnp.bfloat16), grads[0].astype(jnp.bfloat16), grads[1], grads[2], grads[3], grads[4], grads[5], grads[6], grads[7], grads[8], grads[9], grads[10], grads[11], grads[12])
```

```python
import functools
import math

import jax
import jax.numpy as jnp
from jax import lax
from jax.experimental import pallas as pl
from jax.experimental.pallas import tpu as pltpu
from jax.sharding import PartitionSpec as P

HEAD = 56
EPS = 1e-05
LANES = 128
BLK = 256
BF = jnp.bfloat16
F32 = jnp.float32


def head_window(h):
    lo, hi = h * HEAD, (h + 1) * HEAD
    first = lo // LANES * LANES
    last = -(-hi // LANES) * LANES
    return first, last


def head_mask(h, rows):
    first, last = head_window(h)
    lane = lax.broadcasted_iota(jnp.int32, (rows, last - first), 1) + first
    return (lane >= h * HEAD) & (lane < (h + 1) * HEAD)


def stage_in(rank, src, dst, shard, width):
    wide = dst.shape[1]
    for s in range(src.shape[0] // shard):
        rel = pl.multiple_of((rank ^ s) * shard, 16)
        dst[s * shard : (s + 1) * shard, :width] = src[pl.ds(rel, shard), :]
    if wide > width:
        dst[:, width:] = jnp.zeros((dst.shape[0], wide - width), dst.dtype)


def stage_out(rank, src, dst, shard, width):
    for s in range(dst.shape[0] // shard):
        rel = pl.multiple_of((rank ^ s) * shard, 16)
        dst[pl.ds(rel, shard), :] = src[s * shard : (s + 1) * shard, :width]


def tile_mask(start_row, qb, kb):
    kpos = kb * BLK + lax.broadcasted_iota(jnp.int32, (BLK, BLK), 0)
    qpos = qb * BLK + lax.broadcasted_iota(jnp.int32, (BLK, BLK), 1)
    return (kpos <= qpos) & (kpos >= start_row)


def dot_nt(a, b):
    return lax.dot_general(a, b, (((1,), (1,)), ((), ())), preferred_element_type=F32)


def attn_fwd_kernel(heads, shard, meta, start, q, k, v, out, lse, qs, ks, vs, vt, os, ot, ms, ls, acc):
    seq, width = q.shape
    scale2 = HEAD ** (-0.5) * math.log2(math.e)
    rank = meta[0]
    stage_in(rank, q, qs, shard, width)
    stage_in(rank, k, ks, shard, width)
    stage_in(rank, v, vs, shard, width)
    blocks = seq // BLK

    @pl.loop(0, blocks)
    def _(b):
        rows = pl.ds(pl.multiple_of(b * BLK, BLK), BLK)
        flipped = vs[rows, :].astype(F32).T
        for h in range(heads):
            vt[h, :, rows] = flipped[h * HEAD : (h + 1) * HEAD, :].astype(BF)

    lse[...] = jnp.zeros_like(lse)

    @pl.loop(0, blocks)
    def _(b):
        rows = pl.ds(pl.multiple_of(b * BLK, BLK), BLK)
        start_row = start[:, rows]
        ms[...] = jnp.full_like(ms, -1e30)
        ls[...] = jnp.zeros_like(ls)
        acc[...] = jnp.zeros_like(acc)

        def tile(kb, carry):
            krows = pl.ds(pl.multiple_of(kb * BLK, BLK), BLK)
            mask = tile_mask(start_row, b, kb)
            for h in range(heads):
                first, last = head_window(h)
                qm = jnp.where(head_mask(h, BLK), qs[rows, first:last], 0)
                s = dot_nt(ks[krows, first:last], qm) * scale2
                s = jnp.where(mask, s, -1e30)
                old = ms[h : h + 1, :]
                new = jnp.maximum(old, jnp.max(s, axis=0, keepdims=True))
                p = jnp.exp2(s - new)
                p = jnp.where(mask, p, 0.0)
                fade = jnp.exp2(old - new)
                ms[h : h + 1, :] = new
                ls[h : h + 1, :] = ls[h : h + 1, :] * fade + jnp.sum(p, axis=0, keepdims=True)
                acc[h] = acc[h] * fade + jnp.dot(
                    vt[h, :, krows], p.astype(BF), preferred_element_type=F32
                )
            return carry

        lax.fori_loop(meta[1 + b], b + 1, tile, 0)
        for h in range(heads):
            total = ls[h : h + 1, :]
            lse[h : h + 1, rows] = ms[h : h + 1, :] + jnp.log(total) * math.log2(math.e)
            ot[h * HEAD : (h + 1) * HEAD, :] = acc[h] / total
        os[rows, :] = ot[...].T.astype(BF)

    stage_out(rank, os, out, shard, width)


def attn_bwd_kernel(
    heads, shard, meta, start, q, k, v, o, do, lse, dq, dk, dv,
    qs, ks, vs, dos, kt, delta, dqs, dks, dvs, dqt, qm, dm,
):
    seq, width = q.shape
    scale = HEAD ** (-0.5)
    scale2 = scale * math.log2(math.e)
    rank = meta[0]
    blocks = seq // BLK
    stage_in(rank, o, vs, shard, width)
    stage_in(rank, do, dos, shard, width)

    @pl.loop(0, blocks)
    def _(b):
        rows = pl.ds(pl.multiple_of(b * BLK, BLK), BLK)
        flipped = (vs[rows, :].astype(F32) * dos[rows, :].astype(F32)).T
        for h in range(heads):
            delta[h : h + 1, rows] = jnp.sum(
                flipped[h * HEAD : (h + 1) * HEAD, :], axis=0, keepdims=True
            )

    stage_in(rank, q, qs, shard, width)
    stage_in(rank, k, ks, shard, width)
    stage_in(rank, v, vs, shard, width)

    @pl.loop(0, blocks)
    def _(b):
        rows = pl.ds(pl.multiple_of(b * BLK, BLK), BLK)
        flipped = ks[rows, :].astype(F32).T
        for h in range(heads):
            kt[h, :, rows] = flipped[h * HEAD : (h + 1) * HEAD, :].astype(BF)

    dks[...] = jnp.zeros_like(dks)
    dvs[...] = jnp.zeros_like(dvs)
    dqt[...] = jnp.zeros_like(dqt)

    @pl.loop(0, blocks)
    def _(b):
        rows = pl.ds(pl.multiple_of(b * BLK, BLK), BLK)
        start_row = start[:, rows]
        dqt[...] = jnp.zeros_like(dqt)
        for h in range(heads):
            first, last = head_window(h)
            keep = head_mask(h, BLK)
            qm[h, :, : last - first] = jnp.where(keep, qs[rows, first:last], 0)
            dm[h, :, : last - first] = jnp.where(keep, dos[rows, first:last], 0)

        def tile(kb, carry):
            krows = pl.ds(pl.multiple_of(kb * BLK, BLK), BLK)
            mask = tile_mask(start_row, b, kb)
            for h in range(heads):
                first, last = head_window(h)
                qh = qm[h, :, : last - first]
                dh = dm[h, :, : last - first]
                s = dot_nt(ks[krows, first:last], qh) * scale2
                p = jnp.where(mask, jnp.exp2(s - lse[h : h + 1, rows]), 0.0)
                dp = dot_nt(vs[krows, first:last], dh)
                ds = (p * (dp - delta[h : h + 1, rows])).astype(BF)
                dvs[krows, first:last] += jnp.dot(p.astype(BF), dh, preferred_element_type=F32)
                dks[krows, first:last] += jnp.dot(ds, qh, preferred_element_type=F32)
                dqt[h * HEAD : (h + 1) * HEAD, :] += jnp.dot(
                    kt[h, :, krows], ds, preferred_element_type=F32
                )
            return carry

        lax.fori_loop(meta[1 + b], b + 1, tile, 0)
        dqs[rows, :] = (dqt[...].T * scale).astype(BF)

    stage_out(rank, dqs, dq, shard, width)
    for s in range(seq // shard):
        rel = pl.multiple_of((rank ^ s) * shard, 16)
        here = slice(s * shard, (s + 1) * shard)
        dk[pl.ds(rel, shard), :] = (dks[here, :width] * scale).astype(BF)
        dv[pl.ds(rel, shard), :] = dvs[here, :width].astype(BF)


def vmem():
    return pl.BlockSpec(memory_space=pltpu.VMEM)


def smem():
    return pl.BlockSpec(memory_space=pltpu.SMEM)


def attn_cost(seq, width, products):
    return pl.CostEstimate(
        flops=products * seq * seq * width,
        bytes_accessed=8 * seq * width * 2,
        transcendentals=seq * seq * width // (2 * HEAD),
    )


def attn_fwd(meta, start, q, k, v, shard):
    seq, width = q.shape
    heads = width // HEAD
    wide = -(-width // LANES) * LANES
    return pl.pallas_call(
        functools.partial(attn_fwd_kernel, heads, shard),
        out_shape=(
            jax.ShapeDtypeStruct((seq, width), BF),
            jax.ShapeDtypeStruct((8, seq), F32),
        ),
        in_specs=[smem()] + [vmem()] * 4,
        out_specs=(vmem(), vmem()),
        scratch_shapes=[
            pltpu.VMEM((seq, wide), BF),
            pltpu.VMEM((seq, wide), BF),
            pltpu.VMEM((seq, wide), BF),
            pltpu.VMEM((heads, HEAD, seq), BF),
            pltpu.VMEM((seq, wide), BF),
            pltpu.VMEM((wide, BLK), F32),
            pltpu.VMEM((8, BLK), F32),
            pltpu.VMEM((8, BLK), F32),
            pltpu.VMEM((heads, HEAD, BLK), F32),
        ],
        cost_estimate=attn_cost(seq, width, 3),
        name="attn_fwd",
    )(meta, start, q, k, v)


def attn_bwd(meta, start, q, k, v, o, do, lse, shard):
    seq, width = q.shape
    heads = width // HEAD
    wide = -(-width // LANES) * LANES
    grad = jax.ShapeDtypeStruct((seq, width), BF)
    return pl.pallas_call(
        functools.partial(attn_bwd_kernel, heads, shard),
        out_shape=(grad, grad, grad),
        in_specs=[smem()] + [vmem()] * 7,
        out_specs=(vmem(), vmem(), vmem()),
        scratch_shapes=[
            pltpu.VMEM((seq, wide), BF),
            pltpu.VMEM((seq, wide), BF),
            pltpu.VMEM((seq, wide), BF),
            pltpu.VMEM((seq, wide), BF),
            pltpu.VMEM((heads, HEAD, seq), BF),
            pltpu.VMEM((8, seq), F32),
            pltpu.VMEM((seq, wide), BF),
            pltpu.VMEM((seq, wide), F32),
            pltpu.VMEM((seq, wide), F32),
            pltpu.VMEM((wide, BLK), F32),
            pltpu.VMEM((heads, BLK, 2 * LANES), BF),
            pltpu.VMEM((heads, BLK, 2 * LANES), BF),
        ],
        cost_estimate=attn_cost(seq, width, 8),
        name="attn_bwd",
    )(meta, start, q, k, v, o, do, lse)


AXES = ("dp", "tensor")


def send(x, rule):
    nd, nt = lax.axis_size("dp"), lax.axis_size("tensor")
    pairs = []
    for d in range(nd):
        for t in range(nt):
            to = rule(d, t)
            if to is not None:
                pairs.append((d * nt + t, to[0] * nt + to[1]))
    return lax.ppermute(x, AXES, pairs)


def is_home(d, t):
    return (d & 1) == (t >> 1)


def swap_rule(d, t):
    return (d, t) if is_home(d, t) else (d ^ 1, t ^ 2)


def gather4(x):
    xz = send(x, lambda d, t: (d, t ^ 1))
    xc = send(x, lambda d, t: (d ^ 1, t))
    xzc = send(xz, lambda d, t: (d ^ 1, t))
    return jnp.concatenate([x, xz, xc, xzc], axis=0)


def scatter4(part):
    part = part.astype(BF)
    rows = part.shape[0] // 4
    other = send(part[2 * rows :], lambda d, t: (d ^ 1, t))
    far = part[rows : 2 * rows].astype(F32) + other[rows:].astype(F32)
    far = send(far.astype(BF), lambda d, t: (d, t ^ 1))
    return part[:rows].astype(F32) + other[:rows].astype(F32) + far.astype(F32)


def pad_rows(x, unit):
    extra = -x.shape[0] % unit
    return jnp.pad(x, ((0, extra), (0, 0))) if extra else x


def spread_weight(w, home, column, columns):
    rows = w.shape[0]
    w = pad_rows(w, 8 * columns)
    unit = w.shape[0] // columns

    def piece(index):
        return lax.dynamic_slice_in_dim(w, index * unit, unit, 0)

    mine = send(piece(column), lambda d, t: (d, t ^ 2) if is_home(d, t) else None)
    whole = jnp.zeros_like(w)
    for m in range(columns):
        got = mine
        if m:
            got = send(mine, lambda d, t: None if is_home(d, t) else (d ^ (2 * m), t))
        index = column ^ m
        whole = lax.dynamic_update_slice_in_dim(
            whole, jnp.where(home, piece(index), got), index * unit, 0
        )
    return whole[:rows]


def reduce_grad(g, home, column, columns):
    rows = g.shape[0]
    bits = columns.bit_length() - 1
    g = pad_rows(g, 16 * columns)
    half = g.shape[0] // 2
    done = []
    for side in range(2):
        piece = g[side * half : (side + 1) * half]
        order = [(b + side) % bits for b in range(bits)] if bits else []
        for b in order:
            n = piece.shape[0] // 2
            bit = (column >> b) & 1
            keep = lax.dynamic_slice_in_dim(piece, bit * n, n, 0)
            away = lax.dynamic_slice_in_dim(piece, (1 - bit) * n, n, 0)
            got = send(away, lambda d, t: (d ^ (2 << b), t))
            piece = (keep.astype(F32) + got.astype(F32)).astype(BF)
        got = send(piece, lambda d, t: None if is_home(d, t) else (d, t ^ 2))
        piece = (piece.astype(F32) + got.astype(F32)).astype(BF)
        for b in reversed(order):
            bit = (column >> b) & 1
            got = send(piece, lambda d, t: (d ^ (2 << b), t) if is_home(d, t) else None)
            first = jnp.where(bit == 0, piece, got)
            second = jnp.where(bit == 0, got, piece)
            piece = jnp.concatenate([first, second], axis=0)
        done.append(piece)
    whole = jnp.concatenate(done, axis=0)[:rows]
    other = send(whole, lambda d, t: (d ^ 1, t) if is_home(d, t) else None)
    return jnp.where(home, whole, other).astype(F32)


def sum_all(x):
    for axis in range(2):
        size = (lax.axis_size("dp"), lax.axis_size("tensor"))[axis]
        step = 1
        while step < size:
            x = x + send(x, lambda d, t: (d ^ step, t) if axis == 0 else (d, t ^ step))
            step *= 2
    return x


def norm_parts(values):
    center = values - jnp.mean(values, axis=-1, keepdims=True)
    rstd = lax.rsqrt(jnp.mean(center * center, axis=-1, keepdims=True) + EPS)
    return center * rstd, rstd


def norm_back(grad, hat, rstd, gain):
    gn = grad * gain
    return rstd * (
        gn
        - jnp.mean(gn, axis=-1, keepdims=True)
        - hat * jnp.mean(gn * hat, axis=-1, keepdims=True)
    )


def mm(a, b):
    return jnp.dot(a, b, preferred_element_type=F32)


def mm_nt(a, b):
    return lax.dot_general(a, b, (((1,), (1,)), ((), ())), preferred_element_type=F32)


def mm_tn(a, b):
    return lax.dot_general(a, b, (((0,), (0,)), ((), ())), preferred_element_type=F32)


def body(
    hidden,
    segment_ids,
    lengths,
    norm1_gain,
    norm1_shift,
    qkv_weight,
    qv_bias,
    out_weight,
    out_bias,
    norm2_gain,
    norm2_shift,
    up_weight,
    up_bias,
    down_weight,
    down_bias,
    cotangent,
):
    _, shard, model = hidden.shape
    seq = segment_ids.shape[1]
    width = qkv_weight.shape[2]
    hidden_units = up_weight.shape[1]
    d, t = lax.axis_index("dp"), lax.axis_index("tensor")
    columns = lax.axis_size("dp") // 2
    column = d >> 1
    home = is_home(d, t)
    rank = 2 * (d & 1) + (t & 1)

    own = send(hidden[0], swap_rule)
    full = gather4(own)
    ids = jnp.concatenate([segment_ids[0], lengths])
    ids = send(ids, swap_rule)
    length = ids[seq]
    places = jnp.arange(seq, dtype=jnp.int32)
    ids = jnp.where(places < length, ids[:seq], 16 + places)
    start = jnp.sum((ids[None, :] < ids[:, None]).astype(jnp.int32), axis=1)
    meta = jnp.concatenate([rank[None], start[::BLK] // BLK]).astype(jnp.int32)
    start = start[None, :]

    w_qkv = spread_weight(
        jnp.concatenate([qkv_weight[0], qkv_weight[1], qkv_weight[2]], axis=0), home, column, columns
    ).reshape(3, model, width)
    bias = jnp.concatenate([qv_bias.reshape(-1), up_bias])
    far_bias = send(bias, lambda d, t: (d, t ^ 2) if is_home(d, t) else None)
    bias = jnp.where(home, bias, far_bias)
    b_q, b_v, b_up = bias[:width], bias[width : 2 * width], bias[2 * width :]

    cot, own, up_w, down_w, out_w = lax.optimization_barrier(
        (cotangent[0], own, up_weight, down_weight, out_weight)
    )
    w_out = spread_weight(out_w, home, column, columns)
    w_up = spread_weight(up_w, home, column, columns)
    w_down = spread_weight(down_w, home, column, columns)
    cot_own = send(cot, swap_rule)
    cot_full = gather4(cot_own)

    resid_full = full.astype(F32)
    hat1, rstd1 = norm_parts(resid_full)
    normed1 = (hat1 * norm1_gain + norm1_shift).astype(BF)
    q = (mm(normed1, w_qkv[0]) + b_q).astype(BF)
    k = mm(normed1, w_qkv[1]).astype(BF)
    v = (mm(normed1, w_qkv[2]) + b_v).astype(BF)
    attended, lse = attn_fwd(meta, start, q, k, v, shard)

    mid = own.astype(F32) + scatter4(mm(attended, w_out)) + out_bias
    hat2, rstd2 = norm_parts(mid)
    normed2 = gather4((hat2 * norm2_gain + norm2_shift).astype(BF))
    inner = mm(normed2, w_up) + b_up
    c0 = math.sqrt(2.0 / math.pi)
    tanh = jnp.tanh(c0 * (inner + 0.044715 * inner * inner * inner))
    active = (0.5 * inner * (1.0 + tanh)).astype(BF)
    slope = 0.5 * (1.0 + tanh) + 0.5 * inner * (1.0 - tanh * tanh) * c0 * (
        1.0 + 3 * 0.044715 * inner * inner
    )
    grad_inner = (mm_nt(cot_full, w_down) * slope).astype(BF)
    grad_normed2 = scatter4(mm_nt(grad_inner, w_up))
    grad_out = cot_own.astype(F32)
    grad_mid = grad_out + norm_back(grad_normed2, hat2, rstd2, norm2_gain)
    gm_full = gather4(grad_mid.astype(BF))

    output = mid + scatter4(mm(active, w_down)) + down_bias
    output = send(output.astype(BF), swap_rule)
    up_grad = mm_tn(normed2, grad_inner).astype(BF)
    down_grad = mm_tn(active, cot_full).astype(BF)
    mlp_grad = reduce_grad(jnp.concatenate([up_grad, down_grad], axis=0), home, column, columns)

    grad_attended = mm_nt(gm_full, w_out).astype(BF)
    out_grad = reduce_grad(mm_tn(attended, gm_full).astype(BF), home, column, columns)
    dq, dk, dv = attn_bwd(meta, start, q, k, v, attended, grad_attended, lse, shard)
    part1 = mm_nt(dq, w_qkv[0]) + mm_nt(dk, w_qkv[1]) + mm_nt(dv, w_qkv[2])
    grad_normed1 = scatter4(part1)
    hat1_own, rstd1_own = norm_parts(own.astype(F32))
    input_grad = grad_mid + norm_back(grad_normed1, hat1_own, rstd1_own, norm1_gain)
    input_grad = send(input_grad.astype(BF), swap_rule)
    qkv_grad = jnp.concatenate(
        [mm_tn(normed1, dq), mm_tn(normed1, dk), mm_tn(normed1, dv)], axis=0
    ).astype(BF)
    qkv_grad = reduce_grad(qkv_grad, home, column, columns).reshape(3, model, width)

    quarter_bias = jnp.concatenate(
        [
            jnp.sum(dq, axis=0, dtype=F32),
            jnp.sum(dv, axis=0, dtype=F32),
            jnp.sum(grad_inner, axis=0, dtype=F32),
        ]
    )
    slots = lax.broadcasted_iota(jnp.int32, (4, 1), 0) == rank
    small = jnp.concatenate(
        [
            jnp.sum(part1 * hat1, axis=0),
            jnp.sum(part1, axis=0),
            jnp.sum(grad_mid, axis=0),
            jnp.sum(grad_normed2 * hat2, axis=0),
            jnp.sum(grad_normed2, axis=0),
            jnp.sum(grad_out, axis=0),
            jnp.where(slots, quarter_bias[None], 0.0).reshape(-1),
        ]
    )
    small = sum_all(small)
    gain1, shift1, out_b, gain2, shift2, down_b = [
        small[i * model : (i + 1) * model] for i in range(6)
    ]
    split = 2 * width + hidden_units
    quarter = lax.dynamic_slice_in_dim(small, 6 * model + t * split, split, 0)
    return (
        output[None],
        input_grad[None],
        gain1,
        shift1,
        qkv_grad,
        quarter[: 2 * width].reshape(2, width),
        out_grad,
        out_b,
        gain2,
        shift2,
        mlp_grad[:model],
        quarter[2 * width :],
        mlp_grad[model:],
        down_b,
    )


def solution(mesh):
    in_specs = (
        P("dp", "tensor", None),
        P("dp", None),
        P("dp"),
        P(),
        P(),
        P(None, None, "tensor"),
        P(None, "tensor"),
        P("tensor", None),
        P(),
        P(),
        P(),
        P(None, "tensor"),
        P("tensor"),
        P("tensor", None),
        P(),
        P("dp", "tensor", None),
    )
    out_specs = (
        P("dp", "tensor", None),
        P("dp", "tensor", None),
        P(),
        P(),
        P(None, None, "tensor"),
        P(None, "tensor"),
        P("tensor", None),
        P(),
        P(),
        P(),
        P(None, "tensor"),
        P("tensor"),
        P("tensor", None),
        P(),
    )
    return jax.shard_map(body, mesh=mesh, in_specs=in_specs, out_specs=out_specs, check_vma=False)
```

```python
import functools
import math

import jax
import jax.numpy as jnp
from jax import lax
from jax.experimental import pallas as pl
from jax.experimental.pallas import tpu as pltpu
from jax.sharding import PartitionSpec as P

HEAD = 56
EPS = 1e-05
LANES = 128
BLK = 256
BF = jnp.bfloat16
F32 = jnp.float32


def head_window(h):
    lo, hi = h * HEAD, (h + 1) * HEAD
    first = lo // LANES * LANES
    last = -(-hi // LANES) * LANES
    return first, last


def head_mask(h, rows):
    first, last = head_window(h)
    lane = lax.broadcasted_iota(jnp.int32, (rows, last - first), 1) + first
    return (lane >= h * HEAD) & (lane < (h + 1) * HEAD)


def stage_in(rank, src, dst, shard, width):
    wide = dst.shape[1]
    for s in range(src.shape[0] // shard):
        rel = pl.multiple_of((rank ^ s) * shard, 16)
        dst[s * shard : (s + 1) * shard, :width] = src[pl.ds(rel, shard), :]
    if wide > width:
        dst[:, width:] = jnp.zeros((dst.shape[0], wide - width), dst.dtype)


def stage_out(rank, src, dst, shard, width):
    for s in range(dst.shape[0] // shard):
        rel = pl.multiple_of((rank ^ s) * shard, 16)
        dst[pl.ds(rel, shard), :] = src[s * shard : (s + 1) * shard, :width]


def tile_mask(start_row, qb, kb):
    kpos = kb * BLK + lax.broadcasted_iota(jnp.int32, (BLK, BLK), 0)
    qpos = qb * BLK + lax.broadcasted_iota(jnp.int32, (BLK, BLK), 1)
    return (kpos <= qpos) & (kpos >= start_row)


def dot_nt(a, b):
    return lax.dot_general(a, b, (((1,), (1,)), ((), ())), preferred_element_type=F32)


def attn_fwd_kernel(heads, shard, meta, start, q, k, v, out, lse, qs, ks, vs, vt, os, ot, ms, ls, acc):
    seq, width = q.shape
    scale2 = HEAD ** (-0.5) * math.log2(math.e)
    rank = meta[0]
    stage_in(rank, q, qs, shard, width)
    stage_in(rank, k, ks, shard, width)
    stage_in(rank, v, vs, shard, width)
    blocks = seq // BLK

    @pl.loop(0, blocks)
    def _(b):
        rows = pl.ds(pl.multiple_of(b * BLK, BLK), BLK)
        flipped = vs[rows, :].astype(F32).T
        for h in range(heads):
            vt[h, :, rows] = flipped[h * HEAD : (h + 1) * HEAD, :].astype(BF)

    lse[...] = jnp.zeros_like(lse)

    @pl.loop(0, blocks)
    def _(b):
        rows = pl.ds(pl.multiple_of(b * BLK, BLK), BLK)
        start_row = start[:, rows]
        ms[...] = jnp.full_like(ms, -1e30)
        ls[...] = jnp.zeros_like(ls)
        acc[...] = jnp.zeros_like(acc)

        def tile(kb, carry):
            krows = pl.ds(pl.multiple_of(kb * BLK, BLK), BLK)
            mask = tile_mask(start_row, b, kb)
            for h in range(heads):
                first, last = head_window(h)
                qm = jnp.where(head_mask(h, BLK), qs[rows, first:last], 0)
                s = dot_nt(ks[krows, first:last], qm) * scale2
                s = jnp.where(mask, s, -1e30)
                old = ms[h : h + 1, :]
                new = jnp.maximum(old, jnp.max(s, axis=0, keepdims=True))
                p = jnp.exp2(s - new)
                p = jnp.where(mask, p, 0.0)
                fade = jnp.exp2(old - new)
                ms[h : h + 1, :] = new
                ls[h : h + 1, :] = ls[h : h + 1, :] * fade + jnp.sum(p, axis=0, keepdims=True)
                acc[h] = acc[h] * fade + jnp.dot(
                    vt[h, :, krows], p.astype(BF), preferred_element_type=F32
                )
            return carry

        lax.fori_loop(meta[1 + b], b + 1, tile, 0)
        for h in range(heads):
            total = ls[h : h + 1, :]
            lse[h : h + 1, rows] = ms[h : h + 1, :] + jnp.log(total) * math.log2(math.e)
            ot[h * HEAD : (h + 1) * HEAD, :] = acc[h] / total
        os[rows, :] = ot[...].T.astype(BF)

    stage_out(rank, os, out, shard, width)


def attn_bwd_kernel(
    heads, shard, meta, start, q, k, v, o, do, lse, dq, dk, dv,
    qs, ks, vs, dos, kt, delta, dqs, dks, dvs, dqt, qm, dm,
):
    seq, width = q.shape
    scale = HEAD ** (-0.5)
    scale2 = scale * math.log2(math.e)
    rank = meta[0]
    blocks = seq // BLK
    stage_in(rank, o, vs, shard, width)
    stage_in(rank, do, dos, shard, width)

    @pl.loop(0, blocks)
    def _(b):
        rows = pl.ds(pl.multiple_of(b * BLK, BLK), BLK)
        flipped = (vs[rows, :].astype(F32) * dos[rows, :].astype(F32)).T
        for h in range(heads):
            delta[h : h + 1, rows] = jnp.sum(
                flipped[h * HEAD : (h + 1) * HEAD, :], axis=0, keepdims=True
            )

    stage_in(rank, q, qs, shard, width)
    stage_in(rank, k, ks, shard, width)
    stage_in(rank, v, vs, shard, width)

    @pl.loop(0, blocks)
    def _(b):
        rows = pl.ds(pl.multiple_of(b * BLK, BLK), BLK)
        flipped = ks[rows, :].astype(F32).T
        for h in range(heads):
            kt[h, :, rows] = flipped[h * HEAD : (h + 1) * HEAD, :].astype(BF)

    dks[...] = jnp.zeros_like(dks)
    dvs[...] = jnp.zeros_like(dvs)
    dqt[...] = jnp.zeros_like(dqt)

    @pl.loop(0, blocks)
    def _(b):
        rows = pl.ds(pl.multiple_of(b * BLK, BLK), BLK)
        start_row = start[:, rows]
        dqt[...] = jnp.zeros_like(dqt)
        for h in range(heads):
            first, last = head_window(h)
            keep = head_mask(h, BLK)
            qm[h, :, : last - first] = jnp.where(keep, qs[rows, first:last], 0)
            dm[h, :, : last - first] = jnp.where(keep, dos[rows, first:last], 0)

        def tile(kb, carry):
            krows = pl.ds(pl.multiple_of(kb * BLK, BLK), BLK)
            mask = tile_mask(start_row, b, kb)
            for h in range(heads):
                first, last = head_window(h)
                qh = qm[h, :, : last - first]
                dh = dm[h, :, : last - first]
                s = dot_nt(ks[krows, first:last], qh) * scale2
                p = jnp.where(mask, jnp.exp2(s - lse[h : h + 1, rows]), 0.0)
                dp = dot_nt(vs[krows, first:last], dh)
                ds = (p * (dp - delta[h : h + 1, rows])).astype(BF)
                dvs[krows, first:last] += jnp.dot(p.astype(BF), dh, preferred_element_type=F32)
                dks[krows, first:last] += jnp.dot(ds, qh, preferred_element_type=F32)
                dqt[h * HEAD : (h + 1) * HEAD, :] += jnp.dot(
                    kt[h, :, krows], ds, preferred_element_type=F32
                )
            return carry

        lax.fori_loop(meta[1 + b], b + 1, tile, 0)
        dqs[rows, :] = (dqt[...].T * scale).astype(BF)

    stage_out(rank, dqs, dq, shard, width)
    for s in range(seq // shard):
        rel = pl.multiple_of((rank ^ s) * shard, 16)
        here = slice(s * shard, (s + 1) * shard)
        dk[pl.ds(rel, shard), :] = (dks[here, :width] * scale).astype(BF)
        dv[pl.ds(rel, shard), :] = dvs[here, :width].astype(BF)


def vmem():
    return pl.BlockSpec(memory_space=pltpu.VMEM)


def smem():
    return pl.BlockSpec(memory_space=pltpu.SMEM)


def attn_cost(seq, width, products):
    return pl.CostEstimate(
        flops=products * seq * seq * width,
        bytes_accessed=8 * seq * width * 2,
        transcendentals=seq * seq * width // (2 * HEAD),
    )


def attn_fwd(meta, start, q, k, v, shard):
    seq, width = q.shape
    heads = width // HEAD
    wide = -(-width // LANES) * LANES
    return pl.pallas_call(
        functools.partial(attn_fwd_kernel, heads, shard),
        out_shape=(
            jax.ShapeDtypeStruct((seq, width), BF),
            jax.ShapeDtypeStruct((8, seq), F32),
        ),
        in_specs=[smem()] + [vmem()] * 4,
        out_specs=(vmem(), vmem()),
        scratch_shapes=[
            pltpu.VMEM((seq, wide), BF),
            pltpu.VMEM((seq, wide), BF),
            pltpu.VMEM((seq, wide), BF),
            pltpu.VMEM((heads, HEAD, seq), BF),
            pltpu.VMEM((seq, wide), BF),
            pltpu.VMEM((wide, BLK), F32),
            pltpu.VMEM((8, BLK), F32),
            pltpu.VMEM((8, BLK), F32),
            pltpu.VMEM((heads, HEAD, BLK), F32),
        ],
        cost_estimate=attn_cost(seq, width, 3),
        name="attn_fwd",
    )(meta, start, q, k, v)


def attn_bwd(meta, start, q, k, v, o, do, lse, shard):
    seq, width = q.shape
    heads = width // HEAD
    wide = -(-width // LANES) * LANES
    grad = jax.ShapeDtypeStruct((seq, width), BF)
    return pl.pallas_call(
        functools.partial(attn_bwd_kernel, heads, shard),
        out_shape=(grad, grad, grad),
        in_specs=[smem()] + [vmem()] * 7,
        out_specs=(vmem(), vmem(), vmem()),
        scratch_shapes=[
            pltpu.VMEM((seq, wide), BF),
            pltpu.VMEM((seq, wide), BF),
            pltpu.VMEM((seq, wide), BF),
            pltpu.VMEM((seq, wide), BF),
            pltpu.VMEM((heads, HEAD, seq), BF),
            pltpu.VMEM((8, seq), F32),
            pltpu.VMEM((seq, wide), BF),
            pltpu.VMEM((seq, wide), F32),
            pltpu.VMEM((seq, wide), F32),
            pltpu.VMEM((wide, BLK), F32),
            pltpu.VMEM((heads, BLK, 2 * LANES), BF),
            pltpu.VMEM((heads, BLK, 2 * LANES), BF),
        ],
        cost_estimate=attn_cost(seq, width, 8),
        name="attn_bwd",
    )(meta, start, q, k, v, o, do, lse)


MESH = pl.DeviceIdType.MESH
CHUNKS = 2
STEP = 32


class Place:
    def __init__(self, columns):
        d, t = lax.axis_index("dp"), lax.axis_index("tensor")
        core, low, high = lax.rem(d, 2), lax.rem(t, 2), lax.div(t, 2)
        self.d, self.t, self.columns = d, t, columns
        self.bits = columns.bit_length() - 1
        self.core = (d + 1 - 2 * core, t)
        self.near = (d, t + 1 - 2 * low)
        self.far = (d, t + 2 - 4 * high)
        self.swap = (d + 1 - 2 * core, t + 2 - 4 * high)
        self.home = core == high
        self.away = core != high

    def bit(self, b):
        return lax.rem(lax.div(self.d, 2 << b), 2)

    def column(self, m):
        d = self.d
        for b in range(self.bits):
            if (m >> b) & 1:
                d = d + (2 << b) * (1 - 2 * self.bit(b))
        return (d, self.t)


class Link:
    def __init__(self, send_sems, recv_sems):
        self.send_sems, self.recv_sems = send_sems, recv_sems
        self.count = 0
        self.open, self.kept, self.number = [], [], {}

    def make(self, src, dst, to, like=None):
        if like is None:
            i = self.count
            self.count += 1
        else:
            i = self.number[id(like)]
        copy = pltpu.make_async_remote_copy(
            src_ref=src,
            dst_ref=dst,
            send_sem=self.send_sems.at[i],
            recv_sem=self.recv_sems.at[i],
            device_id=to,
            device_id_type=MESH,
        )
        self.number[id(copy)] = i
        self.kept.append(copy)
        return copy

    def start(self, copy, when=None):
        if when is None:
            copy.start()
        else:
            pl.when(when)(copy.start)
        self.open.append((copy, when))

    def send(self, src, dst, to, when=None):
        copy = self.make(src, dst, to)
        self.start(copy, when)
        return copy

    def close(self):
        for copy, when in self.open:
            if when is None:
                copy.wait_send()
            else:
                pl.when(when)(copy.wait_send)


def arrive(copy, when=None):
    if when is None:
        copy.wait_recv()
    else:
        pl.when(when)(copy.wait_recv)


def meet(partners):
    barrier = pltpu.get_barrier_semaphore()
    for to in partners:
        pl.semaphore_signal(barrier, inc=1, device_id=to, device_id_type=MESH)
    pl.semaphore_wait(barrier, len(partners))


def rows_of(ref, first, count):
    return ref.at[pl.ds(first, count)]


def gather_start(link, place, full, shard, i):
    n = shard // CHUNKS
    near = link.send(rows_of(full, i * n, n), rows_of(full, shard + i * n, n), place.near)
    core = link.send(rows_of(full, i * n, n), rows_of(full, 2 * shard + i * n, n), place.core)
    return near, core


def gather_relay(link, place, full, shard, i, near):
    n = shard // CHUNKS
    near.wait_recv()
    return link.send(
        rows_of(full, shard + i * n, n), rows_of(full, 3 * shard + i * n, n), place.core
    )


class Scatter:
    def __init__(self, link, place, part, core_buf, out_buf, near_buf, shard):
        self.link, self.place, self.part = link, place, part
        self.core_buf, self.out_buf, self.near_buf = core_buf, out_buf, near_buf
        self.shard, self.n = shard, shard // CHUNKS
        self.core, self.near = {}, {}

    def start(self):
        for block in (3, 2):
            for i in range(CHUNKS):
                at = (block - 2) * self.shard + i * self.n
                self.core[block - 2, i] = self.link.send(
                    rows_of(self.part, 2 * self.shard + at, self.n),
                    rows_of(self.core_buf, at, self.n),
                    self.place.core,
                )

    def pass_on(self, i):
        at = self.shard + i * self.n
        self.core[1, i].wait_recv()

        @pl.loop(0, self.n // STEP)
        def _(r):
            here = pl.multiple_of(at + r * STEP, STEP)
            there = pl.multiple_of(i * self.n + r * STEP, STEP)
            total = self.part[pl.ds(here, STEP), :].astype(F32) + self.core_buf[
                pl.ds(here, STEP), :
            ].astype(F32)
            self.out_buf[pl.ds(there, STEP), :] = total.astype(BF)

        self.near[i] = self.link.send(
            rows_of(self.out_buf, i * self.n, self.n),
            rows_of(self.near_buf, i * self.n, self.n),
            self.place.near,
        )

    def ready(self, i):
        self.core[0, i].wait_recv()
        self.near[i].wait_recv()

    def rows(self, rows):
        return (
            self.part[rows, :].astype(F32)
            + self.core_buf[rows, :].astype(F32)
            + self.near_buf[rows, :].astype(F32)
        )


def scatter_scratch(shard, model):
    return [
        pltpu.VMEM((2 * shard, model), BF),
        pltpu.VMEM((shard, model), BF),
        pltpu.VMEM((shard, model), BF),
    ]


def over_rows(first, count, step, fn):
    @pl.loop(0, count // step)
    def _(r):
        fn(pl.ds(pl.multiple_of(first + r * step, 16), step))


class Halving:
    def __init__(self, link, place, source, first, size, turn, work, got):
        self.link, self.place = link, place
        self.source, self.first, self.size = source, first, size
        self.order = [(b + turn) % place.bits for b in range(place.bits)]
        self.work, self.got = work, got
        self.copies = []

    def start(self, s):
        n = self.size >> (s + 1)
        bit = self.place.bit(self.order[s])
        src, base = (self.source, self.first) if s == 0 else (self.work[s - 1], 0)
        at = pl.multiple_of(base + (1 - bit) * n, 16)
        self.copies.append(
            self.link.send(
                rows_of(src, at, n), self.got[s], self.place.column(1 << self.order[s])
            )
        )

    def finish(self, s):
        n = self.size >> (s + 1)
        bit = self.place.bit(self.order[s])
        src, base = (self.source, self.first) if s == 0 else (self.work[s - 1], 0)
        self.copies[s].wait_recv()

        @pl.loop(0, n // 16)
        def _(r):
            here = pl.multiple_of(base + bit * n + r * 16, 16)
            to = pl.ds(pl.multiple_of(r * 16, 16), 16)
            total = src[pl.ds(here, 16), :].astype(F32) + self.got[s][to, :].astype(F32)
            self.work[s][to, :] = total.astype(BF)

    def offset(self):
        at, n = 0, self.size
        for b in self.order:
            n //= 2
            at = at + self.place.bit(b) * n
        return self.first + at


def halving_scratch(size, bits, model):
    return [pltpu.VMEM((size >> (s + 1), model), BF) for s in range(bits)]


class Doubling:
    def __init__(self, link, place, half, full, slice_ref, far_buf):
        self.link, self.place, self.half, self.full = link, place, half, full
        self.slice_ref, self.far_buf = slice_ref, far_buf
        self.n = half.size >> place.bits
        self.at = half.offset()
        self.cores, self.waits = [], []

    def start(self):
        self.far = self.link.send(
            self.slice_ref, self.far_buf, self.place.far, self.place.away
        )

    def to_core(self, at, n):
        self.link.send(
            rows_of(self.full, at, n), rows_of(self.full, at, n), self.place.core, self.place.home
        )

    def join(self):
        arrive(self.far, self.place.home)

        @pl.when(self.place.home)
        def _():
            @pl.loop(0, self.n // 16)
            def _(r):
                here = pl.ds(pl.multiple_of(r * 16, 16), 16)
                to = pl.ds(pl.multiple_of(self.at + r * 16, 16), 16)
                total = self.slice_ref[here, :].astype(F32) + self.far_buf[here, :].astype(F32)
                self.full[to, :] = total.astype(BF)

        self.block, self.count = pl.multiple_of(self.at, 16), self.n
        self.stage = 0
        self.push(self.block)

    def push(self, fresh):
        if self.stage < self.place.bits:
            b = self.half.order[self.place.bits - 1 - self.stage]
            self.copy = self.link.send(
                rows_of(self.full, self.block, self.count),
                rows_of(self.full, self.block, self.count),
                self.place.column(1 << b),
                self.place.home,
            )
        copy = self.link.send(
            rows_of(self.full, fresh, self.count if self.stage == 0 else self.count // 2),
            rows_of(self.full, fresh, self.count if self.stage == 0 else self.count // 2),
            self.place.core,
            self.place.home,
        )
        self.cores.append(copy)

    def advance(self):
        b = self.half.order[self.place.bits - 1 - self.stage]
        bit = self.place.bit(b)
        fresh = pl.multiple_of(self.block + (1 - 2 * bit) * self.count, 16)
        arrive(self.copy, self.place.home)
        self.block = pl.multiple_of(self.block - bit * self.count, 16)
        self.count *= 2
        self.stage += 1
        self.push(fresh)


def enter_kernel(
    columns, shard, hid, cot, ids, bias, wq, wo, wu, wd,
    full, cfull, ids_o, bias_o, wq_o, wo_o, wu_o, wd_o, send_sems, recv_sems, local_sems,
):
    place, link = Place(columns), Link(send_sems, recv_sems)
    n = shard // CHUNKS
    home, away = place.home, place.away
    k = lax.div(place.d, 2)
    meet([place.core, place.near, place.far, place.swap] + [place.column(m) for m in range(1, columns)])

    def cut(ref, at, count):
        return ref.at[:, pl.ds(at, count)] if len(ref.shape) == 3 else ref.at[pl.ds(at, count)]

    ids_copy = link.send(ids, ids_o, place.swap, away)
    first, near, core = {}, {}, {}

    def open_gather(src, dst, key):
        for i in range(CHUNKS):
            first[key, i] = link.send(rows_of(src, i * n, n), rows_of(dst, i * n, n), place.swap, away)
        for i in range(CHUNKS):
            near[key, i] = link.make(rows_of(src, i * n, n), rows_of(dst, shard + i * n, n), place.near)
            core[key, i] = link.make(rows_of(src, i * n, n), rows_of(dst, 2 * shard + i * n, n), place.core)
            link.start(near[key, i], home)
            link.start(core[key, i], home)

    def second_gather(dst, key):
        for i in range(CHUNKS):
            arrive(first[key, i], away)
            for copy, block, to in ((near[key, i], 1, place.near), (core[key, i], 2, place.core)):
                again = link.make(
                    rows_of(dst, i * n, n), rows_of(dst, block * shard + i * n, n), to, copy
                )
                link.start(again, away)

    def relay(dst, key):
        for i in range(CHUNKS):
            near[key, i].wait_recv()
            core[key, i, 1] = link.send(
                rows_of(dst, shard + i * n, n), rows_of(dst, 3 * shard + i * n, n), place.core
            )

    def drain(key):
        for i in range(CHUNKS):
            core[key, i].wait_recv()
            core[key, i, 1].wait_recv()

    local = []

    def keep(src, dst):
        copy = pltpu.make_async_copy(src, dst, local_sems.at[len(local)])
        pl.when(home)(copy.start)
        local.append(copy)

    pieces = {}

    def open_weight(src, dst, key):
        rows = src.shape[-2]
        unit = rows // (16 * columns) * 16
        rest = rows - unit * columns
        if unit:
            at = pl.multiple_of(k * unit, 16)
            pieces[key] = link.send(cut(src, at, unit), cut(dst, at, unit), place.far, home)
        pieces[key, 1] = None
        if rest:
            at = unit * columns
            pieces[key, 1] = link.send(cut(src, at, rest), cut(dst, at, rest), place.far, home)

    def share_weight(src, dst, key):
        rows = src.shape[-2]
        unit = rows // (16 * columns) * 16
        pieces[key, 2] = []
        if unit:
            arrive(pieces[key], away)
            at = pl.multiple_of(k * unit, 16)
            for m in range(1, columns):
                pieces[key, 2].append(
                    link.send(cut(dst, at, unit), cut(dst, at, unit), place.column(m), away)
                )

    def drain_weight(key):
        if pieces[key, 1] is not None:
            arrive(pieces[key, 1], away)
        for copy in pieces[key, 2]:
            arrive(copy, away)

    open_gather(hid, full, "h")
    open_weight(wq, wq_o, "q")
    open_weight(wo, wo_o, "o")
    bias_copy = link.send(bias, bias_o, place.far, home)
    open_gather(cot, cfull, "c")
    open_weight(wu, wu_o, "u")
    open_weight(wd, wd_o, "d")
    keep(hid, rows_of(full, 0, shard))
    keep(wq, wq_o)
    keep(wo, wo_o)
    keep(ids, ids_o)
    keep(bias, bias_o)
    keep(cot, rows_of(cfull, 0, shard))
    keep(wu, wu_o)
    keep(wd, wd_o)

    second_gather(full, "h")
    share_weight(wq, wq_o, "q")
    share_weight(wo, wo_o, "o")
    relay(full, "h")
    second_gather(cfull, "c")
    share_weight(wu, wu_o, "u")
    relay(cfull, "c")
    share_weight(wd, wd_o, "d")
    drain("h")
    drain("c")
    for key in "qoud":
        drain_weight(key)
    arrive(ids_copy, away)
    arrive(bias_copy, away)
    for copy in local:
        pl.when(home)(copy.wait)
    link.close()


def norm_stats(values):
    center = values - jnp.mean(values, axis=-1, keepdims=True)
    rstd = lax.rsqrt(jnp.mean(center * center, axis=-1, keepdims=True) + EPS)
    return center * rstd, rstd


def norm_pull(grad, hat, rstd, gain):
    gn = grad * gain
    return rstd * (
        gn
        - jnp.mean(gn, axis=-1, keepdims=True)
        - hat * jnp.mean(gn * hat, axis=-1, keepdims=True)
    )


def mid_kernel(
    columns, shard, part, own, vec, mid, full, core_buf, out_buf, near_buf, send_sems, recv_sems
):
    place, link = Place(columns), Link(send_sems, recv_sems)
    n = shard // CHUNKS
    meet([place.core, place.near])
    total = Scatter(link, place, part, core_buf, out_buf, near_buf, shard)
    total.start()
    for i in range(CHUNKS):
        total.pass_on(i)
    near, core = {}, []
    for i in range(CHUNKS):
        total.ready(i)

        def rows(here):
            value = own[here, :].astype(F32) + total.rows(here) + vec[0:1, :]
            mid[here, :] = value
            full[here, :] = (norm_stats(value)[0] * vec[1:2, :] + vec[2:3, :]).astype(BF)

        over_rows(i * n, n, STEP, rows)
        near[i], copy = gather_start(link, place, full, shard, i)
        core.append(copy)
    for i in range(CHUNKS):
        core.append(gather_relay(link, place, full, shard, i, near[i]))
    for copy in core:
        copy.wait_recv()
    link.close()


def back_kernel(
    columns, shard, part, part2, grads_u, grads_d, mid, cot, vec, *refs
):
    place, link = Place(columns), Link(*refs[-2:])
    bits = place.bits
    gmid, full, out, slice_u, slice_d, sums = refs[:6]
    scratch = list(refs[6:-2])
    a_bufs, b_bufs = scratch[:3], scratch[3:6]
    swap_buf = scratch[6]
    halves = scratch[7:]
    n = shard // CHUNKS
    meet([place.core, place.near, place.swap] + [place.column(1 << b) for b in range(bits)])
    total = Scatter(link, place, part, *a_bufs, shard)
    total2 = Scatter(link, place, part2, *b_bufs, shard)
    size = grads_u.shape[0]
    half_u = Halving(
        link, place, grads_u, 0, size, 0, halves[: bits - 1] + [slice_u], halves[bits - 1 : 2 * bits - 1]
    )
    halves = halves[2 * bits - 1 :]
    half_d = Halving(
        link, place, grads_d, 0, size, 1, halves[: bits - 1] + [slice_d], halves[bits - 1 : 2 * bits - 1]
    )
    total.start()
    half_u.start(0)
    half_d.start(0)
    for i in range(CHUNKS):
        total.pass_on(i)
    total2.start()
    sums[...] = jnp.zeros_like(sums)
    near, core = {}, []
    for i in range(CHUNKS):
        total.ready(i)

        def rows(here):
            grad = total.rows(here)
            out_grad = cot[here, :].astype(F32)
            hat, rstd = norm_stats(mid[here, :])
            value = out_grad + norm_pull(grad, hat, rstd, vec[0:1, :])
            gmid[here, :] = value
            full[here, :] = value.astype(BF)
            for row, term in enumerate((value, grad * hat, grad, out_grad)):
                sums[row : row + 1, :] += jnp.sum(term, axis=0, keepdims=True)

        over_rows(i * n, n, STEP, rows)
        near[i], copy = gather_start(link, place, full, shard, i)
        core.append(copy)
    for i in range(CHUNKS):
        total2.pass_on(i)
    for i in range(CHUNKS):
        core.append(gather_relay(link, place, full, shard, i, near[i]))
    for s in range(bits):
        half_u.finish(s)
        if s + 1 < bits:
            half_u.start(s + 1)
        half_d.finish(s)
        if s + 1 < bits:
            half_d.start(s + 1)
    swaps = []
    for i in range(CHUNKS):
        total2.ready(i)

        def rows2(here):
            value = (mid[here, :] + total2.rows(here) + vec[1:2, :]).astype(BF)
            swap_buf[here, :] = value

            @pl.when(place.home)
            def _():
                out[here, :] = value

        over_rows(i * n, n, STEP, rows2)
        swaps.append(
            link.send(rows_of(swap_buf, i * n, n), rows_of(out, i * n, n), place.swap, place.away)
        )
    for copy in core:
        copy.wait_recv()
    for copy in swaps:
        arrive(copy, place.away)
    link.close()


def exit_kernel(
    columns, shard, part, own, gmid, slice_u, slice_d, grads_a, small_in, vec, *refs
):
    place, link = Place(columns), Link(*refs[-2:])
    bits = place.bits
    inp, full_u, full_d, full_a, small = refs[:5]
    scratch = list(refs[5:-2])
    a_bufs = scratch[:3]
    swap_buf, far_u, far_d, far_a0, far_a1 = scratch[3:8]
    steps = bits + 3
    sum_own, sum_got = scratch[8 : 8 + steps], scratch[8 + steps : 8 + 2 * steps]
    halves = scratch[8 + 2 * steps :]
    n = shard // CHUNKS
    hops = [place.core] + [place.column(1 << b) for b in range(bits)] + [place.near, place.far]
    meet(hops + [place.swap])
    size = full_u.shape[0]
    total = Scatter(link, place, part, *a_bufs, shard)
    half_a = []
    for side in range(2):
        half_a.append(
            Halving(
                link, place, grads_a, side * (size // 2), size // 2, side,
                halves[:bits], halves[bits : 2 * bits],
            )
        )
        halves = halves[2 * bits :]
    half_u = Halving(link, place, None, 0, size, 0, [], [])
    half_d = Halving(link, place, None, 0, size, 1, [], [])
    double = [
        Doubling(link, place, half_u, full_u, slice_u, far_u),
        Doubling(link, place, half_d, full_d, slice_d, far_d),
        Doubling(link, place, half_a[0], full_a, half_a[0].work[bits - 1], far_a0),
        Doubling(link, place, half_a[1], full_a, half_a[1].work[bits - 1], far_a1),
    ]
    total.start()
    half_a[0].start(0)
    half_a[1].start(0)
    for i in range(CHUNKS):
        total.pass_on(i)
    double[0].start()
    double[1].start()
    sum_own[0][...] = small_in[...]
    swaps = []
    for i in range(CHUNKS):
        total.ready(i)

        def rows(here):
            grad = total.rows(here)
            hat, rstd = norm_stats(own[here, :].astype(F32))
            value = (gmid[here, :] + norm_pull(grad, hat, rstd, vec[0:1, :])).astype(BF)
            swap_buf[here, :] = value
            for row, term in enumerate((grad * hat, grad)):
                sum_own[0][row : row + 1, :] += jnp.sum(term, axis=0, keepdims=True)

            @pl.when(place.home)
            def _():
                inp[here, :] = value

        over_rows(i * n, n, STEP, rows)
        swaps.append(
            link.send(rows_of(swap_buf, i * n, n), rows_of(inp, i * n, n), place.swap, place.away)
        )
    hop_copies = [link.send(sum_own[0], sum_got[0], hops[0])]

    def next_hop(s):
        hop_copies[s].wait_recv()
        into = small if s + 1 == steps else sum_own[s + 1]
        into[...] = sum_own[s][...] + sum_got[s][...]
        if s + 1 < steps:
            hop_copies.append(link.send(sum_own[s + 1], sum_got[s + 1], hops[s + 1]))

    hop = 0
    for s in range(bits):
        for half in half_a:
            half.finish(s)
            if s + 1 < bits:
                half.start(s + 1)
        if hop < steps:
            next_hop(hop)
            hop += 1
    double[2].start()
    double[3].start()
    double[0].join()
    double[1].join()
    if hop < steps:
        next_hop(hop)
        hop += 1
    for s in range(bits):
        double[0].advance()
        double[1].advance()
        if hop < steps:
            next_hop(hop)
            hop += 1
        if s == 0:
            double[2].join()
            double[3].join()
    for s in range(bits):
        double[2].advance()
        double[3].advance()
        if hop < steps:
            next_hop(hop)
            hop += 1
    while hop < steps:
        next_hop(hop)
        hop += 1
    for one in double:
        for copy in one.cores:
            arrive(copy, place.away)
    for copy in swaps:
        arrive(copy, place.away)
    link.close()


def any_space():
    return pl.BlockSpec(memory_space=pl.ANY)


SEMS = 112


def sems():
    return [pltpu.SemaphoreType.DMA((SEMS,)), pltpu.SemaphoreType.DMA((SEMS,))]


def remote_call(name, kernel, number, outs, in_specs, scratch, cost=None):
    return pl.pallas_call(
        kernel,
        out_shape=outs,
        in_specs=in_specs,
        out_specs=jax.tree.map(lambda _: vmem(), outs),
        scratch_shapes=scratch + sems(),
        compiler_params=pltpu.CompilerParams(
            collective_id=number, has_side_effects=True, vmem_limit_bytes=60 << 20
        ),
        name=name,
    )


def shaped(shape, dtype):
    return jax.ShapeDtypeStruct(shape, dtype)


def enter(columns, hid, cot, ids, bias, wq, wo, wu, wd):
    shard, model = hid.shape
    outs = (
        shaped((4 * shard, model), BF),
        shaped((4 * shard, model), BF),
        shaped(ids.shape, ids.dtype),
        shaped(bias.shape, F32),
        shaped(wq.shape, BF),
        shaped(wo.shape, BF),
        shaped(wu.shape, BF),
        shaped(wd.shape, BF),
    )
    kernel = functools.partial(enter_kernel, columns, shard)
    call = pl.pallas_call(
        kernel,
        out_shape=outs,
        in_specs=[any_space()] * 8,
        out_specs=tuple(vmem() for _ in outs),
        scratch_shapes=[
            pltpu.SemaphoreType.DMA((48 + 6 * columns,)),
            pltpu.SemaphoreType.DMA((48 + 6 * columns,)),
            pltpu.SemaphoreType.DMA((8,)),
        ],
        compiler_params=pltpu.CompilerParams(
            collective_id=0, has_side_effects=True, vmem_limit_bytes=60 << 20
        ),
        name="enter",
    )
    return call(hid, cot, ids, bias, wq, wo, wu, wd)


def make_mid(columns, part, own, vec):
    shard, model = own.shape
    outs = (shaped((shard, model), F32), shaped((4 * shard, model), BF))
    call = remote_call(
        "mid", functools.partial(mid_kernel, columns, shard), 1, outs, [vmem()] * 3,
        scatter_scratch(shard, model),
    )
    return call(part, own, vec)


def make_back(columns, part, part2, grads_u, grads_d, mid, cot, vec):
    shard, model = mid.shape
    bits = columns.bit_length() - 1
    size = grads_u.shape[0]
    outs = (
        shaped((shard, model), F32),
        shaped((4 * shard, model), BF),
        shaped((shard, model), BF),
        shaped((size // columns, model), BF),
        shaped((size // columns, model), BF),
        shaped((8, model), F32),
    )
    per_side = halving_scratch(size, bits, model)
    halves = per_side[: bits - 1] + per_side
    call = remote_call(
        "back", functools.partial(back_kernel, columns, shard), 2, outs, [vmem()] * 7,
        scatter_scratch(shard, model)
        + scatter_scratch(shard, model)
        + [pltpu.VMEM((shard, model), BF)]
        + halves
        + halves,
    )
    return call(part, part2, grads_u, grads_d, mid, cot, vec)


def make_exit(columns, part, own, gmid, slice_u, slice_d, grads_a, small, vec):
    shard, model = own.shape
    bits = columns.bit_length() - 1
    size = grads_a.shape[0]
    outs = (
        shaped((shard, model), BF),
        shaped((size, model), BF),
        shaped((size, model), BF),
        shaped((size, model), BF),
        shaped(small.shape, F32),
    )
    n = size // columns
    per_side = halving_scratch(size // 2, bits, model)
    steps = bits + 3
    call = remote_call(
        "exit", functools.partial(exit_kernel, columns, shard), 3, outs, [vmem()] * 8,
        scatter_scratch(shard, model)
        + [
            pltpu.VMEM((shard, model), BF),
            pltpu.VMEM((n, model), BF),
            pltpu.VMEM((n, model), BF),
            pltpu.VMEM((n // 2, model), BF),
            pltpu.VMEM((n // 2, model), BF),
        ]
        + [pltpu.VMEM(small.shape, F32)] * (2 * steps)
        + (per_side + per_side) * 2,
    )
    return call(part, own, gmid, slice_u, slice_d, grads_a, small, vec)


def mm(a, b):
    return jnp.dot(a, b, preferred_element_type=F32)


def mm_nt(a, b):
    return lax.dot_general(a, b, (((1,), (1,)), ((), ())), preferred_element_type=F32)


def mm_tn(a, b):
    return lax.dot_general(a, b, (((0,), (0,)), ((), ())), preferred_element_type=F32)


def stack_rows(rows, model):
    rows = [jnp.pad(r, (0, model - r.shape[0])) for r in rows]
    rows = rows + [jnp.zeros((model,), F32)] * (-len(rows) % 8)
    return jnp.stack(rows)


def body(
    hidden,
    segment_ids,
    lengths,
    norm1_gain,
    norm1_shift,
    qkv_weight,
    qv_bias,
    out_weight,
    out_bias,
    norm2_gain,
    norm2_shift,
    up_weight,
    up_bias,
    down_weight,
    down_bias,
    cotangent,
):
    _, shard, model = hidden.shape
    seq = segment_ids.shape[1]
    width = qkv_weight.shape[2]
    d, t = lax.axis_index("dp"), lax.axis_index("tensor")
    columns = lax.axis_size("dp") // 2
    rank = 2 * (d & 1) + (t & 1)

    ids = jnp.concatenate([segment_ids[0], lengths, jnp.zeros((LANES - 1,), jnp.int32)])
    ids = jnp.broadcast_to(ids[None], (8, seq + LANES))
    bias = jnp.broadcast_to(jnp.concatenate([qv_bias.reshape(-1), up_bias])[None], (8, 2 * width + up_bias.shape[0]))
    full, cot_full, ids, bias, w_qkv, w_out, w_up, w_down = enter(
        columns, hidden[0], cotangent[0], ids, bias, qkv_weight, out_weight, up_weight, down_weight
    )
    length = ids[0, seq]
    places = jnp.arange(seq, dtype=jnp.int32)
    ids = jnp.where(places < length, ids[0, :seq], 16 + places)
    start = jnp.sum((ids[None, :] < ids[:, None]).astype(jnp.int32), axis=1)
    meta = jnp.concatenate([rank[None], start[::BLK] // BLK]).astype(jnp.int32)
    start = start[None, :]
    b_q, b_v, b_up = bias[0, :width], bias[0, width : 2 * width], bias[0, 2 * width :]
    own, cot_own = full[:shard], cot_full[:shard]

    normed1 = (norm_stats(full.astype(F32))[0] * norm1_gain + norm1_shift).astype(BF)
    q = (mm(normed1, w_qkv[0]) + b_q).astype(BF)
    k = mm(normed1, w_qkv[1]).astype(BF)
    v = (mm(normed1, w_qkv[2]) + b_v).astype(BF)
    attended, lse = attn_fwd(meta, start, q, k, v, shard)

    mid, normed2 = make_mid(
        columns, mm(attended, w_out).astype(BF), own, stack_rows([out_bias, norm2_gain, norm2_shift], model)
    )
    inner = mm(normed2, w_up) + b_up
    c0 = math.sqrt(2.0 / math.pi)
    tanh = jnp.tanh(c0 * (inner + 0.044715 * inner * inner * inner))
    active = (0.5 * inner * (1.0 + tanh)).astype(BF)
    slope = 0.5 * (1.0 + tanh) + 0.5 * inner * (1.0 - tanh * tanh) * c0 * (
        1.0 + 3 * 0.044715 * inner * inner
    )
    grad_inner = (mm_nt(cot_full, w_down) * slope).astype(BF)
    unit = 32 * columns
    pad = -model % unit
    up_grad = jnp.pad(mm_tn(normed2, grad_inner).astype(BF), ((0, pad), (0, 0)))
    down_grad = jnp.pad(mm_tn(active, cot_full).astype(BF), ((0, pad), (0, 0)))
    grad_mid, gm_full, output, slice_u, slice_d, sums = make_back(
        columns,
        mm_nt(grad_inner, w_up).astype(BF),
        mm(active, w_down).astype(BF),
        up_grad,
        down_grad,
        mid,
        cot_own,
        stack_rows([norm2_gain, down_bias], model),
    )
    grad_attended = mm_nt(gm_full, w_out).astype(BF)
    dq, dk, dv = attn_bwd(meta, start, q, k, v, attended, grad_attended, lse, shard)
    part1 = mm_nt(dq, w_qkv[0]) + mm_nt(dk, w_qkv[1]) + mm_nt(dv, w_qkv[2])
    att_grad = jnp.concatenate(
        [mm_tn(dq, normed1), mm_tn(dk, normed1), mm_tn(dv, normed1), mm_tn(attended, gm_full)], axis=0
    ).astype(BF)
    att_grad = jnp.pad(att_grad, ((0, pad), (0, 0)))

    qv_grad = jnp.concatenate([jnp.sum(dq, axis=0, dtype=F32), jnp.sum(dv, axis=0, dtype=F32)])
    qv_grad = jnp.pad(qv_grad, (0, model - 2 * width))
    up_b_grad = jnp.sum(grad_inner, axis=0, dtype=F32)
    slots = lax.broadcasted_iota(jnp.int32, (4, 1), 0) == rank
    small = jnp.concatenate(
        [
            jnp.zeros((2, model), F32),
            sums[:4],
            jnp.zeros((2, model), F32),
            jnp.where(slots, up_b_grad[None], 0.0),
            jnp.where(slots, qv_grad[None], 0.0),
        ]
    )
    input_grad, up_grad, down_grad, att_grad, small = make_exit(
        columns,
        part1.astype(BF),
        own,
        grad_mid,
        slice_u,
        slice_d,
        att_grad,
        small,
        stack_rows([norm1_gain], model),
    )
    quarter = lax.dynamic_slice_in_dim(small, 12 + t, 1, 0)[0, : 2 * width].reshape(2, width)
    qkv_grad = att_grad[: 3 * width].reshape(3, width, model).astype(F32)
    return (
        output[None],
        input_grad[None],
        small[0],
        small[1],
        jnp.swapaxes(qkv_grad, 1, 2),
        quarter,
        att_grad[3 * width : 4 * width].astype(F32),
        small[2],
        small[3],
        small[4],
        up_grad[:model].astype(F32),
        lax.dynamic_slice_in_dim(small, 8 + t, 1, 0)[0],
        down_grad[:model].astype(F32),
        small[5],
    )


def solution(mesh):
    in_specs = (
        P("dp", "tensor", None),
        P("dp", None),
        P("dp"),
        P(),
        P(),
        P(None, None, "tensor"),
        P(None, "tensor"),
        P("tensor", None),
        P(),
        P(),
        P(),
        P(None, "tensor"),
        P("tensor"),
        P("tensor", None),
        P(),
        P("dp", "tensor", None),
    )
    out_specs = (
        P("dp", "tensor", None),
        P("dp", "tensor", None),
        P(),
        P(),
        P(None, None, "tensor"),
        P(None, "tensor"),
        P("tensor", None),
        P(),
        P(),
        P(),
        P(None, "tensor"),
        P("tensor"),
        P("tensor", None),
        P(),
    )
    return jax.shard_map(body, mesh=mesh, in_specs=in_specs, out_specs=out_specs, check_vma=False)
```

```python
import functools
import math

import jax
import jax.numpy as jnp
from jax import lax
from jax.experimental import pallas as pl
from jax.experimental.pallas import tpu as pltpu
from jax.sharding import PartitionSpec as P

HEAD = 56
EPS = 1e-05
LANES = 128
BLK = 256
BF = jnp.bfloat16
F32 = jnp.float32


def mm(a, b):
    return jnp.dot(a, b, preferred_element_type=F32)


def mm_nt(a, b):
    return lax.dot_general(a, b, (((1,), (1,)), ((), ())), preferred_element_type=F32)


def mm_tn(a, b):
    return lax.dot_general(a, b, (((0,), (0,)), ((), ())), preferred_element_type=F32)


def head_window(h):
    lo, hi = h * HEAD, (h + 1) * HEAD
    first = lo // LANES * LANES
    last = -(-hi // LANES) * LANES
    return first, last


def head_mask(h, rows):
    first, last = head_window(h)
    lane = lax.broadcasted_iota(jnp.int32, (rows, last - first), 1) + first
    return (lane >= h * HEAD) & (lane < (h + 1) * HEAD)


def stage_in(rank, src, dst, shard, width):
    wide = dst.shape[1]
    for s in range(src.shape[0] // shard):
        rel = pl.multiple_of((rank ^ s) * shard, 16)
        dst[s * shard : (s + 1) * shard, :width] = src[pl.ds(rel, shard), :]
    if wide > width:
        dst[:, width:] = jnp.zeros((dst.shape[0], wide - width), dst.dtype)


def project(rank, src, shard, width, products):
    @pl.loop(0, src.shape[0] // shard)
    def _(s):
        rel = pl.multiple_of((rank ^ s) * shard, 16)
        rows = pl.ds(pl.multiple_of(s * shard, 16), shard)
        x = src[pl.ds(rel, shard), :]
        for dst, weight, bias in products:
            value = dot_nt(x, weight[...])
            if bias is not None:
                value = value + bias
            dst[rows, :width] = value.astype(BF)

    for dst, _, _ in products:
        if dst.shape[1] > width:
            dst[:, width:] = jnp.zeros((dst.shape[0], dst.shape[1] - width), BF)


def stage_out(rank, src, dst, shard, width):
    for s in range(dst.shape[0] // shard):
        rel = pl.multiple_of((rank ^ s) * shard, 16)
        dst[pl.ds(rel, shard), :] = src[s * shard : (s + 1) * shard, :width]


def tile_mask(start_row, qb, kb):
    kpos = kb * BLK + lax.broadcasted_iota(jnp.int32, (BLK, BLK), 0)
    qpos = qb * BLK + lax.broadcasted_iota(jnp.int32, (BLK, BLK), 1)
    return (kpos <= qpos) & (kpos >= start_row)


def dot_nt(a, b):
    return lax.dot_general(a, b, (((1,), (1,)), ((), ())), preferred_element_type=F32)


def attn_fwd_kernel(heads, shard, meta, start, normed, wq, bias, out, lse, qs, ks, vs, vt, os, ot, ms, ls, acc):
    seq, width = out.shape
    scale2 = HEAD ** (-0.5) * math.log2(math.e)
    rank = meta[0]
    b_q, b_v = bias[0:1, :], bias[1:2, :]
    project(
        rank, normed, shard, width, [(qs, wq.at[0], b_q), (ks, wq.at[1], None), (vs, wq.at[2], b_v)]
    )
    blocks = seq // BLK

    @pl.loop(0, blocks)
    def _(b):
        rows = pl.ds(pl.multiple_of(b * BLK, BLK), BLK)
        flipped = vs[rows, :].astype(F32).T
        for h in range(heads):
            vt[h, :, rows] = flipped[h * HEAD : (h + 1) * HEAD, :].astype(BF)

    lse[...] = jnp.zeros_like(lse)

    @pl.loop(0, blocks)
    def _(b):
        rows = pl.ds(pl.multiple_of(b * BLK, BLK), BLK)
        start_row = start[0:1, rows]
        ms[...] = jnp.full_like(ms, -1e30)
        ls[...] = jnp.zeros_like(ls)
        acc[...] = jnp.zeros_like(acc)

        def tile(kb, carry):
            krows = pl.ds(pl.multiple_of(kb * BLK, BLK), BLK)
            mask = tile_mask(start_row, b, kb)
            for h in range(heads):
                first, last = head_window(h)
                qm = jnp.where(head_mask(h, BLK), qs[rows, first:last], 0)
                s = dot_nt(ks[krows, first:last], qm) * scale2
                s = jnp.where(mask, s, -1e30)
                old = ms[h : h + 1, :]
                new = jnp.maximum(old, jnp.max(s, axis=0, keepdims=True))
                p = jnp.exp2(s - new)
                p = jnp.where(mask, p, 0.0)
                fade = jnp.exp2(old - new)
                ms[h : h + 1, :] = new
                ls[h : h + 1, :] = ls[h : h + 1, :] * fade + jnp.sum(p, axis=0, keepdims=True)
                acc[h] = acc[h] * fade + jnp.dot(
                    vt[h, :, krows], p.astype(BF), preferred_element_type=F32
                )
            return carry

        lax.fori_loop(meta[1 + b], b + 1, tile, 0)
        for h in range(heads):
            total = ls[h : h + 1, :]
            lse[h : h + 1, rows] = ms[h : h + 1, :] + jnp.log(total) * math.log2(math.e)
            ot[h * HEAD : (h + 1) * HEAD, :] = acc[h] / total
        os[rows, :] = ot[...].T.astype(BF)

    stage_out(rank, os, out, shard, width)


def attn_bwd_kernel(
    heads, shard, meta, start, qs, ks, vs, o, gm, wo, lse, dq, dk, dv,
    os, dos, kt, delta, dqs, dks, dvs, dqt, qm, dm,
):
    seq, width = o.shape
    scale = HEAD ** (-0.5)
    scale2 = scale * math.log2(math.e)
    rank = meta[0]
    blocks = seq // BLK
    stage_in(rank, o, os, shard, width)
    project(rank, gm, shard, width, [(dos, wo, None)])

    @pl.loop(0, blocks)
    def _(b):
        rows = pl.ds(pl.multiple_of(b * BLK, BLK), BLK)
        flipped = (os[rows, :].astype(F32) * dos[rows, :].astype(F32)).T
        for h in range(heads):
            delta[h : h + 1, rows] = jnp.sum(
                flipped[h * HEAD : (h + 1) * HEAD, :], axis=0, keepdims=True
            )

    @pl.loop(0, blocks)
    def _(b):
        rows = pl.ds(pl.multiple_of(b * BLK, BLK), BLK)
        flipped = ks[rows, :].astype(F32).T
        for h in range(heads):
            kt[h, :, rows] = flipped[h * HEAD : (h + 1) * HEAD, :].astype(BF)

    dks[...] = jnp.zeros_like(dks)
    dvs[...] = jnp.zeros_like(dvs)
    dqt[...] = jnp.zeros_like(dqt)

    @pl.loop(0, blocks)
    def _(b):
        rows = pl.ds(pl.multiple_of(b * BLK, BLK), BLK)
        start_row = start[0:1, rows]
        dqt[...] = jnp.zeros_like(dqt)
        for h in range(heads):
            first, last = head_window(h)
            keep = head_mask(h, BLK)
            qm[h, :, : last - first] = jnp.where(keep, qs[rows, first:last], 0)
            dm[h, :, : last - first] = jnp.where(keep, dos[rows, first:last], 0)

        def tile(kb, carry):
            krows = pl.ds(pl.multiple_of(kb * BLK, BLK), BLK)
            mask = tile_mask(start_row, b, kb)
            for h in range(heads):
                first, last = head_window(h)
                qh = qm[h, :, : last - first]
                dh = dm[h, :, : last - first]
                s = dot_nt(ks[krows, first:last], qh) * scale2
                p = jnp.where(mask, jnp.exp2(s - lse[h : h + 1, rows]), 0.0)
                dp = dot_nt(vs[krows, first:last], dh)
                ds = (p * (dp - delta[h : h + 1, rows])).astype(BF)
                dvs[krows, first:last] += jnp.dot(p.astype(BF), dh, preferred_element_type=F32)
                dks[krows, first:last] += jnp.dot(ds, qh, preferred_element_type=F32)
                dqt[h * HEAD : (h + 1) * HEAD, :] += jnp.dot(
                    kt[h, :, krows], ds, preferred_element_type=F32
                )
            return carry

        lax.fori_loop(meta[1 + b], b + 1, tile, 0)
        dqs[rows, :] = (dqt[...].T * scale).astype(BF)

    stage_out(rank, dqs, dq, shard, width)
    for s in range(seq // shard):
        rel = pl.multiple_of((rank ^ s) * shard, 16)
        here = slice(s * shard, (s + 1) * shard)
        dk[pl.ds(rel, shard), :] = (dks[here, :width] * scale).astype(BF)
        dv[pl.ds(rel, shard), :] = dvs[here, :width].astype(BF)


def vmem():
    return pl.BlockSpec(memory_space=pltpu.VMEM)


def smem():
    return pl.BlockSpec(memory_space=pltpu.SMEM)


def attn_cost(seq, width, products):
    return pl.CostEstimate(
        flops=products * seq * seq * width,
        bytes_accessed=8 * seq * width * 2,
        transcendentals=seq * seq * width // (2 * HEAD),
    )


def attn_fwd(meta, start, normed, wq, bias, shard):
    seq, (_, width, _) = normed.shape[0], wq.shape
    heads = width // HEAD
    wide = -(-width // LANES) * LANES
    staged = jax.ShapeDtypeStruct((seq, wide), BF)
    return pl.pallas_call(
        functools.partial(attn_fwd_kernel, heads, shard),
        out_shape=(
            jax.ShapeDtypeStruct((seq, width), BF),
            jax.ShapeDtypeStruct((8, seq), F32),
            staged,
            staged,
            staged,
        ),
        in_specs=[smem()] + [vmem()] * 4,
        out_specs=(vmem(),) * 5,
        scratch_shapes=[
            pltpu.VMEM((heads, HEAD, seq), BF),
            pltpu.VMEM((seq, wide), BF),
            pltpu.VMEM((wide, BLK), F32),
            pltpu.VMEM((8, BLK), F32),
            pltpu.VMEM((8, BLK), F32),
            pltpu.VMEM((heads, HEAD, BLK), F32),
        ],
        cost_estimate=attn_cost(seq, width, 3),
        name="attn_fwd",
    )(meta, start, normed, wq, bias)


def attn_bwd(meta, start, q, k, v, o, gm, wo, lse, shard):
    seq, width = o.shape
    heads = width // HEAD
    wide = q.shape[1]
    grad = jax.ShapeDtypeStruct((seq, width), BF)
    return pl.pallas_call(
        functools.partial(attn_bwd_kernel, heads, shard),
        out_shape=(grad, grad, grad),
        in_specs=[smem()] + [vmem()] * 8,
        out_specs=(vmem(), vmem(), vmem()),
        scratch_shapes=[
            pltpu.VMEM((seq, wide), BF),
            pltpu.VMEM((seq, wide), BF),
            pltpu.VMEM((heads, HEAD, seq), BF),
            pltpu.VMEM((8, seq), F32),
            pltpu.VMEM((seq, wide), BF),
            pltpu.VMEM((seq, wide), F32),
            pltpu.VMEM((seq, wide), F32),
            pltpu.VMEM((wide, BLK), F32),
            pltpu.VMEM((heads, BLK, 2 * LANES), BF),
            pltpu.VMEM((heads, BLK, 2 * LANES), BF),
        ],
        cost_estimate=attn_cost(seq, width, 8),
        name="attn_bwd",
    )(meta, start, q, k, v, o, gm, wo, lse)


MESH = pl.DeviceIdType.MESH
CHUNKS = 2
STEP = 32


class Place:
    def __init__(self, columns):
        d, t = lax.axis_index("dp"), lax.axis_index("tensor")
        core, low, high = lax.rem(d, 2), lax.rem(t, 2), lax.div(t, 2)
        self.d, self.t, self.columns = d, t, columns
        self.bits = columns.bit_length() - 1
        self.core = (d + 1 - 2 * core, t)
        self.near = (d, t + 1 - 2 * low)
        self.far = (d, t + 2 - 4 * high)
        self.swap = (d + 1 - 2 * core, t + 2 - 4 * high)
        self.home = core == high
        self.away = core != high

    def bit(self, b):
        return lax.rem(lax.div(self.d, 2 << b), 2)

    def column(self, m):
        d = self.d
        for b in range(self.bits):
            if (m >> b) & 1:
                d = d + (2 << b) * (1 - 2 * self.bit(b))
        return (d, self.t)


class Link:
    def __init__(self, send_sems, recv_sems):
        self.send_sems, self.recv_sems = send_sems, recv_sems
        self.count = 0
        self.open, self.kept, self.number = [], [], {}

    def make(self, src, dst, to, like=None):
        if like is None:
            i = self.count
            self.count += 1
        else:
            i = self.number[id(like)]
        copy = pltpu.make_async_remote_copy(
            src_ref=src,
            dst_ref=dst,
            send_sem=self.send_sems.at[i],
            recv_sem=self.recv_sems.at[i],
            device_id=to,
            device_id_type=MESH,
        )
        self.number[id(copy)] = i
        self.kept.append(copy)
        return copy

    def start(self, copy, when=None):
        if when is None:
            copy.start()
        else:
            pl.when(when)(copy.start)
        self.open.append((copy, when))

    def send(self, src, dst, to, when=None):
        copy = self.make(src, dst, to)
        self.start(copy, when)
        return copy

    def close(self):
        for copy, when in self.open:
            if when is None:
                copy.wait_send()
            else:
                pl.when(when)(copy.wait_send)


def arrive(copy, when=None):
    if when is None:
        copy.wait_recv()
    else:
        pl.when(when)(copy.wait_recv)


def meet(partners):
    barrier = pltpu.get_barrier_semaphore()
    for to in partners:
        pl.semaphore_signal(barrier, inc=1, device_id=to, device_id_type=MESH)
    pl.semaphore_wait(barrier, len(partners))


def row_of(ref):
    return ref[...][None, :]


def rows_of(ref, first, count):
    return ref.at[pl.ds(first, count)]


def gather_start(link, place, full, shard, i):
    n = shard // CHUNKS
    near = link.send(rows_of(full, i * n, n), rows_of(full, shard + i * n, n), place.near)
    core = link.send(rows_of(full, i * n, n), rows_of(full, 2 * shard + i * n, n), place.core)
    return near, core


def gather_relay(link, place, full, shard, i, near):
    n = shard // CHUNKS
    near.wait_recv()
    return link.send(
        rows_of(full, shard + i * n, n), rows_of(full, 3 * shard + i * n, n), place.core
    )


class Scatter:
    def __init__(self, link, place, make, part, core_buf, out_buf, near_buf, shard):
        self.link, self.place, self.make, self.part = link, place, make, part
        self.core_buf, self.out_buf, self.near_buf = core_buf, out_buf, near_buf
        self.shard, self.n = shard, shard // CHUNKS
        self.core, self.near = {}, {}

    def fill(self, block):
        rows = pl.ds(pl.multiple_of(block * self.shard, 16), self.shard)
        self.part[rows, :] = self.make(rows).astype(BF)

    def to_core(self, block):
        for i in range(CHUNKS):
            at = (block - 2) * self.shard + i * self.n
            self.core[block - 2, i] = self.link.send(
                rows_of(self.part, 2 * self.shard + at, self.n),
                rows_of(self.core_buf, at, self.n),
                self.place.core,
            )

    def start(self):
        self.fill(3)
        self.to_core(3)
        self.fill(1)

    def rest(self):
        @pl.loop(0, 2)
        def _(b):
            self.fill(2 - 2 * b)

        self.to_core(2)

    def pass_on(self, i):
        at = self.shard + i * self.n
        self.core[1, i].wait_recv()

        @pl.loop(0, self.n // STEP)
        def _(r):
            here = pl.multiple_of(at + r * STEP, STEP)
            there = pl.multiple_of(i * self.n + r * STEP, STEP)
            total = self.part[pl.ds(here, STEP), :].astype(F32) + self.core_buf[
                pl.ds(here, STEP), :
            ].astype(F32)
            self.out_buf[pl.ds(there, STEP), :] = total.astype(BF)

        self.near[i] = self.link.send(
            rows_of(self.out_buf, i * self.n, self.n),
            rows_of(self.near_buf, i * self.n, self.n),
            self.place.near,
        )

    def pair(self, rows):
        return self.part[rows, :].astype(F32) + self.core_buf[rows, :].astype(F32)

    def ready(self, i):
        self.core[0, i].wait_recv()
        self.near[i].wait_recv()

    def rows(self, rows):
        return (
            self.part[rows, :].astype(F32)
            + self.core_buf[rows, :].astype(F32)
            + self.near_buf[rows, :].astype(F32)
        )


class Spread:
    def __init__(self, link, place, src, dst):
        self.link, self.place, self.src, self.dst = link, place, src, dst
        rows = src.shape[-2]
        self.unit = rows // (16 * place.columns) * 16
        self.rest = rows - self.unit * place.columns
        self.at = pl.multiple_of(lax.div(place.d, 2) * self.unit, 16)
        self.pieces, self.shared = [], []

    def cut(self, ref, at, count):
        return ref.at[:, pl.ds(at, count)] if len(ref.shape) == 3 else ref.at[pl.ds(at, count)]

    def move(self, src, at, count, to, when):
        return self.link.send(self.cut(src, at, count), self.cut(self.dst, at, count), to, when)

    def open(self):
        far, home = self.place.far, self.place.home
        if self.unit:
            self.first = self.move(self.src, self.at, self.unit, far, home)
        if self.rest:
            at = self.unit * self.place.columns
            self.pieces.append(self.move(self.src, at, self.rest, far, home))

    def share(self):
        away = self.place.away
        if self.unit:
            arrive(self.first, away)
            for m in range(1, self.place.columns):
                to = self.place.column(m)
                self.pieces.append(self.move(self.dst, self.at, self.unit, to, away))

    def drain(self):
        for copy in self.pieces:
            arrive(copy, self.place.away)


class Local:
    def __init__(self, sems, when=None, base=0):
        self.sems, self.when, self.base, self.copies = sems, when, base, []

    def keep(self, src, dst):
        copy = pltpu.make_async_copy(src, dst, self.sems.at[self.base + len(self.copies)])
        self.copies.append(copy)
        self.run(copy.start)
        return copy

    def run(self, act):
        if self.when is None:
            act()
        else:
            pl.when(self.when)(act)

    def drain(self, first=0):
        for copy in self.copies[first:]:
            self.run(copy.wait)


def pack(local, sources, buf):
    block = buf.shape[0] // len(sources)
    for j, src in enumerate(sources):
        count = src.shape[0]
        local.keep(src, rows_of(buf, j * block, count))
        if count < block:
            buf[j * block + count : (j + 1) * block, :] = jnp.zeros((block - count, buf.shape[1]), buf.dtype)


def scatter_scratch(shard, model):
    return [
        pltpu.VMEM((4 * shard, model), BF),
        pltpu.VMEM((2 * shard, model), BF),
        pltpu.VMEM((shard, model), BF),
        pltpu.VMEM((shard, model), BF),
    ]


def over_rows(first, count, step, fn):
    @pl.loop(0, count // step)
    def _(r):
        fn(pl.ds(pl.multiple_of(first + r * step, 16), step))


class Halving:
    def __init__(self, link, place, source, first, size, turn, work, got):
        self.link, self.place = link, place
        self.source, self.first, self.size = source, first, size
        self.order = [(b + turn) % place.bits for b in range(place.bits)]
        self.work, self.got = work, got
        self.copies = []

    def start(self, s):
        n = self.size >> (s + 1)
        bit = self.place.bit(self.order[s])
        src, base = (self.source, self.first) if s == 0 else (self.work[s - 1], 0)
        at = pl.multiple_of(base + (1 - bit) * n, 16)
        self.copies.append(
            self.link.send(
                rows_of(src, at, n), self.got[s], self.place.column(1 << self.order[s])
            )
        )

    def finish(self, s):
        n = self.size >> (s + 1)
        bit = self.place.bit(self.order[s])
        src, base = (self.source, self.first) if s == 0 else (self.work[s - 1], 0)
        self.copies[s].wait_recv()

        @pl.loop(0, n // 16)
        def _(r):
            here = pl.multiple_of(base + bit * n + r * 16, 16)
            to = pl.ds(pl.multiple_of(r * 16, 16), 16)
            total = src[pl.ds(here, 16), :].astype(F32) + self.got[s][to, :].astype(F32)
            self.work[s][to, :] = total.astype(BF)

    def offset(self):
        at, n = 0, self.size
        for b in self.order:
            n //= 2
            at = at + self.place.bit(b) * n
        return self.first + at


def halving_scratch(size, bits, model):
    return [pltpu.VMEM((size >> (s + 1), model), BF) for s in range(bits)]


class Doubling:
    def __init__(self, link, place, half, full, slice_ref, far_buf):
        self.link, self.place, self.half, self.full = link, place, half, full
        self.far = None
        self.slice_ref, self.far_buf = slice_ref, far_buf
        self.n = half.size >> place.bits
        self.at = half.offset()
        self.cores, self.waits = [], []

    def start(self):
        self.far = self.link.send(
            self.slice_ref, self.far_buf, self.place.far, self.place.away
        )

    def to_core(self, at, n):
        self.link.send(
            rows_of(self.full, at, n), rows_of(self.full, at, n), self.place.core, self.place.home
        )

    def join(self):
        if self.far is not None:
            arrive(self.far, self.place.home)

        @pl.when(self.place.home)
        def _():
            @pl.loop(0, self.n // 16)
            def _(r):
                here = pl.ds(pl.multiple_of(r * 16, 16), 16)
                to = pl.ds(pl.multiple_of(self.at + r * 16, 16), 16)
                total = self.slice_ref[here, :].astype(F32) + self.far_buf[here, :].astype(F32)
                self.full[to, :] = total.astype(BF)

        self.block, self.count = pl.multiple_of(self.at, 16), self.n
        self.stage = 0
        self.push(self.block)

    def push(self, fresh):
        if self.stage < self.place.bits:
            b = self.half.order[self.place.bits - 1 - self.stage]
            self.copy = self.link.send(
                rows_of(self.full, self.block, self.count),
                rows_of(self.full, self.block, self.count),
                self.place.column(1 << b),
                self.place.home,
            )
        copy = self.link.send(
            rows_of(self.full, fresh, self.count if self.stage == 0 else self.count // 2),
            rows_of(self.full, fresh, self.count if self.stage == 0 else self.count // 2),
            self.place.core,
            self.place.home,
        )
        self.cores.append(copy)

    def advance(self):
        b = self.half.order[self.place.bits - 1 - self.stage]
        bit = self.place.bit(b)
        fresh = pl.multiple_of(self.block + (1 - 2 * bit) * self.count, 16)
        arrive(self.copy, self.place.home)
        self.block = pl.multiple_of(self.block - bit * self.count, 16)
        self.count *= 2
        self.stage += 1
        self.push(fresh)


def norm_stats(values):
    center = values - jnp.mean(values, axis=-1, keepdims=True)
    rstd = lax.rsqrt(jnp.mean(center * center, axis=-1, keepdims=True) + EPS)
    return center * rstd, rstd


def norm_pull(grad, hat, rstd, gain):
    gn = grad * gain
    return rstd * (
        gn
        - jnp.mean(gn, axis=-1, keepdims=True)
        - hat * jnp.mean(gn * hat, axis=-1, keepdims=True)
    )


def enter_kernel(
    columns, shard, hid, cot, ids, qv, ub, wq, wo, gain, shift,
    own, full, cot_own, ids_o, qv_o, ub_o, wq_o, wo_o, send_sems, recv_sems, local_sems,
):
    place, link = Place(columns), Link(send_sems, recv_sems)
    n = shard // CHUNKS
    home, away = place.home, place.away
    meet([place.core, place.near, place.far, place.swap] + [place.column(m) for m in range(1, columns)])
    weights = [Spread(link, place, wq, wq_o), Spread(link, place, wo, wo_o)]

    ids_copy = link.send(ids, ids_o, place.swap, away)
    swaps = [
        link.send(rows_of(hid, i * n, n), rows_of(own, i * n, n), place.swap, away) for i in range(CHUNKS)
    ]
    for weight in weights:
        weight.open()
    qv_copy = link.send(qv, qv_o, place.far, home)
    ub_copy = link.send(ub, ub_o, place.far, home)
    local = Local(local_sems, home)
    held = [local.keep(rows_of(hid, i * n, n), rows_of(own, i * n, n)) for i in range(CHUNKS)]
    local.keep(cot, cot_own)
    local.keep(wq, wq_o)
    local.keep(wo, wo_o)
    local.keep(ids, ids_o)
    local.keep(qv, qv_o)
    local.keep(ub, ub_o)

    near, core = {}, []
    for i in range(CHUNKS):
        pl.when(home)(held[i].wait)
        arrive(swaps[i], away)

        def rows(here):
            hat = norm_stats(own[here, :].astype(F32))[0]
            full[here, :] = (hat * row_of(gain) + row_of(shift)).astype(BF)

        over_rows(i * n, n, STEP, rows)
        near[i], copy = gather_start(link, place, full, shard, i)
        core.append(copy)
    cot_copy = link.send(cot, cot_own, place.swap, away)
    for i in range(CHUNKS):
        core.append(gather_relay(link, place, full, shard, i, near[i]))
    for weight in weights:
        weight.share()
    for copy in core:
        copy.wait_recv()
    for weight in weights:
        weight.drain()
    for copy in (ids_copy, qv_copy, ub_copy, cot_copy):
        arrive(copy, away)
    local.drain(CHUNKS)
    link.close()


def mid_kernel(
    columns, shard, att, wo, own, bias, gain, shift, wu, wd, pieces, cot_own, cot_near,
    mid, full, cfull, wu_o, wd_o,
    part, core_buf, out_buf, near_buf, send_sems, recv_sems, local_sems
):
    place, link = Place(columns), Link(send_sems, recv_sems)
    n = shard // CHUNKS
    home, away = place.home, place.away
    unit, rest = pieces_of(wu, columns)
    at = pl.multiple_of(lax.div(place.d, 2) * unit, 16)
    mine = Local(local_sems, home, 0)
    mine.keep(wu, wu_o)
    mine.keep(wd, wd_o)
    both = Local(local_sems, None, 2)
    both.keep(cot_own, rows_of(cfull, 0, shard))
    both.keep(cot_near, rows_of(cfull, shard, shard))
    other = Local(local_sems, away, 4)
    for j, out in enumerate((wu_o, wd_o)):
        if unit:
            other.keep(rows_of(pieces, j * unit, unit), rows_of(out, at, unit))
        if rest:
            last = rows_of(pieces, 2 * unit + j * rest, rest)
            other.keep(last, rows_of(out, unit * columns, rest))
    meet([place.core, place.near, place.far] + [place.column(m) for m in range(1, columns)])
    shared = []
    if unit:
        for j, out in enumerate((wu_o, wd_o)):
            for m in range(1, columns):
                src = rows_of(pieces, j * unit, unit)
                shared.append(link.send(src, rows_of(out, at, unit), place.column(m), away))

    def make(rows):
        return mm(att[rows, :], wo[...])

    total = Scatter(link, place, make, part, core_buf, out_buf, near_buf, shard)
    total.start()
    for i in range(CHUNKS):
        total.pass_on(i)
    total.rest()
    core = [
        link.send(cot_own, rows_of(cfull, 2 * shard, shard), place.core),
        link.send(cot_near, rows_of(cfull, 3 * shard, shard), place.core),
    ]
    near = {}
    for i in range(CHUNKS):
        total.ready(i)

        def rows(here):
            value = own[here, :].astype(F32) + total.rows(here) + row_of(bias)
            mid[here, :] = value
            full[here, :] = (norm_stats(value)[0] * row_of(gain) + row_of(shift)).astype(BF)

        over_rows(i * n, n, STEP, rows)
        near[i], copy = gather_start(link, place, full, shard, i)
        core.append(copy)
    for i in range(CHUNKS):
        core.append(gather_relay(link, place, full, shard, i, near[i]))
    for copy in core:
        copy.wait_recv()
    for copy in shared:
        arrive(copy, away)
    for local in (mine, both, other):
        local.drain()
    link.close()


def pieces_of(weight, columns):
    rows = weight.shape[0]
    unit = rows // (16 * columns) * 16
    return unit, rows - unit * columns


def back_kernel(
    columns, shard, gi, wu, act, wd, raw_u, raw_d, mid, cot_full, gain, bias, *refs
):
    place, link = Place(columns), Link(*refs[-3:-1])
    bits = place.bits
    gmid, full, res, res_near, slices, sums = refs[:6]
    scratch = list(refs[6:-3])
    a_bufs, b_bufs = scratch[:4], scratch[4:6]
    cot, grads_u, grads_d = scratch[6:9]
    halves = scratch[9:]
    n = shard // CHUNKS
    local = Local(refs[-1])
    pack(local, [raw_u], grads_u)
    pack(local, [raw_d], grads_d)
    local.keep(rows_of(cot_full, 0, shard), cot)
    meet([place.core, place.near] + [place.column(1 << b) for b in range(bits)])

    def make(rows):
        return mm_nt(gi[rows, :], wu[...])

    def make2(rows):
        return mm(act[rows, :], wd[...])

    total = Scatter(link, place, make, *a_bufs, shard)
    total2 = Scatter(link, place, make2, *b_bufs, None, None, shard)
    size = grads_u.shape[0]
    slice_u, slice_d = (rows_of(slices, j * (size // columns), size // columns) for j in range(2))
    half_u = Halving(
        link, place, grads_u, 0, size, 0, halves[: bits - 1] + [slice_u], halves[bits - 1 : 2 * bits - 1]
    )
    halves = halves[2 * bits - 1 :]
    half_d = Halving(
        link, place, grads_d, 0, size, 1, halves[: bits - 1] + [slice_d], halves[bits - 1 : 2 * bits - 1]
    )
    local.drain()
    half_u.start(0)
    half_d.start(0)
    total.start()
    for i in range(CHUNKS):
        total.pass_on(i)
    total.rest()
    total2.start()
    total2.rest()
    for copy in total2.core.values():
        copy.wait_recv()

    def rows2(here):
        res[here, :] = mid[here, :] + total2.pair(here) + row_of(bias)

    def rows3(here):
        there = pl.ds(pl.multiple_of(here.start - shard, STEP), STEP)
        res_near[there, :] = total2.pair(here).astype(BF)

    over_rows(0, shard, STEP, rows2)
    over_rows(shard, shard, STEP, rows3)
    sums[...] = jnp.zeros_like(sums)
    near, core = {}, []
    for i in range(CHUNKS):
        total.ready(i)

        def rows(here):
            grad = total.rows(here)
            out_grad = cot[here, :].astype(F32)
            hat, rstd = norm_stats(mid[here, :])
            value = out_grad + norm_pull(grad, hat, rstd, row_of(gain))
            gmid[here, :] = value
            full[here, :] = value.astype(BF)
            for row, term in enumerate((value, grad * hat, grad, out_grad)):
                sums[row : row + 1, :] += jnp.sum(term, axis=0, keepdims=True)

        over_rows(i * n, n, STEP, rows)
        near[i], copy = gather_start(link, place, full, shard, i)
        core.append(copy)
    half_u.finish(0)
    half_d.finish(0)
    if bits > 1:
        half_u.start(1)
        half_d.start(1)
    for i in range(CHUNKS):
        core.append(gather_relay(link, place, full, shard, i, near[i]))
    for s in range(1, bits):
        half_u.finish(s)
        if s + 1 < bits:
            half_u.start(s + 1)
        half_d.finish(s)
        if s + 1 < bits:
            half_d.start(s + 1)
    for copy in core:
        copy.wait_recv()
    link.close()


def exit_kernel(
    columns, shard, dq, dk, dv, wq, own, gmid, slices, far, res, res_near, gq, gk, gv, go, small_in, gain, *refs
):
    place, link = Place(columns), Link(*refs[-3:-1])
    bits = place.bits
    inp, out, full_u, full_d, full_a, small = refs[:6]
    scratch = list(refs[6:-3])
    a_bufs = scratch[:4]
    swap_buf, out_buf, far_a0, far_a1, grads_a = scratch[4:9]
    steps = bits + 3
    sum_own, sum_got = scratch[9 : 9 + steps], scratch[9 + steps : 9 + 2 * steps]
    halves = scratch[9 + 2 * steps :]
    n = shard // CHUNKS
    local = Local(refs[-1])
    pack(local, [gq, gk, gv, go], grads_a)
    hops = [place.core] + [place.column(1 << b) for b in range(bits)] + [place.near, place.far]
    meet(hops + [place.swap])
    size = full_u.shape[0]

    def make(rows):
        return mm(dq[rows, :], wq[0]) + mm(dk[rows, :], wq[1]) + mm(dv[rows, :], wq[2])

    total = Scatter(link, place, make, *a_bufs, shard)
    half_a = []
    for side in range(2):
        half_a.append(
            Halving(
                link, place, grads_a, side * (size // 2), size // 2, side,
                halves[:bits], halves[bits : 2 * bits],
            )
        )
        halves = halves[2 * bits :]
    half_u = Halving(link, place, None, 0, size, 0, [], [])
    half_d = Halving(link, place, None, 0, size, 1, [], [])
    held = size // columns
    double = [
        Doubling(link, place, half_u, full_u, rows_of(slices, 0, held), rows_of(far, 0, held)),
        Doubling(link, place, half_d, full_d, rows_of(slices, held, held), rows_of(far, held, held)),
        Doubling(link, place, half_a[0], full_a, half_a[0].work[bits - 1], far_a0),
        Doubling(link, place, half_a[1], full_a, half_a[1].work[bits - 1], far_a1),
    ]
    local.drain()
    half_a[0].start(0)
    half_a[1].start(0)
    total.start()
    for i in range(CHUNKS):
        total.pass_on(i)
    total.rest()

    def finish_out(here):
        value = (res[here, :] + res_near[here, :].astype(F32)).astype(BF)
        out_buf[here, :] = value

        @pl.when(place.home)
        def _():
            out[here, :] = value

    over_rows(0, shard, STEP, finish_out)
    swaps = [link.send(out_buf, out, place.swap, place.away)]
    sum_own[0][...] = small_in[...]
    for s in range(bits):
        for half in half_a:
            half.finish(s)
            if s + 1 < bits:
                half.start(s + 1)
    double[2].start()
    double[3].start()
    double[0].join()
    double[1].join()
    for i in range(CHUNKS):
        total.ready(i)

        def rows(here):
            grad = total.rows(here)
            hat, rstd = norm_stats(own[here, :].astype(F32))
            value = (gmid[here, :] + norm_pull(grad, hat, rstd, row_of(gain))).astype(BF)
            swap_buf[here, :] = value
            for row, term in enumerate((grad * hat, grad)):
                sum_own[0][row : row + 1, :] += jnp.sum(term, axis=0, keepdims=True)

            @pl.when(place.home)
            def _():
                inp[here, :] = value

        over_rows(i * n, n, STEP, rows)
        swaps.append(
            link.send(rows_of(swap_buf, i * n, n), rows_of(inp, i * n, n), place.swap, place.away)
        )
    hop_copies = [link.send(sum_own[0], sum_got[0], hops[0])]

    def next_hop(s):
        hop_copies[s].wait_recv()
        into = small if s + 1 == steps else sum_own[s + 1]
        into[...] = sum_own[s][...] + sum_got[s][...]
        if s + 1 < steps:
            hop_copies.append(link.send(sum_own[s + 1], sum_got[s + 1], hops[s + 1]))

    hop = 0
    for s in range(bits):
        double[0].advance()
        double[1].advance()
        if s == 0:
            double[2].join()
            double[3].join()
        else:
            double[2].advance()
            double[3].advance()
        if hop < steps:
            next_hop(hop)
            hop += 1
    double[2].advance()
    double[3].advance()
    while hop < steps:
        next_hop(hop)
        hop += 1
    for one in double:
        for copy in one.cores:
            arrive(copy, place.away)
    for copy in swaps:
        arrive(copy, place.away)
    link.close()


def any_space():
    return pl.BlockSpec(memory_space=pl.ANY)


SEMS = 160


def sems(local=8):
    return [
        pltpu.SemaphoreType.DMA((SEMS,)),
        pltpu.SemaphoreType.DMA((SEMS,)),
        pltpu.SemaphoreType.DMA((local,)),
    ]


def remote_call(name, kernel, number, outs, in_specs, scratch):
    return pl.pallas_call(
        kernel,
        out_shape=outs,
        in_specs=in_specs,
        out_specs=jax.tree.map(lambda _: vmem(), outs),
        scratch_shapes=scratch + sems(),
        compiler_params=pltpu.CompilerParams(
            collective_id=number, has_side_effects=True, vmem_limit_bytes=62 << 20
        ),
        name=name,
    )


def shaped(shape, dtype):
    return jax.ShapeDtypeStruct(shape, dtype)


def like(x):
    return shaped(x.shape, x.dtype)


def enter(columns, hid, cot, ids, qv, ub, wq, wo, *vecs):
    shard, model = hid.shape
    outs = (like(hid), shaped((4 * shard, model), BF), like(cot), like(ids), like(qv), like(ub), like(wq), like(wo))
    call = remote_call(
        "enter", functools.partial(enter_kernel, columns, shard), 0, outs, [any_space()] * 7 + [vmem()] * 2, []
    )
    return call(hid, cot, ids, qv, ub, wq, wo, *vecs)


def make_mid(columns, att, wo, own, vecs, wu, wd, pieces, cot_own, cot_near):
    shard, model = own.shape
    whole = shaped((4 * shard, model), BF)
    outs = (shaped((shard, model), F32), whole, whole, like(wu), like(wd))
    call = remote_call(
        "mid", functools.partial(mid_kernel, columns, shard), 1, outs, [vmem()] * 6 + [any_space()] * 5,
        scatter_scratch(shard, model),
    )
    return call(att, wo, own, *vecs, wu, wd, pieces, cot_own, cot_near)


def make_back(columns, size, gi, wu, act, wd, grads_u, grads_d, mid, cot, *vecs):
    shard, model = mid.shape
    bits = columns.bit_length() - 1
    outs = (
        shaped((shard, model), F32),
        shaped((4 * shard, model), BF),
        shaped((shard, model), F32),
        shaped((shard, model), BF),
        shaped((2 * (size // columns), model), BF),
        shaped((8, model), F32),
    )
    per_side = halving_scratch(size, bits, model)
    halves = per_side[: bits - 1] + per_side
    call = remote_call(
        "back", functools.partial(back_kernel, columns, shard), 2, outs,
        [vmem()] * 4 + [any_space()] * 2 + [vmem(), any_space(), vmem(), vmem()],
        scatter_scratch(shard, model)
        + scatter_scratch(shard, model)[:2]
        + [pltpu.VMEM((shard, model), BF)]
        + [pltpu.VMEM((size, model), BF)] * 2
        + halves
        + halves,
    )
    return call(gi, wu, act, wd, grads_u, grads_d, mid, cot, *vecs)


def make_exit(columns, size, dq, dk, dv, wq, own, gmid, slices, far, res, res_near, grads, small, vec):
    shard, model = own.shape
    bits = columns.bit_length() - 1
    outs = (
        shaped((shard, model), BF),
        shaped((shard, model), BF),
        shaped((size, model), BF),
        shaped((size, model), BF),
        shaped((size, model), BF),
        shaped(small.shape, F32),
    )
    n = size // columns
    per_side = halving_scratch(size // 2, bits, model)
    steps = bits + 3
    call = remote_call(
        "exit", functools.partial(exit_kernel, columns, shard), 3, outs,
        [vmem()] * 10 + [any_space()] * 4 + [vmem()] * 2,
        scatter_scratch(shard, model)
        + [
            pltpu.VMEM((shard, model), BF),
            pltpu.VMEM((shard, model), BF),
            pltpu.VMEM((n // 2, model), BF),
            pltpu.VMEM((n // 2, model), BF),
            pltpu.VMEM((size, model), BF),
        ]
        + [pltpu.VMEM(small.shape, F32)] * (2 * steps)
        + (per_side + per_side) * 2,
    )
    return call(dq, dk, dv, wq, own, gmid, slices, far, res, res_near, *grads, small, vec)


def body(
    hidden,
    segment_ids,
    lengths,
    norm1_gain,
    norm1_shift,
    qkv_weight,
    qv_bias,
    out_weight,
    out_bias,
    norm2_gain,
    norm2_shift,
    up_weight,
    up_bias,
    down_weight,
    down_bias,
    cotangent,
):
    _, shard, model = hidden.shape
    seq = segment_ids.shape[1]
    width = qkv_weight.shape[2]
    d, t = lax.axis_index("dp"), lax.axis_index("tensor")
    columns = lax.axis_size("dp") // 2
    rank = 2 * (d & 1) + (t & 1)

    places = jnp.arange(seq, dtype=jnp.int32)
    ids = jnp.where(places < lengths[0], segment_ids[0], 16 + places)
    start = jnp.sum((ids[None, :] < ids[:, None]).astype(jnp.int32), axis=1)
    blocks = seq // BLK
    start = jnp.concatenate([start, start[::BLK] // BLK, jnp.zeros((LANES - blocks,), jnp.int32)])
    start = start[None]

    own, normed1, cot_own, start, b_qv, b_up, w_qkv, w_out = enter(
        columns, hidden[0], cotangent[0], start, qv_bias, up_bias, jnp.swapaxes(qkv_weight, 1, 2), out_weight,
        norm1_gain, norm1_shift,
    )
    everywhere = [(i, j) for i in range(2 * columns) for j in range(4)]
    to_near = [(4 * i + j, 4 * i + (j ^ 1)) for i, j in everywhere]
    to_away = [(4 * i + j, 4 * i + (j ^ 2)) for i, j in everywhere if i % 2 == j // 2]
    to_home = [(4 * i + j, 4 * i + (j ^ 2)) for i, j in everywhere if i % 2 != j // 2]
    axes = ("dp", "tensor")
    unit, rest = pieces_of(up_weight, columns)
    pieces = [lax.dynamic_slice_in_dim(w, (d // 2) * unit, unit, 0) for w in (up_weight, down_weight)]
    pieces += [w[unit * columns :] for w in (up_weight, down_weight)]
    cot_own, pieces, normed1 = lax.optimization_barrier((cot_own, jnp.concatenate(pieces), normed1))
    cot_near = lax.ppermute(cot_own, axes, to_near)
    pieces = lax.ppermute(pieces, axes, to_away)

    meta = jnp.concatenate([rank[None].astype(jnp.int32), start[0, seq : seq + blocks]])

    attended, lse, q, k, v = attn_fwd(meta, start, normed1, w_qkv, b_qv, shard)

    mid, normed2, cot_full, w_up, w_down = make_mid(
        columns,
        attended,
        w_out,
        own,
        (out_bias, norm2_gain, norm2_shift),
        up_weight,
        down_weight,
        pieces,
        cot_own,
        cot_near,
    )
    inner = mm(normed2, w_up) + b_up
    c0 = math.sqrt(2.0 / math.pi)
    tanh = jnp.tanh(c0 * (inner + 0.044715 * inner * inner * inner))
    active = (0.5 * inner * (1.0 + tanh)).astype(BF)
    slope = 0.5 * (1.0 + tanh) + 0.5 * inner * (1.0 - tanh * tanh) * c0 * (
        1.0 + 3 * 0.044715 * inner * inner
    )
    grad_inner = (mm_nt(cot_full, w_down) * slope).astype(BF)
    unit = 32 * columns
    size = -(-model // unit) * unit
    grad_mid, gm_full, res, res_near, slices, sums = make_back(
        columns,
        size,
        grad_inner,
        w_up,
        active,
        w_down,
        mm_tn(normed2, grad_inner).astype(BF),
        mm_tn(active, cot_full).astype(BF),
        mid,
        cot_full,
        norm2_gain,
        down_bias,
    )
    far = lax.ppermute(slices, axes, to_home)
    res_near = lax.ppermute(res_near, axes, to_near)
    dq, dk, dv = attn_bwd(meta, start, q, k, v, attended, gm_full, w_out, lse, shard)
    far, dk, dv = lax.optimization_barrier((far, dk, dv))
    res_near, dq = lax.optimization_barrier((res_near, dq))
    att_grads = [
        mm_tn(dq, normed1).astype(BF),
        mm_tn(dk, normed1).astype(BF),
        mm_tn(dv, normed1).astype(BF),
        mm_tn(attended, gm_full).astype(BF),
    ]

    qv_grad = jnp.concatenate([jnp.sum(dq, axis=0, dtype=F32), jnp.sum(dv, axis=0, dtype=F32)])
    qv_grad = jnp.pad(qv_grad, (0, model - 2 * width))
    up_b_grad = jnp.sum(grad_inner, axis=0, dtype=F32)
    slots = lax.broadcasted_iota(jnp.int32, (4, 1), 0) == rank
    small = jnp.concatenate(
        [
            jnp.zeros((2, model), F32),
            sums[:4],
            jnp.zeros((2, model), F32),
            jnp.where(slots, up_b_grad[None], 0.0),
            jnp.where(slots, qv_grad[None], 0.0),
        ]
    )
    input_grad, output, up_grad, down_grad, att_grad, small = make_exit(
        columns,
        size,
        dq,
        dk,
        dv,
        w_qkv,
        own,
        grad_mid,
        slices,
        far,
        res,
        res_near,
        att_grads,
        small,
        norm1_gain,
    )
    quarter = lax.dynamic_slice_in_dim(small, 12 + t, 1, 0)[0, : 2 * width].reshape(2, width)
    att_grad = att_grad.reshape(4, size // 4, model)
    qkv_grad = att_grad[:3, :width].astype(F32)
    return (
        output[None],
        input_grad[None],
        small[0],
        small[1],
        jnp.swapaxes(qkv_grad, 1, 2),
        quarter,
        att_grad[3, :width].astype(F32),
        small[2],
        small[3],
        small[4],
        up_grad[:model].astype(F32),
        lax.dynamic_slice_in_dim(small, 8 + t, 1, 0)[0],
        down_grad[:model].astype(F32),
        small[5],
    )


def solution(mesh):
    in_specs = (
        P("dp", "tensor", None),
        P("dp", None),
        P("dp"),
        P(),
        P(),
        P(None, None, "tensor"),
        P(None, "tensor"),
        P("tensor", None),
        P(),
        P(),
        P(),
        P(None, "tensor"),
        P("tensor"),
        P("tensor", None),
        P(),
        P("dp", "tensor", None),
    )
    out_specs = (
        P("dp", "tensor", None),
        P("dp", "tensor", None),
        P(),
        P(),
        P(None, None, "tensor"),
        P(None, "tensor"),
        P("tensor", None),
        P(),
        P(),
        P(),
        P(None, "tensor"),
        P("tensor"),
        P("tensor", None),
        P(),
    )
    return jax.shard_map(body, mesh=mesh, in_specs=in_specs, out_specs=out_specs, check_vma=False)
```

```python
import functools
import math

import jax
import jax.numpy as jnp
from jax import lax
from jax.experimental import pallas as pl
from jax.experimental.pallas import tpu as pltpu
from jax.sharding import PartitionSpec as P

HEAD = 56
EPS = 1e-05
LANES = 128
BLK = 256
BF = jnp.bfloat16
F32 = jnp.float32


def mm(a, b):
    return jnp.dot(a, b, preferred_element_type=F32)


def mm_nt(a, b):
    return lax.dot_general(a, b, (((1,), (1,)), ((), ())), preferred_element_type=F32)


def mm_tn(a, b):
    return lax.dot_general(a, b, (((0,), (0,)), ((), ())), preferred_element_type=F32)


def head_window(h):
    lo, hi = h * HEAD, (h + 1) * HEAD
    first = lo // LANES * LANES
    last = -(-hi // LANES) * LANES
    return first, last


def head_mask(h, rows):
    first, last = head_window(h)
    lane = lax.broadcasted_iota(jnp.int32, (rows, last - first), 1) + first
    return (lane >= h * HEAD) & (lane < (h + 1) * HEAD)


def stage_in(rank, src, dst, shard, width):
    wide = dst.shape[1]
    for s in range(src.shape[0] // shard):
        rel = pl.multiple_of((rank ^ s) * shard, 16)
        dst[s * shard : (s + 1) * shard, :width] = src[pl.ds(rel, shard), :]
    if wide > width:
        dst[:, width:] = jnp.zeros((dst.shape[0], wide - width), dst.dtype)


def project(rank, src, shard, width, products):
    @pl.loop(0, src.shape[0] // shard)
    def _(s):
        rel = pl.multiple_of((rank ^ s) * shard, 16)
        rows = pl.ds(pl.multiple_of(s * shard, 16), shard)
        x = src[pl.ds(rel, shard), :]
        for dst, weight, bias in products:
            value = dot_nt(x, weight[...])
            if bias is not None:
                value = value + bias
            dst[rows, :width] = value.astype(BF)

    for dst, _, _ in products:
        if dst.shape[1] > width:
            dst[:, width:] = jnp.zeros((dst.shape[0], dst.shape[1] - width), BF)


def stage_out(rank, src, dst, shard, width):
    for s in range(dst.shape[0] // shard):
        rel = pl.multiple_of((rank ^ s) * shard, 16)
        dst[pl.ds(rel, shard), :] = src[s * shard : (s + 1) * shard, :width]


def tile_mask(start_row, qb, kb):
    kpos = kb * BLK + lax.broadcasted_iota(jnp.int32, (BLK, BLK), 0)
    qpos = qb * BLK + lax.broadcasted_iota(jnp.int32, (BLK, BLK), 1)
    return (kpos <= qpos) & (kpos >= start_row)


def dot_nt(a, b):
    return lax.dot_general(a, b, (((1,), (1,)), ((), ())), preferred_element_type=F32)


def attn_fwd_kernel(heads, shard, meta, start, normed, wq, bias, out, lse, qs, ks, vs, vt, os, ot, ms, ls, acc):
    seq, width = out.shape
    scale2 = HEAD ** (-0.5) * math.log2(math.e)
    rank = meta[0]
    b_q, b_v = bias[0:1, :], bias[1:2, :]
    project(
        rank, normed, shard, width, [(qs, wq.at[0], b_q), (ks, wq.at[1], None), (vs, wq.at[2], b_v)]
    )
    blocks = seq // BLK

    @pl.loop(0, blocks)
    def _(b):
        rows = pl.ds(pl.multiple_of(b * BLK, BLK), BLK)
        flipped = vs[rows, :].astype(F32).T
        for h in range(heads):
            vt[h, :, rows] = flipped[h * HEAD : (h + 1) * HEAD, :].astype(BF)

    lse[...] = jnp.zeros_like(lse)

    @pl.loop(0, blocks)
    def _(b):
        rows = pl.ds(pl.multiple_of(b * BLK, BLK), BLK)
        start_row = start[0:1, rows]
        ms[...] = jnp.full_like(ms, -1e30)
        ls[...] = jnp.zeros_like(ls)
        acc[...] = jnp.zeros_like(acc)

        def tile(kb, carry):
            krows = pl.ds(pl.multiple_of(kb * BLK, BLK), BLK)
            mask = tile_mask(start_row, b, kb)
            for h in range(heads):
                first, last = head_window(h)
                qm = jnp.where(head_mask(h, BLK), qs[rows, first:last], 0)
                s = dot_nt(ks[krows, first:last], qm) * scale2
                s = jnp.where(mask, s, -1e30)
                old = ms[h : h + 1, :]
                new = jnp.maximum(old, jnp.max(s, axis=0, keepdims=True))
                p = jnp.exp2(s - new)
                p = jnp.where(mask, p, 0.0)
                fade = jnp.exp2(old - new)
                ms[h : h + 1, :] = new
                ls[h : h + 1, :] = ls[h : h + 1, :] * fade + jnp.sum(p, axis=0, keepdims=True)
                acc[h] = acc[h] * fade + jnp.dot(
                    vt[h, :, krows], p.astype(BF), preferred_element_type=F32
                )
            return carry

        lax.fori_loop(meta[1 + b], b + 1, tile, 0)
        for h in range(heads):
            total = ls[h : h + 1, :]
            lse[h : h + 1, rows] = ms[h : h + 1, :] + jnp.log(total) * math.log2(math.e)
            ot[h * HEAD : (h + 1) * HEAD, :] = acc[h] / total
        os[rows, :] = ot[...].T.astype(BF)

    stage_out(rank, os, out, shard, width)


def attn_bwd_kernel(
    heads, shard, meta, start, qs, ks, vs, o, gm, wo, lse, dq, dk, dv,
    os, dos, kt, delta, dqs, dks, dvs, dqt, qm, dm,
):
    seq, width = o.shape
    scale = HEAD ** (-0.5)
    scale2 = scale * math.log2(math.e)
    rank = meta[0]
    blocks = seq // BLK
    stage_in(rank, o, os, shard, width)
    project(rank, gm, shard, width, [(dos, wo, None)])

    @pl.loop(0, blocks)
    def _(b):
        rows = pl.ds(pl.multiple_of(b * BLK, BLK), BLK)
        flipped = (os[rows, :].astype(F32) * dos[rows, :].astype(F32)).T
        for h in range(heads):
            delta[h : h + 1, rows] = jnp.sum(
                flipped[h * HEAD : (h + 1) * HEAD, :], axis=0, keepdims=True
            )

    @pl.loop(0, blocks)
    def _(b):
        rows = pl.ds(pl.multiple_of(b * BLK, BLK), BLK)
        flipped = ks[rows, :].astype(F32).T
        for h in range(heads):
            kt[h, :, rows] = flipped[h * HEAD : (h + 1) * HEAD, :].astype(BF)

    dks[...] = jnp.zeros_like(dks)
    dvs[...] = jnp.zeros_like(dvs)
    dqt[...] = jnp.zeros_like(dqt)

    @pl.loop(0, blocks)
    def _(b):
        rows = pl.ds(pl.multiple_of(b * BLK, BLK), BLK)
        start_row = start[0:1, rows]
        dqt[...] = jnp.zeros_like(dqt)
        for h in range(heads):
            first, last = head_window(h)
            keep = head_mask(h, BLK)
            qm[h, :, : last - first] = jnp.where(keep, qs[rows, first:last], 0)
            dm[h, :, : last - first] = jnp.where(keep, dos[rows, first:last], 0)

        def tile(kb, carry):
            krows = pl.ds(pl.multiple_of(kb * BLK, BLK), BLK)
            mask = tile_mask(start_row, b, kb)
            for h in range(heads):
                first, last = head_window(h)
                qh = qm[h, :, : last - first]
                dh = dm[h, :, : last - first]
                s = dot_nt(ks[krows, first:last], qh) * scale2
                p = jnp.where(mask, jnp.exp2(s - lse[h : h + 1, rows]), 0.0)
                dp = dot_nt(vs[krows, first:last], dh)
                ds = (p * (dp - delta[h : h + 1, rows])).astype(BF)
                dvs[krows, first:last] += jnp.dot(p.astype(BF), dh, preferred_element_type=F32)
                dks[krows, first:last] += jnp.dot(ds, qh, preferred_element_type=F32)
                dqt[h * HEAD : (h + 1) * HEAD, :] += jnp.dot(
                    kt[h, :, krows], ds, preferred_element_type=F32
                )
            return carry

        lax.fori_loop(meta[1 + b], b + 1, tile, 0)
        dqs[rows, :] = (dqt[...].T * scale).astype(BF)

    stage_out(rank, dqs, dq, shard, width)
    for s in range(seq // shard):
        rel = pl.multiple_of((rank ^ s) * shard, 16)
        here = slice(s * shard, (s + 1) * shard)
        dk[pl.ds(rel, shard), :] = (dks[here, :width] * scale).astype(BF)
        dv[pl.ds(rel, shard), :] = dvs[here, :width].astype(BF)


def vmem():
    return pl.BlockSpec(memory_space=pltpu.VMEM)


def smem():
    return pl.BlockSpec(memory_space=pltpu.SMEM)


def attn_cost(seq, width, products):
    return pl.CostEstimate(
        flops=products * seq * seq * width,
        bytes_accessed=8 * seq * width * 2,
        transcendentals=seq * seq * width // (2 * HEAD),
    )


def attn_fwd(meta, start, normed, wq, bias, shard):
    seq, (_, width, _) = normed.shape[0], wq.shape
    heads = width // HEAD
    wide = -(-width // LANES) * LANES
    staged = jax.ShapeDtypeStruct((seq, wide), BF)
    return pl.pallas_call(
        functools.partial(attn_fwd_kernel, heads, shard),
        out_shape=(
            jax.ShapeDtypeStruct((seq, width), BF),
            jax.ShapeDtypeStruct((8, seq), F32),
            staged,
            staged,
            staged,
        ),
        in_specs=[smem()] + [vmem()] * 4,
        out_specs=(vmem(),) * 5,
        scratch_shapes=[
            pltpu.VMEM((heads, HEAD, seq), BF),
            pltpu.VMEM((seq, wide), BF),
            pltpu.VMEM((wide, BLK), F32),
            pltpu.VMEM((8, BLK), F32),
            pltpu.VMEM((8, BLK), F32),
            pltpu.VMEM((heads, HEAD, BLK), F32),
        ],
        cost_estimate=attn_cost(seq, width, 3),
        name="attn_fwd",
    )(meta, start, normed, wq, bias)


def attn_bwd(meta, start, q, k, v, o, gm, wo, lse, shard):
    seq, width = o.shape
    heads = width // HEAD
    wide = q.shape[1]
    grad = jax.ShapeDtypeStruct((seq, width), BF)
    return pl.pallas_call(
        functools.partial(attn_bwd_kernel, heads, shard),
        out_shape=(grad, grad, grad),
        in_specs=[smem()] + [vmem()] * 8,
        out_specs=(vmem(), vmem(), vmem()),
        scratch_shapes=[
            pltpu.VMEM((seq, wide), BF),
            pltpu.VMEM((seq, wide), BF),
            pltpu.VMEM((heads, HEAD, seq), BF),
            pltpu.VMEM((8, seq), F32),
            pltpu.VMEM((seq, wide), BF),
            pltpu.VMEM((seq, wide), F32),
            pltpu.VMEM((seq, wide), F32),
            pltpu.VMEM((wide, BLK), F32),
            pltpu.VMEM((heads, BLK, 2 * LANES), BF),
            pltpu.VMEM((heads, BLK, 2 * LANES), BF),
        ],
        cost_estimate=attn_cost(seq, width, 8),
        name="attn_bwd",
    )(meta, start, q, k, v, o, gm, wo, lse)


MESH = pl.DeviceIdType.MESH
CHUNKS = 2
STEP = 32


class Place:
    def __init__(self, columns):
        d, t = lax.axis_index("dp"), lax.axis_index("tensor")
        core, low, high = lax.rem(d, 2), lax.rem(t, 2), lax.div(t, 2)
        self.d, self.t, self.columns = d, t, columns
        self.bits = columns.bit_length() - 1
        self.core = (d + 1 - 2 * core, t)
        self.near = (d, t + 1 - 2 * low)
        self.far = (d, t + 2 - 4 * high)
        self.swap = (d + 1 - 2 * core, t + 2 - 4 * high)
        self.home = core == high
        self.away = core != high

    def bit(self, b):
        return lax.rem(lax.div(self.d, 2 << b), 2)

    def column(self, m):
        d = self.d
        for b in range(self.bits):
            if (m >> b) & 1:
                d = d + (2 << b) * (1 - 2 * self.bit(b))
        return (d, self.t)


class Link:
    def __init__(self, send_sems, recv_sems):
        self.send_sems, self.recv_sems = send_sems, recv_sems
        self.count = 0
        self.open, self.kept, self.number = [], [], {}

    def make(self, src, dst, to, like=None):
        if like is None:
            i = self.count
            self.count += 1
        else:
            i = self.number[id(like)]
        copy = pltpu.make_async_remote_copy(
            src_ref=src,
            dst_ref=dst,
            send_sem=self.send_sems.at[i],
            recv_sem=self.recv_sems.at[i],
            device_id=to,
            device_id_type=MESH,
        )
        self.number[id(copy)] = i
        self.kept.append(copy)
        return copy

    def start(self, copy, when=None):
        if when is None:
            copy.start()
        else:
            pl.when(when)(copy.start)
        self.open.append((copy, when))

    def send(self, src, dst, to, when=None):
        copy = self.make(src, dst, to)
        self.start(copy, when)
        return copy

    def close(self):
        for copy, when in self.open:
            if when is None:
                copy.wait_send()
            else:
                pl.when(when)(copy.wait_send)


def arrive(copy, when=None):
    if when is None:
        copy.wait_recv()
    else:
        pl.when(when)(copy.wait_recv)


def meet(partners):
    barrier = pltpu.get_barrier_semaphore()
    for to in partners:
        pl.semaphore_signal(barrier, inc=1, device_id=to, device_id_type=MESH)
    pl.semaphore_wait(barrier, len(partners))


def row_of(ref):
    return ref[...][None, :]


def rows_of(ref, first, count):
    return ref.at[pl.ds(first, count)]


def gather_start(link, place, full, shard, i):
    n = shard // CHUNKS
    near = link.send(rows_of(full, i * n, n), rows_of(full, shard + i * n, n), place.near)
    core = link.send(rows_of(full, i * n, n), rows_of(full, 2 * shard + i * n, n), place.core)
    return near, core


def gather_relay(link, place, full, shard, i, near):
    n = shard // CHUNKS
    near.wait_recv()
    return link.send(
        rows_of(full, shard + i * n, n), rows_of(full, 3 * shard + i * n, n), place.core
    )


class Scatter:
    def __init__(self, link, place, make, part, core_buf, out_buf, near_buf, shard):
        self.link, self.place, self.make, self.part = link, place, make, part
        self.core_buf, self.out_buf, self.near_buf = core_buf, out_buf, near_buf
        self.shard, self.n = shard, shard // CHUNKS
        self.core, self.near = {}, {}

    def fill(self, block):
        rows = pl.ds(pl.multiple_of(block * self.shard, 16), self.shard)
        self.part[rows, :] = self.make(rows).astype(BF)

    def to_core(self, block):
        for i in range(CHUNKS):
            at = (block - 2) * self.shard + i * self.n
            self.core[block - 2, i] = self.link.send(
                rows_of(self.part, 2 * self.shard + at, self.n),
                rows_of(self.core_buf, at, self.n),
                self.place.core,
            )

    def start(self):
        self.fill(3)
        self.to_core(3)
        self.fill(1)

    def rest(self):
        @pl.loop(0, 2)
        def _(b):
            self.fill(2 - 2 * b)

        self.to_core(2)

    def pass_on(self, i):
        at = self.shard + i * self.n
        self.core[1, i].wait_recv()

        @pl.loop(0, self.n // STEP)
        def _(r):
            here = pl.multiple_of(at + r * STEP, STEP)
            there = pl.multiple_of(i * self.n + r * STEP, STEP)
            total = self.part[pl.ds(here, STEP), :].astype(F32) + self.core_buf[
                pl.ds(here, STEP), :
            ].astype(F32)
            self.out_buf[pl.ds(there, STEP), :] = total.astype(BF)

        self.near[i] = self.link.send(
            rows_of(self.out_buf, i * self.n, self.n),
            rows_of(self.near_buf, i * self.n, self.n),
            self.place.near,
        )

    def pair(self, rows):
        return self.part[rows, :].astype(F32) + self.core_buf[rows, :].astype(F32)

    def ready(self, i):
        self.core[0, i].wait_recv()
        self.near[i].wait_recv()

    def rows(self, rows):
        return (
            self.part[rows, :].astype(F32)
            + self.core_buf[rows, :].astype(F32)
            + self.near_buf[rows, :].astype(F32)
        )


class Spread:
    def __init__(self, link, place, src, dst):
        self.link, self.place, self.src, self.dst = link, place, src, dst
        rows = src.shape[-2]
        self.unit = rows // (16 * place.columns) * 16
        self.rest = rows - self.unit * place.columns
        self.at = pl.multiple_of(lax.div(place.d, 2) * self.unit, 16)
        self.pieces, self.shared = [], []

    def move(self, src, at, count, to, when):
        return self.link.send(rows_of(src, at, count), rows_of(self.dst, at, count), to, when)

    def open(self):
        far, home = self.place.far, self.place.home
        if self.unit:
            self.first = self.move(self.src, self.at, self.unit, far, home)
        if self.rest:
            at = self.unit * self.place.columns
            self.pieces.append(self.move(self.src, at, self.rest, far, home))

    def share(self):
        away = self.place.away
        if self.unit:
            arrive(self.first, away)
            for m in range(1, self.place.columns):
                to = self.place.column(m)
                self.pieces.append(self.move(self.dst, self.at, self.unit, to, away))

    def drain(self):
        for copy in self.pieces:
            arrive(copy, self.place.away)


class Local:
    def __init__(self, sems, when=None, base=0):
        self.sems, self.when, self.base, self.copies = sems, when, base, []

    def keep(self, src, dst):
        copy = pltpu.make_async_copy(src, dst, self.sems.at[self.base + len(self.copies)])
        self.copies.append(copy)
        self.run(copy.start)
        return copy

    def run(self, act):
        if self.when is None:
            act()
        else:
            pl.when(self.when)(act)

    def drain(self, first=0):
        for copy in self.copies[first:]:
            self.run(copy.wait)


def pack(local, sources, buf):
    block = buf.shape[0] // len(sources)
    for j, src in enumerate(sources):
        count = src.shape[0]
        local.keep(src, rows_of(buf, j * block, count))
        if count < block:
            buf[j * block + count : (j + 1) * block, :] = jnp.zeros((block - count, buf.shape[1]), buf.dtype)


def scatter_scratch(shard, model):
    return [
        pltpu.VMEM((4 * shard, model), BF),
        pltpu.VMEM((2 * shard, model), BF),
        pltpu.VMEM((shard, model), BF),
        pltpu.VMEM((shard, model), BF),
    ]


def over_rows(first, count, step, fn):
    @pl.loop(0, count // step)
    def _(r):
        fn(pl.ds(pl.multiple_of(first + r * step, 16), step))


class Halving:
    def __init__(self, link, place, source, first, size, turn, work, got):
        self.link, self.place = link, place
        self.source, self.first, self.size = source, first, size
        self.order = [(b + turn) % place.bits for b in range(place.bits)]
        self.work, self.got = work, got
        self.copies = []

    def start(self, s):
        n = self.size >> (s + 1)
        bit = self.place.bit(self.order[s])
        src, base = (self.source, self.first) if s == 0 else (self.work[s - 1], 0)
        at = pl.multiple_of(base + (1 - bit) * n, 16)
        self.copies.append(
            self.link.send(
                rows_of(src, at, n), self.got[s], self.place.column(1 << self.order[s])
            )
        )

    def finish(self, s):
        n = self.size >> (s + 1)
        bit = self.place.bit(self.order[s])
        src, base = (self.source, self.first) if s == 0 else (self.work[s - 1], 0)
        self.copies[s].wait_recv()

        step = step_of(n)

        @pl.loop(0, n // step)
        def _(r):
            here = pl.multiple_of(base + bit * n + r * step, 16)
            to = pl.ds(pl.multiple_of(r * step, 16), step)
            total = src[pl.ds(here, step), :].astype(F32) + self.got[s][to, :].astype(F32)
            self.work[s][to, :] = total.astype(BF)

    def offset(self):
        at, n = 0, self.size
        for b in self.order:
            n //= 2
            at = at + self.place.bit(b) * n
        return self.first + at


def step_of(n):
    return next(step for step in (48, 32, 16) if n % step == 0)


def groups_of(side, unit):
    units = side // unit
    first = max(1, min(units - 1, 2 * units // 3))
    return [count * unit for count in (first, units - first) if count]


def halving_scratch(size, bits, model):
    return [pltpu.VMEM((size >> (s + 1), model), BF) for s in range(bits)]


class Doubling:
    def __init__(self, link, place, half, full, slice_ref, far_buf):
        self.link, self.place, self.half, self.full = link, place, half, full
        self.far = None
        self.slice_ref, self.far_buf = slice_ref, far_buf
        self.n = half.size >> place.bits
        self.at = half.offset()
        self.cores, self.waits = [], []

    def start(self):
        self.far = self.link.send(
            self.slice_ref, self.far_buf, self.place.far, self.place.away
        )

    def to_core(self, at, n):
        self.link.send(
            rows_of(self.full, at, n), rows_of(self.full, at, n), self.place.core, self.place.home
        )

    def join(self):
        if self.far is not None:
            arrive(self.far, self.place.home)

        @pl.when(self.place.home)
        def _():
            step = step_of(self.n)

            @pl.loop(0, self.n // step)
            def _(r):
                here = pl.ds(pl.multiple_of(r * step, 16), step)
                to = pl.ds(pl.multiple_of(self.at + r * step, 16), step)
                total = self.slice_ref[here, :].astype(F32) + self.far_buf[here, :].astype(F32)
                self.full[to, :] = total.astype(BF)

        self.block, self.count = pl.multiple_of(self.at, 16), self.n
        self.stage = 0
        self.push(self.block)

    def push(self, fresh):
        if self.stage < self.place.bits:
            b = self.half.order[self.place.bits - 1 - self.stage]
            self.copy = self.link.send(
                rows_of(self.full, self.block, self.count),
                rows_of(self.full, self.block, self.count),
                self.place.column(1 << b),
                self.place.home,
            )
        copy = self.link.send(
            rows_of(self.full, fresh, self.count if self.stage == 0 else self.count // 2),
            rows_of(self.full, fresh, self.count if self.stage == 0 else self.count // 2),
            self.place.core,
            self.place.home,
        )
        self.cores.append(copy)

    def advance(self):
        b = self.half.order[self.place.bits - 1 - self.stage]
        bit = self.place.bit(b)
        fresh = pl.multiple_of(self.block + (1 - 2 * bit) * self.count, 16)
        arrive(self.copy, self.place.home)
        self.block = pl.multiple_of(self.block - bit * self.count, 16)
        self.count *= 2
        self.stage += 1
        self.push(fresh)


def norm_stats(values):
    center = values - jnp.mean(values, axis=-1, keepdims=True)
    rstd = lax.rsqrt(jnp.mean(center * center, axis=-1, keepdims=True) + EPS)
    return center * rstd, rstd


def norm_pull(grad, hat, rstd, gain):
    gn = grad * gain
    return rstd * (
        gn
        - jnp.mean(gn, axis=-1, keepdims=True)
        - hat * jnp.mean(gn * hat, axis=-1, keepdims=True)
    )


def enter_kernel(
    columns, shard, hid, cot, ids, qv, ub, wq, wo, gain, shift,
    own, full, cot_own, ids_o, qv_o, ub_o, wq_o, wo_o, send_sems, recv_sems, local_sems,
):
    place, link = Place(columns), Link(send_sems, recv_sems)
    n = shard // CHUNKS
    home, away = place.home, place.away
    meet([place.core, place.near, place.far, place.swap] + [place.column(m) for m in range(1, columns)])
    weights = [Spread(link, place, wq.at[j], wq_o.at[j]) for j in range(wq.shape[0])]
    weights.append(Spread(link, place, wo, wo_o))

    ids_copy = link.send(ids, ids_o, place.swap, away)
    swaps = [
        link.send(rows_of(hid, i * n, n), rows_of(own, i * n, n), place.swap, away) for i in range(CHUNKS)
    ]
    for weight in weights:
        weight.open()
    qv_copy = link.send(qv, qv_o, place.far, home)
    ub_copy = link.send(ub, ub_o, place.far, home)
    local = Local(local_sems, home)
    held = [local.keep(rows_of(hid, i * n, n), rows_of(own, i * n, n)) for i in range(CHUNKS)]
    local.keep(cot, cot_own)
    local.keep(wq, wq_o)
    local.keep(wo, wo_o)
    local.keep(ids, ids_o)
    local.keep(qv, qv_o)
    local.keep(ub, ub_o)

    near, core = {}, []
    for i in range(CHUNKS):
        pl.when(home)(held[i].wait)
        arrive(swaps[i], away)

        def rows(here):
            hat = norm_stats(own[here, :].astype(F32))[0]
            full[here, :] = (hat * row_of(gain) + row_of(shift)).astype(BF)

        over_rows(i * n, n, STEP, rows)
        near[i], copy = gather_start(link, place, full, shard, i)
        core.append(copy)
    cot_copy = link.send(cot, cot_own, place.swap, away)
    for i in range(CHUNKS):
        core.append(gather_relay(link, place, full, shard, i, near[i]))
    for weight in weights:
        weight.share()
    for copy in core:
        copy.wait_recv()
    for weight in weights:
        weight.drain()
    for copy in (ids_copy, qv_copy, ub_copy, cot_copy):
        arrive(copy, away)
    local.drain(CHUNKS)
    link.close()


def mid_kernel(
    columns, shard, att, wo, own, bias, gain, shift, wu, wd, pieces, cot_own, cot_near,
    mid, full, cfull, wu_o, wd_o,
    part, core_buf, out_buf, near_buf, send_sems, recv_sems, local_sems
):
    place, link = Place(columns), Link(send_sems, recv_sems)
    n = shard // CHUNKS
    home, away = place.home, place.away
    unit, rest = pieces_of(wu, columns)
    at = pl.multiple_of(lax.div(place.d, 2) * unit, 16)
    mine = Local(local_sems, home, 0)
    mine.keep(wu, wu_o)
    mine.keep(wd, wd_o)
    both = Local(local_sems, None, 2)
    both.keep(cot_own, rows_of(cfull, 0, shard))
    both.keep(cot_near, rows_of(cfull, shard, shard))
    other = Local(local_sems, away, 4)
    for j, out in enumerate((wu_o, wd_o)):
        if unit:
            other.keep(rows_of(pieces, j * unit, unit), rows_of(out, at, unit))
        if rest:
            last = rows_of(pieces, 2 * unit + j * rest, rest)
            other.keep(last, rows_of(out, unit * columns, rest))
    meet([place.core, place.near, place.far] + [place.column(m) for m in range(1, columns)])
    shared = []
    if unit:
        for j, out in enumerate((wu_o, wd_o)):
            for m in range(1, columns):
                src = rows_of(pieces, j * unit, unit)
                shared.append(link.send(src, rows_of(out, at, unit), place.column(m), away))

    def make(rows):
        return mm(att[rows, :], wo[...])

    total = Scatter(link, place, make, part, core_buf, out_buf, near_buf, shard)
    total.start()
    for i in range(CHUNKS):
        total.pass_on(i)
    total.rest()
    core = [
        link.send(cot_own, rows_of(cfull, 2 * shard, shard), place.core),
        link.send(cot_near, rows_of(cfull, 3 * shard, shard), place.core),
    ]
    near = {}
    for i in range(CHUNKS):
        total.ready(i)

        def rows(here):
            value = own[here, :].astype(F32) + total.rows(here) + row_of(bias)
            mid[here, :] = value
            full[here, :] = (norm_stats(value)[0] * row_of(gain) + row_of(shift)).astype(BF)

        over_rows(i * n, n, STEP, rows)
        near[i], copy = gather_start(link, place, full, shard, i)
        core.append(copy)
    for i in range(CHUNKS):
        core.append(gather_relay(link, place, full, shard, i, near[i]))
    for copy in core:
        copy.wait_recv()
    for copy in shared:
        arrive(copy, away)
    for local in (mine, both, other):
        local.drain()
    link.close()


def pieces_of(weight, columns):
    rows = weight.shape[0]
    unit = rows // (16 * columns) * 16
    return unit, rows - unit * columns


def back_kernel(
    columns, shard, gi, wu, act, wd, raw_u, raw_d, mid, cot_full, gain, bias, *refs
):
    place, link = Place(columns), Link(*refs[-3:-1])
    bits = place.bits
    gmid, full, res, res_near, slices, sums = refs[:6]
    scratch = list(refs[6:-3])
    a_bufs, b_bufs = scratch[:4], scratch[4:6]
    cot, grads_u, grads_d = scratch[6:9]
    halves = scratch[9:]
    n = shard // CHUNKS
    local = Local(refs[-1])
    pack(local, [raw_u], grads_u)
    pack(local, [raw_d], grads_d)
    local.keep(rows_of(cot_full, 0, shard), cot)
    meet([place.core, place.near] + [place.column(1 << b) for b in range(bits)])

    def make(rows):
        return mm_nt(gi[rows, :], wu[...])

    def make2(rows):
        return mm(act[rows, :], wd[...])

    total = Scatter(link, place, make, *a_bufs, shard)
    total2 = Scatter(link, place, make2, *b_bufs, None, None, shard)
    size = grads_u.shape[0]
    slice_u, slice_d = (rows_of(slices, j * (size // columns), size // columns) for j in range(2))
    half_u = Halving(
        link, place, grads_u, 0, size, 0, halves[: bits - 1] + [slice_u], halves[bits - 1 : 2 * bits - 1]
    )
    halves = halves[2 * bits - 1 :]
    half_d = Halving(
        link, place, grads_d, 0, size, 1, halves[: bits - 1] + [slice_d], halves[bits - 1 : 2 * bits - 1]
    )
    local.drain()
    half_u.start(0)
    half_d.start(0)
    total.start()
    for i in range(CHUNKS):
        total.pass_on(i)
    total.rest()
    total2.start()
    total2.rest()
    for copy in total2.core.values():
        copy.wait_recv()

    def rows2(here):
        res[here, :] = mid[here, :] + total2.pair(here) + row_of(bias)

    def rows3(here):
        there = pl.ds(pl.multiple_of(here.start - shard, STEP), STEP)
        res_near[there, :] = total2.pair(here).astype(BF)

    over_rows(0, shard, STEP, rows2)
    over_rows(shard, shard, STEP, rows3)
    sums[...] = jnp.zeros_like(sums)
    near, core = {}, []
    for i in range(CHUNKS):
        total.ready(i)

        def rows(here):
            grad = total.rows(here)
            out_grad = cot[here, :].astype(F32)
            hat, rstd = norm_stats(mid[here, :])
            value = out_grad + norm_pull(grad, hat, rstd, row_of(gain))
            gmid[here, :] = value
            full[here, :] = value.astype(BF)
            for row, term in enumerate((value, grad * hat, grad, out_grad)):
                sums[row : row + 1, :] += jnp.sum(term, axis=0, keepdims=True)

        over_rows(i * n, n, STEP, rows)
        near[i], copy = gather_start(link, place, full, shard, i)
        core.append(copy)
    half_u.finish(0)
    half_d.finish(0)
    if bits > 1:
        half_u.start(1)
        half_d.start(1)
    for i in range(CHUNKS):
        core.append(gather_relay(link, place, full, shard, i, near[i]))
    for s in range(1, bits):
        half_u.finish(s)
        if s + 1 < bits:
            half_u.start(s + 1)
        half_d.finish(s)
        if s + 1 < bits:
            half_d.start(s + 1)
    for copy in core:
        copy.wait_recv()
    link.close()


def exit_kernel(
    columns, shard, dq, dk, dv, wq, own, gmid, slices, far, res, res_near, gq, gk, gv, go, small_in, gain, *refs
):
    place, link = Place(columns), Link(*refs[-3:-1])
    bits = place.bits
    inp, out, full_u, full_d, full_a, small = refs[:6]
    scratch = list(refs[6:-3])
    a_bufs = scratch[:4]
    swap_buf, out_buf, grads_a = scratch[4:7]
    steps = bits + 3
    sum_own, sum_got = scratch[7 : 7 + steps], scratch[7 + steps : 7 + 2 * steps]
    halves = scratch[7 + 2 * steps :]
    n = shard // CHUNKS
    local = Local(refs[-1])
    pack(local, [gq, gk, gv, go], grads_a)
    hops = [place.core] + [place.column(1 << b) for b in range(bits)] + [place.near, place.far]
    meet(hops + [place.swap])
    size = full_u.shape[0]

    def make(rows):
        return mm(dq[rows, :], wq[0]) + mm(dk[rows, :], wq[1]) + mm(dv[rows, :], wq[2])

    total = Scatter(link, place, make, *a_bufs, shard)
    groups, at = [], 0
    for count in groups_of(size // 2, 16 * columns):
        group = []
        for side in range(2):
            half = Halving(
                link, place, grads_a, side * (size // 2) + at, count, side,
                halves[:bits], halves[bits : 2 * bits],
            )
            group.append(Doubling(link, place, half, full_a, half.work[bits - 1], halves[2 * bits]))
            halves = halves[2 * bits + 1 :]
        groups.append(group)
        at += count
    half_u = Halving(link, place, None, 0, size, 0, [], [])
    half_d = Halving(link, place, None, 0, size, 1, [], [])
    held = size // columns
    double = [
        Doubling(link, place, half_u, full_u, rows_of(slices, 0, held), rows_of(far, 0, held)),
        Doubling(link, place, half_d, full_d, rows_of(slices, held, held), rows_of(far, held, held)),
    ]
    local.drain()
    for group in groups:
        for one in group:
            one.half.start(0)

    def finish_out(here):
        value = (res[here, :] + res_near[here, :].astype(F32)).astype(BF)
        out_buf[here, :] = value

        @pl.when(place.home)
        def _():
            out[here, :] = value

    over_rows(0, shard, STEP, finish_out)
    swaps = [link.send(out_buf, out, place.swap, place.away)]
    total.start()
    for i in range(CHUNKS):
        total.pass_on(i)
    total.rest()
    sum_own[0][...] = small_in[...]
    for s in range(bits):
        for group in groups:
            for one in group:
                one.half.finish(s)
                if s + 1 < bits:
                    one.half.start(s + 1)
                else:
                    one.start()
    for one in double:
        one.join()
    for i in range(CHUNKS):
        total.ready(i)

        def rows(here):
            grad = total.rows(here)
            hat, rstd = norm_stats(own[here, :].astype(F32))
            value = (gmid[here, :] + norm_pull(grad, hat, rstd, row_of(gain))).astype(BF)
            swap_buf[here, :] = value
            for row, term in enumerate((grad * hat, grad)):
                sum_own[0][row : row + 1, :] += jnp.sum(term, axis=0, keepdims=True)

            @pl.when(place.home)
            def _():
                inp[here, :] = value

        over_rows(i * n, n, STEP, rows)
        swaps.append(
            link.send(rows_of(swap_buf, i * n, n), rows_of(inp, i * n, n), place.swap, place.away)
        )
    hop_copies = [link.send(sum_own[0], sum_got[0], hops[0])]

    def next_hop(s):
        hop_copies[s].wait_recv()
        into = small if s + 1 == steps else sum_own[s + 1]
        into[...] = sum_own[s][...] + sum_got[s][...]
        if s + 1 < steps:
            hop_copies.append(link.send(sum_own[s + 1], sum_got[s + 1], hops[s + 1]))

    chain = [one.join for one in groups[0]] + [None]
    for s in range(bits):
        chain += [one.advance for one in double] + [None] + [one.advance for one in groups[0]]
        chain += [one.advance if s else one.join for group in groups[1:] for one in group] + [None]
    chain += [one.advance for group in groups[1:] for one in group]
    hop = 0
    for act in chain + [None] * steps:
        if act is not None:
            act()
        elif hop < steps:
            next_hop(hop)
            hop += 1
    for one in double + [one for group in groups for one in group]:
        for copy in one.cores:
            arrive(copy, place.away)
    for copy in swaps:
        arrive(copy, place.away)
    link.close()


def any_space():
    return pl.BlockSpec(memory_space=pl.ANY)


SEMS = 160


def sems(local=8):
    return [
        pltpu.SemaphoreType.DMA((SEMS,)),
        pltpu.SemaphoreType.DMA((SEMS,)),
        pltpu.SemaphoreType.DMA((local,)),
    ]


def remote_call(name, kernel, number, outs, in_specs, scratch):
    return pl.pallas_call(
        kernel,
        out_shape=outs,
        in_specs=in_specs,
        out_specs=jax.tree.map(lambda _: vmem(), outs),
        scratch_shapes=scratch + sems(),
        compiler_params=pltpu.CompilerParams(
            collective_id=number, has_side_effects=True, vmem_limit_bytes=62 << 20
        ),
        name=name,
    )


def shaped(shape, dtype):
    return jax.ShapeDtypeStruct(shape, dtype)


def like(x):
    return shaped(x.shape, x.dtype)


def enter(columns, hid, cot, ids, qv, ub, wq, wo, *vecs):
    shard, model = hid.shape
    outs = (like(hid), shaped((4 * shard, model), BF), like(cot), like(ids), like(qv), like(ub), like(wq), like(wo))
    call = remote_call(
        "enter", functools.partial(enter_kernel, columns, shard), 0, outs, [any_space()] * 7 + [vmem()] * 2, []
    )
    return call(hid, cot, ids, qv, ub, wq, wo, *vecs)


def make_mid(columns, att, wo, own, vecs, wu, wd, pieces, cot_own, cot_near):
    shard, model = own.shape
    whole = shaped((4 * shard, model), BF)
    outs = (shaped((shard, model), F32), whole, whole, like(wu), like(wd))
    call = remote_call(
        "mid", functools.partial(mid_kernel, columns, shard), 1, outs, [vmem()] * 6 + [any_space()] * 5,
        scatter_scratch(shard, model),
    )
    return call(att, wo, own, *vecs, wu, wd, pieces, cot_own, cot_near)


def make_back(columns, size, gi, wu, act, wd, grads_u, grads_d, mid, cot, *vecs):
    shard, model = mid.shape
    bits = columns.bit_length() - 1
    outs = (
        shaped((shard, model), F32),
        shaped((4 * shard, model), BF),
        shaped((shard, model), F32),
        shaped((shard, model), BF),
        shaped((2 * (size // columns), model), BF),
        shaped((8, model), F32),
    )
    per_side = halving_scratch(size, bits, model)
    halves = per_side[: bits - 1] + per_side
    call = remote_call(
        "back", functools.partial(back_kernel, columns, shard), 2, outs,
        [vmem()] * 4 + [any_space()] * 2 + [vmem(), any_space(), vmem(), vmem()],
        scatter_scratch(shard, model)
        + scatter_scratch(shard, model)[:2]
        + [pltpu.VMEM((shard, model), BF)]
        + [pltpu.VMEM((size, model), BF)] * 2
        + halves
        + halves,
    )
    return call(gi, wu, act, wd, grads_u, grads_d, mid, cot, *vecs)


def make_exit(columns, size, dq, dk, dv, wq, own, gmid, slices, far, res, res_near, grads, small, vec):
    shard, model = own.shape
    bits = columns.bit_length() - 1
    outs = (
        shaped((shard, model), BF),
        shaped((shard, model), BF),
        shaped((size, model), BF),
        shaped((size, model), BF),
        shaped((size, model), BF),
        shaped(small.shape, F32),
    )
    halves = []
    for count in groups_of(size // 2, 16 * columns):
        per_side = halving_scratch(count, bits, model)
        halves += (per_side + per_side + [per_side[-1]]) * 2
    steps = bits + 3
    call = remote_call(
        "exit", functools.partial(exit_kernel, columns, shard), 3, outs,
        [vmem()] * 10 + [any_space()] * 4 + [vmem()] * 2,
        scatter_scratch(shard, model)
        + [
            pltpu.VMEM((shard, model), BF),
            pltpu.VMEM((shard, model), BF),
            pltpu.VMEM((size, model), BF),
        ]
        + [pltpu.VMEM(small.shape, F32)] * (2 * steps)
        + halves,
    )
    return call(dq, dk, dv, wq, own, gmid, slices, far, res, res_near, *grads, small, vec)


def body(
    hidden,
    segment_ids,
    lengths,
    norm1_gain,
    norm1_shift,
    qkv_weight,
    qv_bias,
    out_weight,
    out_bias,
    norm2_gain,
    norm2_shift,
    up_weight,
    up_bias,
    down_weight,
    down_bias,
    cotangent,
):
    _, shard, model = hidden.shape
    seq = segment_ids.shape[1]
    width = qkv_weight.shape[2]
    d, t = lax.axis_index("dp"), lax.axis_index("tensor")
    columns = lax.axis_size("dp") // 2
    rank = 2 * (d & 1) + (t & 1)

    places = jnp.arange(seq, dtype=jnp.int32)
    ids = jnp.where(places < lengths[0], segment_ids[0], 16 + places)
    start = jnp.sum((ids[None, :] < ids[:, None]).astype(jnp.int32), axis=1)
    blocks = seq // BLK
    start = jnp.concatenate([start, start[::BLK] // BLK, jnp.zeros((LANES - blocks,), jnp.int32)])
    start = start[None]

    own, normed1, cot_own, start, b_qv, b_up, w_qkv, w_out = enter(
        columns, hidden[0], cotangent[0], start, qv_bias, up_bias, jnp.swapaxes(qkv_weight, 1, 2), out_weight,
        norm1_gain, norm1_shift,
    )
    everywhere = [(i, j) for i in range(2 * columns) for j in range(4)]
    to_near = [(4 * i + j, 4 * i + (j ^ 1)) for i, j in everywhere]
    to_away = [(4 * i + j, 4 * i + (j ^ 2)) for i, j in everywhere if i % 2 == j // 2]
    to_home = [(4 * i + j, 4 * i + (j ^ 2)) for i, j in everywhere if i % 2 != j // 2]
    axes = ("dp", "tensor")
    unit, rest = pieces_of(up_weight, columns)
    pieces = [lax.dynamic_slice_in_dim(w, (d // 2) * unit, unit, 0) for w in (up_weight, down_weight)]
    pieces += [w[unit * columns :] for w in (up_weight, down_weight)]
    cot_own, pieces, normed1 = lax.optimization_barrier((cot_own, jnp.concatenate(pieces), normed1))
    cot_near = lax.ppermute(cot_own, axes, to_near)
    pieces = lax.ppermute(pieces, axes, to_away)

    meta = jnp.concatenate([rank[None].astype(jnp.int32), start[0, seq : seq + blocks]])

    attended, lse, q, k, v = attn_fwd(meta, start, normed1, w_qkv, b_qv, shard)

    mid, normed2, cot_full, w_up, w_down = make_mid(
        columns,
        attended,
        w_out,
        own,
        (out_bias, norm2_gain, norm2_shift),
        up_weight,
        down_weight,
        pieces,
        cot_own,
        cot_near,
    )
    inner = mm(normed2, w_up) + b_up
    c0 = math.sqrt(2.0 / math.pi)
    tanh = jnp.tanh(c0 * (inner + 0.044715 * inner * inner * inner))
    active = (0.5 * inner * (1.0 + tanh)).astype(BF)
    slope = 0.5 * (1.0 + tanh) + 0.5 * inner * (1.0 - tanh * tanh) * c0 * (
        1.0 + 3 * 0.044715 * inner * inner
    )
    grad_inner = (mm_nt(cot_full, w_down) * slope).astype(BF)
    unit = 32 * columns
    size = -(-model // unit) * unit
    grad_mid, gm_full, res, res_near, slices, sums = make_back(
        columns,
        size,
        grad_inner,
        w_up,
        active,
        w_down,
        mm_tn(normed2, grad_inner).astype(BF),
        mm_tn(active, cot_full).astype(BF),
        mid,
        cot_full,
        norm2_gain,
        down_bias,
    )
    far = lax.ppermute(slices, axes, to_home)
    res_near = lax.ppermute(res_near, axes, to_near)
    dq, dk, dv = attn_bwd(meta, start, q, k, v, attended, gm_full, w_out, lse, shard)
    far, dk, dv = lax.optimization_barrier((far, dk, dv))
    res_near, dq = lax.optimization_barrier((res_near, dq))
    att_grads = [
        mm_tn(dq, normed1).astype(BF),
        mm_tn(dk, normed1).astype(BF),
        mm_tn(dv, normed1).astype(BF),
        mm_tn(attended, gm_full).astype(BF),
    ]

    qv_grad = jnp.concatenate([jnp.sum(dq, axis=0, dtype=F32), jnp.sum(dv, axis=0, dtype=F32)])
    qv_grad = jnp.pad(qv_grad, (0, model - 2 * width))
    up_b_grad = jnp.sum(grad_inner, axis=0, dtype=F32)
    slots = lax.broadcasted_iota(jnp.int32, (4, 1), 0) == rank
    small = jnp.concatenate(
        [
            jnp.zeros((2, model), F32),
            sums[:4],
            jnp.zeros((2, model), F32),
            jnp.where(slots, up_b_grad[None], 0.0),
            jnp.where(slots, qv_grad[None], 0.0),
        ]
    )
    input_grad, output, up_grad, down_grad, att_grad, small = make_exit(
        columns,
        size,
        dq,
        dk,
        dv,
        w_qkv,
        own,
        grad_mid,
        slices,
        far,
        res,
        res_near,
        att_grads,
        small,
        norm1_gain,
    )
    quarter = lax.dynamic_slice_in_dim(small, 12 + t, 1, 0)[0, : 2 * width].reshape(2, width)
    att_grad = att_grad.reshape(4, size // 4, model)
    qkv_grad = att_grad[:3, :width].astype(F32)
    return (
        output[None],
        input_grad[None],
        small[0],
        small[1],
        jnp.swapaxes(qkv_grad, 1, 2),
        quarter,
        att_grad[3, :width].astype(F32),
        small[2],
        small[3],
        small[4],
        up_grad[:model].astype(F32),
        lax.dynamic_slice_in_dim(small, 8 + t, 1, 0)[0],
        down_grad[:model].astype(F32),
        small[5],
    )


def solution(mesh):
    in_specs = (
        P("dp", "tensor", None),
        P("dp", None),
        P("dp"),
        P(),
        P(),
        P(None, None, "tensor"),
        P(None, "tensor"),
        P("tensor", None),
        P(),
        P(),
        P(),
        P(None, "tensor"),
        P("tensor"),
        P("tensor", None),
        P(),
        P("dp", "tensor", None),
    )
    out_specs = (
        P("dp", "tensor", None),
        P("dp", "tensor", None),
        P(),
        P(),
        P(None, None, "tensor"),
        P(None, "tensor"),
        P("tensor", None),
        P(),
        P(),
        P(),
        P(None, "tensor"),
        P("tensor"),
        P("tensor", None),
        P(),
    )
    return jax.shard_map(body, mesh=mesh, in_specs=in_specs, out_specs=out_specs, check_vma=False)
```

```python
import functools
import math

import jax
import jax.numpy as jnp
from jax import lax
from jax.experimental import pallas as pl
from jax.experimental.pallas import tpu as pltpu
from jax.sharding import PartitionSpec as P

HEAD = 56
EPS = 1e-05
LANES = 128
BLK = 256
BF = jnp.bfloat16
F32 = jnp.float32


def mm(a, b):
    return jnp.dot(a, b, preferred_element_type=F32)


def mm_nt(a, b):
    return lax.dot_general(a, b, (((1,), (1,)), ((), ())), preferred_element_type=F32)


def mm_tn(a, b):
    return lax.dot_general(a, b, (((0,), (0,)), ((), ())), preferred_element_type=F32)


def head_window(h):
    lo, hi = h * HEAD, (h + 1) * HEAD
    first = lo // LANES * LANES
    last = -(-hi // LANES) * LANES
    return first, last


def head_mask(h, rows):
    first, last = head_window(h)
    lane = lax.broadcasted_iota(jnp.int32, (rows, last - first), 1) + first
    return (lane >= h * HEAD) & (lane < (h + 1) * HEAD)


def stage_in(rank, src, dst, shard, width):
    wide = dst.shape[1]
    for s in range(src.shape[0] // shard):
        rel = pl.multiple_of((rank ^ s) * shard, 16)
        dst[s * shard : (s + 1) * shard, :width] = src[pl.ds(rel, shard), :]
    if wide > width:
        dst[:, width:] = jnp.zeros((dst.shape[0], wide - width), dst.dtype)


def project(rank, src, shard, width, products):
    @pl.loop(0, src.shape[0] // shard)
    def _(s):
        rel = pl.multiple_of((rank ^ s) * shard, 16)
        rows = pl.ds(pl.multiple_of(s * shard, 16), shard)
        x = src[pl.ds(rel, shard), :]
        for dst, weight, bias in products:
            value = dot_nt(x, weight[...])
            if bias is not None:
                value = value + bias
            dst[rows, :width] = value.astype(BF)

    for dst, _, _ in products:
        if dst.shape[1] > width:
            dst[:, width:] = jnp.zeros((dst.shape[0], dst.shape[1] - width), BF)


def stage_out(rank, src, dst, shard, width):
    for s in range(dst.shape[0] // shard):
        rel = pl.multiple_of((rank ^ s) * shard, 16)
        dst[pl.ds(rel, shard), :] = src[s * shard : (s + 1) * shard, :width]


def tile_mask(start_row, qb, kb):
    kpos = kb * BLK + lax.broadcasted_iota(jnp.int32, (BLK, BLK), 0)
    qpos = qb * BLK + lax.broadcasted_iota(jnp.int32, (BLK, BLK), 1)
    return (kpos <= qpos) & (kpos >= start_row)


def dot_nt(a, b):
    return lax.dot_general(a, b, (((1,), (1,)), ((), ())), preferred_element_type=F32)


def attn_fwd_kernel(heads, shard, meta, start, normed, wq, bias, out, lse, qs, ks, vs, vt, os, ot, ms, ls, acc):
    seq, width = out.shape
    scale2 = HEAD ** (-0.5) * math.log2(math.e)
    rank = meta[0]
    b_q, b_v = bias[0:1, :], bias[1:2, :]
    project(
        rank, normed, shard, width, [(qs, wq.at[0], b_q), (ks, wq.at[1], None), (vs, wq.at[2], b_v)]
    )
    blocks = seq // BLK

    @pl.loop(0, blocks)
    def _(b):
        rows = pl.ds(pl.multiple_of(b * BLK, BLK), BLK)
        flipped = vs[rows, :].astype(F32).T
        for h in range(heads):
            vt[h, :, rows] = flipped[h * HEAD : (h + 1) * HEAD, :].astype(BF)

    lse[...] = jnp.zeros_like(lse)

    @pl.loop(0, blocks)
    def _(b):
        rows = pl.ds(pl.multiple_of(b * BLK, BLK), BLK)
        start_row = start[0:1, rows]
        ms[...] = jnp.full_like(ms, -1e30)
        ls[...] = jnp.zeros_like(ls)
        acc[...] = jnp.zeros_like(acc)

        def tile(kb, carry):
            krows = pl.ds(pl.multiple_of(kb * BLK, BLK), BLK)
            mask = tile_mask(start_row, b, kb)
            for h in range(heads):
                first, last = head_window(h)
                qm = jnp.where(head_mask(h, BLK), qs[rows, first:last], 0)
                s = dot_nt(ks[krows, first:last], qm) * scale2
                s = jnp.where(mask, s, -1e30)
                old = ms[h : h + 1, :]
                new = jnp.maximum(old, jnp.max(s, axis=0, keepdims=True))
                p = jnp.exp2(s - new)
                p = jnp.where(mask, p, 0.0)
                fade = jnp.exp2(old - new)
                ms[h : h + 1, :] = new
                ls[h : h + 1, :] = ls[h : h + 1, :] * fade + jnp.sum(p, axis=0, keepdims=True)
                acc[h] = acc[h] * fade + jnp.dot(
                    vt[h, :, krows], p.astype(BF), preferred_element_type=F32
                )
            return carry

        lax.fori_loop(meta[1 + b], b + 1, tile, 0)
        for h in range(heads):
            total = ls[h : h + 1, :]
            lse[h : h + 1, rows] = ms[h : h + 1, :] + jnp.log(total) * math.log2(math.e)
            ot[h * HEAD : (h + 1) * HEAD, :] = acc[h] / total
        os[rows, :] = ot[...].T.astype(BF)

    stage_out(rank, os, out, shard, width)


def attn_bwd_kernel(
    heads, shard, meta, start, qs, ks, vs, o, gm, wo, lse, dq, dk, dv,
    os, dos, kt, delta, dqs, dks, dvs, dqt, qm, dm,
):
    seq, width = o.shape
    scale = HEAD ** (-0.5)
    scale2 = scale * math.log2(math.e)
    rank = meta[0]
    blocks = seq // BLK
    stage_in(rank, o, os, shard, width)
    project(rank, gm, shard, width, [(dos, wo, None)])

    @pl.loop(0, blocks)
    def _(b):
        rows = pl.ds(pl.multiple_of(b * BLK, BLK), BLK)
        flipped = (os[rows, :].astype(F32) * dos[rows, :].astype(F32)).T
        for h in range(heads):
            delta[h : h + 1, rows] = jnp.sum(
                flipped[h * HEAD : (h + 1) * HEAD, :], axis=0, keepdims=True
            )

    @pl.loop(0, blocks)
    def _(b):
        rows = pl.ds(pl.multiple_of(b * BLK, BLK), BLK)
        flipped = ks[rows, :].astype(F32).T
        for h in range(heads):
            kt[h, :, rows] = flipped[h * HEAD : (h + 1) * HEAD, :].astype(BF)

    dks[...] = jnp.zeros_like(dks)
    dvs[...] = jnp.zeros_like(dvs)
    dqt[...] = jnp.zeros_like(dqt)

    @pl.loop(0, blocks)
    def _(b):
        rows = pl.ds(pl.multiple_of(b * BLK, BLK), BLK)
        start_row = start[0:1, rows]
        dqt[...] = jnp.zeros_like(dqt)
        for h in range(heads):
            first, last = head_window(h)
            keep = head_mask(h, BLK)
            qm[h, :, : last - first] = jnp.where(keep, qs[rows, first:last], 0)
            dm[h, :, : last - first] = jnp.where(keep, dos[rows, first:last], 0)

        def tile(kb, carry):
            krows = pl.ds(pl.multiple_of(kb * BLK, BLK), BLK)
            mask = tile_mask(start_row, b, kb)
            for h in range(heads):
                first, last = head_window(h)
                qh = qm[h, :, : last - first]
                dh = dm[h, :, : last - first]
                s = dot_nt(ks[krows, first:last], qh) * scale2
                p = jnp.where(mask, jnp.exp2(s - lse[h : h + 1, rows]), 0.0)
                dp = dot_nt(vs[krows, first:last], dh)
                ds = (p * (dp - delta[h : h + 1, rows])).astype(BF)
                dvs[krows, first:last] += jnp.dot(p.astype(BF), dh, preferred_element_type=F32)
                dks[krows, first:last] += jnp.dot(ds, qh, preferred_element_type=F32)
                dqt[h * HEAD : (h + 1) * HEAD, :] += jnp.dot(
                    kt[h, :, krows], ds, preferred_element_type=F32
                )
            return carry

        lax.fori_loop(meta[1 + b], b + 1, tile, 0)
        dqs[rows, :] = (dqt[...].T * scale).astype(BF)

    stage_out(rank, dqs, dq, shard, width)
    for s in range(seq // shard):
        rel = pl.multiple_of((rank ^ s) * shard, 16)
        here = slice(s * shard, (s + 1) * shard)
        dk[pl.ds(rel, shard), :] = (dks[here, :width] * scale).astype(BF)
        dv[pl.ds(rel, shard), :] = dvs[here, :width].astype(BF)


def vmem():
    return pl.BlockSpec(memory_space=pltpu.VMEM)


def smem():
    return pl.BlockSpec(memory_space=pltpu.SMEM)


def attn_cost(seq, width, products):
    return pl.CostEstimate(
        flops=products * seq * seq * width,
        bytes_accessed=8 * seq * width * 2,
        transcendentals=seq * seq * width // (2 * HEAD),
    )


def attn_fwd(meta, start, normed, wq, bias, shard):
    seq, (_, width, _) = normed.shape[0], wq.shape
    heads = width // HEAD
    wide = -(-width // LANES) * LANES
    staged = jax.ShapeDtypeStruct((seq, wide), BF)
    return pl.pallas_call(
        functools.partial(attn_fwd_kernel, heads, shard),
        out_shape=(
            jax.ShapeDtypeStruct((seq, width), BF),
            jax.ShapeDtypeStruct((8, seq), F32),
            staged,
            staged,
            staged,
        ),
        in_specs=[smem()] + [vmem()] * 4,
        out_specs=(vmem(),) * 5,
        scratch_shapes=[
            pltpu.VMEM((heads, HEAD, seq), BF),
            pltpu.VMEM((seq, wide), BF),
            pltpu.VMEM((wide, BLK), F32),
            pltpu.VMEM((8, BLK), F32),
            pltpu.VMEM((8, BLK), F32),
            pltpu.VMEM((heads, HEAD, BLK), F32),
        ],
        cost_estimate=attn_cost(seq, width, 3),
        name="attn_fwd",
    )(meta, start, normed, wq, bias)


def attn_bwd(meta, start, q, k, v, o, gm, wo, lse, shard):
    seq, width = o.shape
    heads = width // HEAD
    wide = q.shape[1]
    grad = jax.ShapeDtypeStruct((seq, width), BF)
    return pl.pallas_call(
        functools.partial(attn_bwd_kernel, heads, shard),
        out_shape=(grad, grad, grad),
        in_specs=[smem()] + [vmem()] * 8,
        out_specs=(vmem(), vmem(), vmem()),
        scratch_shapes=[
            pltpu.VMEM((seq, wide), BF),
            pltpu.VMEM((seq, wide), BF),
            pltpu.VMEM((heads, HEAD, seq), BF),
            pltpu.VMEM((8, seq), F32),
            pltpu.VMEM((seq, wide), BF),
            pltpu.VMEM((seq, wide), F32),
            pltpu.VMEM((seq, wide), F32),
            pltpu.VMEM((wide, BLK), F32),
            pltpu.VMEM((heads, BLK, 2 * LANES), BF),
            pltpu.VMEM((heads, BLK, 2 * LANES), BF),
        ],
        cost_estimate=attn_cost(seq, width, 8),
        name="attn_bwd",
    )(meta, start, q, k, v, o, gm, wo, lse)


MESH = pl.DeviceIdType.MESH
CHUNKS = 2
STEP = 32


class Place:
    def __init__(self, columns):
        d, t = lax.axis_index("dp"), lax.axis_index("tensor")
        core, low, high = lax.rem(d, 2), lax.rem(t, 2), lax.div(t, 2)
        self.d, self.t, self.columns = d, t, columns
        self.bits = columns.bit_length() - 1
        self.core = (d + 1 - 2 * core, t)
        self.near = (d, t + 1 - 2 * low)
        self.far = (d, t + 2 - 4 * high)
        self.swap = (d + 1 - 2 * core, t + 2 - 4 * high)
        self.home = core == high
        self.away = core != high

    def bit(self, b):
        return lax.rem(lax.div(self.d, 2 << b), 2)

    def column(self, m):
        d = self.d
        for b in range(self.bits):
            if (m >> b) & 1:
                d = d + (2 << b) * (1 - 2 * self.bit(b))
        return (d, self.t)


class Link:
    def __init__(self, send_sems, recv_sems):
        self.send_sems, self.recv_sems = send_sems, recv_sems
        self.count = 0
        self.open, self.kept, self.number = [], [], {}

    def make(self, src, dst, to, like=None):
        if like is None:
            i = self.count
            self.count += 1
        else:
            i = self.number[id(like)]
        copy = pltpu.make_async_remote_copy(
            src_ref=src,
            dst_ref=dst,
            send_sem=self.send_sems.at[i],
            recv_sem=self.recv_sems.at[i],
            device_id=to,
            device_id_type=MESH,
        )
        self.number[id(copy)] = i
        self.kept.append(copy)
        return copy

    def start(self, copy, when=None):
        if when is None:
            copy.start()
        else:
            pl.when(when)(copy.start)
        self.open.append((copy, when))

    def send(self, src, dst, to, when=None):
        copy = self.make(src, dst, to)
        self.start(copy, when)
        return copy

    def close(self):
        for copy, when in self.open:
            if when is None:
                copy.wait_send()
            else:
                pl.when(when)(copy.wait_send)


def arrive(copy, when=None):
    if when is None:
        copy.wait_recv()
    else:
        pl.when(when)(copy.wait_recv)


def meet(partners):
    barrier = pltpu.get_barrier_semaphore()
    for to in partners:
        pl.semaphore_signal(barrier, inc=1, device_id=to, device_id_type=MESH)
    pl.semaphore_wait(barrier, len(partners))


def row_of(ref):
    return ref[...][None, :]


def rows_of(ref, first, count):
    return ref.at[pl.ds(first, count)]


def gather_start(link, place, full, shard, i):
    n = shard // CHUNKS
    near = link.send(rows_of(full, i * n, n), rows_of(full, shard + i * n, n), place.near)
    core = link.send(rows_of(full, i * n, n), rows_of(full, 2 * shard + i * n, n), place.core)
    return near, core


def gather_relay(link, place, full, shard, i, near):
    n = shard // CHUNKS
    near.wait_recv()
    return link.send(
        rows_of(full, shard + i * n, n), rows_of(full, 3 * shard + i * n, n), place.core
    )


class Scatter:
    def __init__(self, link, place, make, part, core_buf, out_buf, near_buf, shard):
        self.link, self.place, self.make, self.part = link, place, make, part
        self.core_buf, self.out_buf, self.near_buf = core_buf, out_buf, near_buf
        self.shard, self.n = shard, shard // CHUNKS
        self.core, self.near = {}, {}

    def fill(self, block):
        rows = pl.ds(pl.multiple_of(block * self.shard, 16), self.shard)
        self.part[rows, :] = self.make(rows).astype(BF)

    def to_core(self, block):
        for i in range(CHUNKS):
            at = (block - 2) * self.shard + i * self.n
            self.core[block - 2, i] = self.link.send(
                rows_of(self.part, 2 * self.shard + at, self.n),
                rows_of(self.core_buf, at, self.n),
                self.place.core,
            )

    def start(self):
        self.fill(3)
        self.to_core(3)
        self.fill(1)

    def rest(self):
        @pl.loop(0, 2)
        def _(b):
            self.fill(2 - 2 * b)

        self.to_core(2)

    def pass_on(self, i):
        at = self.shard + i * self.n
        self.core[1, i].wait_recv()

        @pl.loop(0, self.n // STEP)
        def _(r):
            here = pl.multiple_of(at + r * STEP, STEP)
            there = pl.multiple_of(i * self.n + r * STEP, STEP)
            total = self.part[pl.ds(here, STEP), :].astype(F32) + self.core_buf[
                pl.ds(here, STEP), :
            ].astype(F32)
            self.out_buf[pl.ds(there, STEP), :] = total.astype(BF)

        self.near[i] = self.link.send(
            rows_of(self.out_buf, i * self.n, self.n),
            rows_of(self.near_buf, i * self.n, self.n),
            self.place.near,
        )

    def pair(self, rows):
        return self.part[rows, :].astype(F32) + self.core_buf[rows, :].astype(F32)

    def ready(self, i):
        self.core[0, i].wait_recv()
        self.near[i].wait_recv()

    def rows(self, rows):
        return (
            self.part[rows, :].astype(F32)
            + self.core_buf[rows, :].astype(F32)
            + self.near_buf[rows, :].astype(F32)
        )


class Spread:
    def __init__(self, link, place, src, dst):
        self.link, self.place, self.src, self.dst = link, place, src, dst
        rows = src.shape[-2]
        self.unit = rows // (16 * place.columns) * 16
        self.rest = rows - self.unit * place.columns
        self.at = pl.multiple_of(lax.div(place.d, 2) * self.unit, 16)
        self.pieces, self.shared = [], []

    def move(self, src, at, count, to, when):
        return self.link.send(rows_of(src, at, count), rows_of(self.dst, at, count), to, when)

    def open(self):
        far, home = self.place.far, self.place.home
        if self.unit:
            self.first = self.move(self.src, self.at, self.unit, far, home)
        if self.rest:
            at = self.unit * self.place.columns
            self.pieces.append(self.move(self.src, at, self.rest, far, home))

    def share(self):
        away = self.place.away
        if self.unit:
            arrive(self.first, away)
            for m in range(1, self.place.columns):
                to = self.place.column(m)
                self.pieces.append(self.move(self.dst, self.at, self.unit, to, away))

    def drain(self):
        for copy in self.pieces:
            arrive(copy, self.place.away)


class Local:
    def __init__(self, sems, when=None, base=0):
        self.sems, self.when, self.base, self.copies = sems, when, base, []

    def keep(self, src, dst):
        copy = pltpu.make_async_copy(src, dst, self.sems.at[self.base + len(self.copies)])
        self.copies.append(copy)
        self.run(copy.start)
        return copy

    def run(self, act):
        if self.when is None:
            act()
        else:
            pl.when(self.when)(act)

    def drain(self, first=0):
        for copy in self.copies[first:]:
            self.run(copy.wait)


def pack(local, sources, buf):
    block = buf.shape[0] // len(sources)
    for j, src in enumerate(sources):
        count = src.shape[0]
        local.keep(src, rows_of(buf, j * block, count))
        if count < block:
            buf[j * block + count : (j + 1) * block, :] = jnp.zeros((block - count, buf.shape[1]), buf.dtype)


def scatter_scratch(shard, model):
    return [
        pltpu.VMEM((4 * shard, model), BF),
        pltpu.VMEM((2 * shard, model), BF),
        pltpu.VMEM((shard, model), BF),
        pltpu.VMEM((shard, model), BF),
    ]


def over_rows(first, count, step, fn):
    @pl.loop(0, count // step)
    def _(r):
        fn(pl.ds(pl.multiple_of(first + r * step, 16), step))


class Halving:
    def __init__(self, link, place, source, first, size, turn, work, got):
        self.link, self.place = link, place
        self.source, self.first, self.size = source, first, size
        self.order = [(b + turn) % place.bits for b in range(place.bits)]
        self.work, self.got = work, got
        self.copies = []

    def start(self, s):
        n = self.size >> (s + 1)
        bit = self.place.bit(self.order[s])
        src, base = (self.source, self.first) if s == 0 else (self.work[s - 1], 0)
        at = pl.multiple_of(base + (1 - bit) * n, 16)
        self.copies.append(
            self.link.send(
                rows_of(src, at, n), self.got[s], self.place.column(1 << self.order[s])
            )
        )

    def finish(self, s):
        n = self.size >> (s + 1)
        bit = self.place.bit(self.order[s])
        src, base = (self.source, self.first) if s == 0 else (self.work[s - 1], 0)
        self.copies[s].wait_recv()

        step = step_of(n)

        @pl.loop(0, n // step)
        def _(r):
            here = pl.multiple_of(base + bit * n + r * step, 16)
            to = pl.ds(pl.multiple_of(r * step, 16), step)
            total = src[pl.ds(here, step), :].astype(F32) + self.got[s][to, :].astype(F32)
            self.work[s][to, :] = total.astype(BF)

    def offset(self):
        at, n = 0, self.size
        for b in self.order:
            n //= 2
            at = at + self.place.bit(b) * n
        return self.first + at


def step_of(n):
    return next(step for step in (48, 32, 16) if n % step == 0)


def groups_of(side, unit):
    units = side // unit
    first = max(1, min(units - 1, 2 * units // 3))
    return [count * unit for count in (first, units - first) if count]


def halving_scratch(size, bits, model):
    return [pltpu.VMEM((size >> (s + 1), model), BF) for s in range(bits)]


class Doubling:
    def __init__(self, link, place, half, full, slice_ref, far_buf):
        self.link, self.place, self.half, self.full = link, place, half, full
        self.far = None
        self.slice_ref, self.far_buf = slice_ref, far_buf
        self.n = half.size >> place.bits
        self.at = half.offset()
        self.cores, self.waits = [], []

    def start(self):
        self.far = self.link.send(
            self.slice_ref, self.far_buf, self.place.far, self.place.away
        )

    def to_core(self, at, n):
        self.link.send(
            rows_of(self.full, at, n), rows_of(self.full, at, n), self.place.core, self.place.home
        )

    def join(self):
        if self.far is not None:
            arrive(self.far, self.place.home)

        @pl.when(self.place.home)
        def _():
            step = step_of(self.n)

            @pl.loop(0, self.n // step)
            def _(r):
                here = pl.ds(pl.multiple_of(r * step, 16), step)
                to = pl.ds(pl.multiple_of(self.at + r * step, 16), step)
                total = self.slice_ref[here, :].astype(F32) + self.far_buf[here, :].astype(F32)
                self.full[to, :] = total.astype(BF)

        self.block, self.count = pl.multiple_of(self.at, 16), self.n
        self.stage = 0
        self.push(self.block)

    def push(self, fresh):
        if self.stage < self.place.bits:
            b = self.half.order[self.place.bits - 1 - self.stage]
            self.copy = self.link.send(
                rows_of(self.full, self.block, self.count),
                rows_of(self.full, self.block, self.count),
                self.place.column(1 << b),
                self.place.home,
            )
        copy = self.link.send(
            rows_of(self.full, fresh, self.count if self.stage == 0 else self.count // 2),
            rows_of(self.full, fresh, self.count if self.stage == 0 else self.count // 2),
            self.place.core,
            self.place.home,
        )
        self.cores.append(copy)

    def advance(self):
        b = self.half.order[self.place.bits - 1 - self.stage]
        bit = self.place.bit(b)
        fresh = pl.multiple_of(self.block + (1 - 2 * bit) * self.count, 16)
        arrive(self.copy, self.place.home)
        self.block = pl.multiple_of(self.block - bit * self.count, 16)
        self.count *= 2
        self.stage += 1
        self.push(fresh)


def norm_stats(values):
    center = values - jnp.mean(values, axis=-1, keepdims=True)
    rstd = lax.rsqrt(jnp.mean(center * center, axis=-1, keepdims=True) + EPS)
    return center * rstd, rstd


def norm_pull(grad, hat, rstd, gain):
    gn = grad * gain
    return rstd * (
        gn
        - jnp.mean(gn, axis=-1, keepdims=True)
        - hat * jnp.mean(gn * hat, axis=-1, keepdims=True)
    )


def enter_kernel(
    columns, shard, hid, cot, ids, qv, ub, wq, wo, gain, shift,
    own, full, cot_own, ids_o, qv_o, ub_o, wq_o, wo_o, send_sems, recv_sems, local_sems,
):
    place, link = Place(columns), Link(send_sems, recv_sems)
    n = shard // CHUNKS
    home, away = place.home, place.away
    meet([place.core, place.near, place.far, place.swap] + [place.column(m) for m in range(1, columns)])
    weights = [Spread(link, place, wq.at[j], wq_o.at[j]) for j in range(wq.shape[0])]
    weights.append(Spread(link, place, wo, wo_o))

    ids_copy = link.send(ids, ids_o, place.swap, away)
    swaps = [
        link.send(rows_of(hid, i * n, n), rows_of(own, i * n, n), place.swap, away) for i in range(CHUNKS)
    ]
    for weight in weights:
        weight.open()
    qv_copy = link.send(qv, qv_o, place.far, home)
    ub_copy = link.send(ub, ub_o, place.far, home)
    local = Local(local_sems, home)
    held = [local.keep(rows_of(hid, i * n, n), rows_of(own, i * n, n)) for i in range(CHUNKS)]
    local.keep(cot, cot_own)
    local.keep(wq, wq_o)
    local.keep(wo, wo_o)
    local.keep(ids, ids_o)
    local.keep(qv, qv_o)
    local.keep(ub, ub_o)

    near, core = {}, []
    for i in range(CHUNKS):
        pl.when(home)(held[i].wait)
        arrive(swaps[i], away)

        def rows(here):
            hat = norm_stats(own[here, :].astype(F32))[0]
            full[here, :] = (hat * row_of(gain) + row_of(shift)).astype(BF)

        over_rows(i * n, n, STEP, rows)
        near[i], copy = gather_start(link, place, full, shard, i)
        core.append(copy)
    cot_copy = link.send(cot, cot_own, place.swap, away)
    for i in range(CHUNKS):
        core.append(gather_relay(link, place, full, shard, i, near[i]))
    for weight in weights:
        weight.share()
    for copy in core:
        copy.wait_recv()
    for weight in weights:
        weight.drain()
    for copy in (ids_copy, qv_copy, ub_copy, cot_copy):
        arrive(copy, away)
    local.drain(CHUNKS)
    link.close()


def mid_kernel(
    columns, shard, att, wo, own, bias, gain, shift, wu, wd, pieces, cot_own, cot_near,
    mid, full_out, cfull_out, wu_out, wd_out, full, cfull, wu_o, wd_o,
    part, core_buf, out_buf, near_buf, send_sems, recv_sems, local_sems
):
    place, link = Place(columns), Link(send_sems, recv_sems)
    n = shard // CHUNKS
    home, away = place.home, place.away
    stores = Local(local_sems, None, 8)
    unit, rest = pieces_of(wu, columns)
    at = pl.multiple_of(lax.div(place.d, 2) * unit, 16)
    mine = Local(local_sems, home, 0)
    mine.keep(wu, wu_o)
    mine.keep(wd, wd_o)
    both = Local(local_sems, None, 2)
    both.keep(cot_own, rows_of(cfull, 0, shard))
    both.keep(cot_near, rows_of(cfull, shard, shard))
    other = Local(local_sems, away, 4)
    for j, out in enumerate((wu_o, wd_o)):
        if unit:
            other.keep(rows_of(pieces, j * unit, unit), rows_of(out, at, unit))
        if rest:
            last = rows_of(pieces, 2 * unit + j * rest, rest)
            other.keep(last, rows_of(out, unit * columns, rest))
    meet([place.core, place.near, place.far] + [place.column(m) for m in range(1, columns)])
    shared = []
    if unit:
        for j, out in enumerate((wu_o, wd_o)):
            for m in range(1, columns):
                src = rows_of(pieces, j * unit, unit)
                shared.append(link.send(src, rows_of(out, at, unit), place.column(m), away))

    def make(rows):
        return mm(att[rows, :], wo[...])

    total = Scatter(link, place, make, part, core_buf, out_buf, near_buf, shard)
    total.start()
    for i in range(CHUNKS):
        total.pass_on(i)
    total.rest()
    core = [
        link.send(cot_own, rows_of(cfull, 2 * shard, shard), place.core),
        link.send(cot_near, rows_of(cfull, 3 * shard, shard), place.core),
    ]
    near = {}
    for i in range(CHUNKS):
        total.ready(i)

        def rows(here):
            value = own[here, :].astype(F32) + total.rows(here) + row_of(bias)
            mid[here, :] = value
            full[here, :] = (norm_stats(value)[0] * row_of(gain) + row_of(shift)).astype(BF)

        over_rows(i * n, n, STEP, rows)
        near[i], copy = gather_start(link, place, full, shard, i)
        core.append(copy)
    for copy in shared:
        arrive(copy, away)
    for local in (mine, both, other):
        local.drain()
    for copy in core[:2]:
        copy.wait_recv()
    stores.keep(wu_o, wu_out)
    stores.keep(wd_o, wd_out)
    stores.keep(cfull, cfull_out)
    for i in range(CHUNKS):
        core.append(gather_relay(link, place, full, shard, i, near[i]))
    stores.keep(rows_of(full, 0, 2 * shard), rows_of(full_out, 0, 2 * shard))
    for copy in core[2:]:
        copy.wait_recv()
    stores.keep(rows_of(full, 2 * shard, 2 * shard), rows_of(full_out, 2 * shard, 2 * shard))
    stores.drain()
    link.close()


def pieces_of(weight, columns):
    rows = weight.shape[0]
    unit = rows // (16 * columns) * 16
    return unit, rows - unit * columns


def back_kernel(
    columns, shard, gi, wu, act, wd, raw_u, raw_d, mid, cot_full, gain, bias, *refs
):
    place, link = Place(columns), Link(*refs[-3:-1])
    bits = place.bits
    gmid, full, res, res_near, slices, sums = refs[:6]
    scratch = list(refs[6:-3])
    a_bufs, b_bufs = scratch[:4], scratch[4:6]
    cot, grads_u, grads_d = scratch[6:9]
    halves = scratch[9:]
    n = shard // CHUNKS
    local = Local(refs[-1])
    pack(local, [raw_u], grads_u)
    pack(local, [raw_d], grads_d)
    local.keep(rows_of(cot_full, 0, shard), cot)
    meet([place.core, place.near] + [place.column(1 << b) for b in range(bits)])

    def make(rows):
        return mm_nt(gi[rows, :], wu[...])

    def make2(rows):
        return mm(act[rows, :], wd[...])

    total = Scatter(link, place, make, *a_bufs, shard)
    total2 = Scatter(link, place, make2, *b_bufs, None, None, shard)
    size = grads_u.shape[0]
    slice_u, slice_d = (rows_of(slices, j * (size // columns), size // columns) for j in range(2))
    half_u = Halving(
        link, place, grads_u, 0, size, 0, halves[: bits - 1] + [slice_u], halves[bits - 1 : 2 * bits - 1]
    )
    halves = halves[2 * bits - 1 :]
    half_d = Halving(
        link, place, grads_d, 0, size, 1, halves[: bits - 1] + [slice_d], halves[bits - 1 : 2 * bits - 1]
    )
    local.drain()
    half_u.start(0)
    half_d.start(0)
    total.start()
    for i in range(CHUNKS):
        total.pass_on(i)
    total.rest()
    total2.start()
    total2.rest()
    for copy in total2.core.values():
        copy.wait_recv()

    def rows2(here):
        res[here, :] = mid[here, :] + total2.pair(here) + row_of(bias)

    def rows3(here):
        there = pl.ds(pl.multiple_of(here.start - shard, STEP), STEP)
        res_near[there, :] = total2.pair(here).astype(BF)

    over_rows(0, shard, STEP, rows2)
    over_rows(shard, shard, STEP, rows3)
    sums[...] = jnp.zeros_like(sums)
    near, core = {}, []
    for i in range(CHUNKS):
        total.ready(i)

        def rows(here):
            grad = total.rows(here)
            out_grad = cot[here, :].astype(F32)
            hat, rstd = norm_stats(mid[here, :])
            value = out_grad + norm_pull(grad, hat, rstd, row_of(gain))
            gmid[here, :] = value
            full[here, :] = value.astype(BF)
            for row, term in enumerate((value, grad * hat, grad, out_grad)):
                sums[row : row + 1, :] += jnp.sum(term, axis=0, keepdims=True)

        over_rows(i * n, n, STEP, rows)
        near[i], copy = gather_start(link, place, full, shard, i)
        core.append(copy)
    half_u.finish(0)
    half_d.finish(0)
    if bits > 1:
        half_u.start(1)
        half_d.start(1)
    for i in range(CHUNKS):
        core.append(gather_relay(link, place, full, shard, i, near[i]))
    for s in range(1, bits):
        half_u.finish(s)
        if s + 1 < bits:
            half_u.start(s + 1)
        half_d.finish(s)
        if s + 1 < bits:
            half_d.start(s + 1)
    for copy in core:
        copy.wait_recv()
    link.close()


def exit_kernel(
    columns, shard, *refs
):
    place, link = Place(columns), Link(*refs[-3:-1])
    bits = place.bits
    given, (gq, gk, gv, go, small_in, gain), refs = refs[:10], refs[10:16], refs[16:]
    inp, out, out_u, out_d, out_a, small = refs[:6]
    held, (full_u, full_d, full_a), scratch = refs[6:16], refs[16:19], list(refs[19:-3])
    res, res_near, dq, dk, dv, wq, slices, far, gmid, own = held
    a_bufs = scratch[:4]
    swap_buf, out_buf, grads_a = scratch[4:7]
    steps = bits + 3
    sum_own, sum_got = scratch[7 : 7 + steps], scratch[7 + steps : 7 + 2 * steps]
    halves = scratch[7 + 2 * steps :]
    n = shard // CHUNKS
    local = Local(refs[-1])
    pack(local, [gq, gk, gv, go], grads_a)
    loads = Local(refs[-1], None, 4)
    for src, dst in zip(given, held):
        loads.keep(src, dst)
    stores = Local(refs[-1], None, 14)
    hops = [place.core] + [place.column(1 << b) for b in range(bits)] + [place.near, place.far]
    meet(hops + [place.swap])
    size = full_u.shape[0]

    def make(rows):
        return mm(dq[rows, :], wq[0]) + mm(dk[rows, :], wq[1]) + mm(dv[rows, :], wq[2])

    total = Scatter(link, place, make, *a_bufs, shard)
    groups, at = [], 0
    for count in groups_of(size // 2, 16 * columns):
        group = []
        for side in range(2):
            half = Halving(
                link, place, grads_a, side * (size // 2) + at, count, side,
                halves[:bits], halves[bits : 2 * bits],
            )
            group.append(Doubling(link, place, half, full_a, half.work[bits - 1], halves[2 * bits]))
            halves = halves[2 * bits + 1 :]
        groups.append(group)
        at += count
    half_u = Halving(link, place, None, 0, size, 0, [], [])
    half_d = Halving(link, place, None, 0, size, 1, [], [])
    part = size // columns
    double = [
        Doubling(link, place, half_u, full_u, rows_of(slices, 0, part), rows_of(far, 0, part)),
        Doubling(link, place, half_d, full_d, rows_of(slices, part, part), rows_of(far, part, part)),
    ]
    local.drain()
    for group in groups:
        for one in group:
            one.half.start(0)

    def finish_out(here):
        value = (res[here, :] + res_near[here, :].astype(F32)).astype(BF)
        out_buf[here, :] = value

        @pl.when(place.home)
        def _():
            out[here, :] = value

    for copy in loads.copies[:2]:
        copy.wait()
    over_rows(0, shard, STEP, finish_out)
    swaps = [link.send(out_buf, out, place.swap, place.away)]
    for copy in loads.copies[2:6]:
        copy.wait()
    total.start()
    for i in range(CHUNKS):
        total.pass_on(i)
    total.rest()
    sum_own[0][...] = small_in[...]
    for s in range(bits):
        for group in groups:
            for one in group:
                one.half.finish(s)
                if s + 1 < bits:
                    one.half.start(s + 1)
                else:
                    one.start()
    for copy in loads.copies[6:]:
        copy.wait()
    for one in double:
        one.join()
    for i in range(CHUNKS):
        total.ready(i)

        def rows(here):
            grad = total.rows(here)
            hat, rstd = norm_stats(own[here, :].astype(F32))
            value = (gmid[here, :] + norm_pull(grad, hat, rstd, row_of(gain))).astype(BF)
            swap_buf[here, :] = value
            for row, term in enumerate((grad * hat, grad)):
                sum_own[0][row : row + 1, :] += jnp.sum(term, axis=0, keepdims=True)

            @pl.when(place.home)
            def _():
                inp[here, :] = value

        over_rows(i * n, n, STEP, rows)
        swaps.append(
            link.send(rows_of(swap_buf, i * n, n), rows_of(inp, i * n, n), place.swap, place.away)
        )
    hop_copies = [link.send(sum_own[0], sum_got[0], hops[0])]

    def next_hop(s):
        hop_copies[s].wait_recv()
        into = small if s + 1 == steps else sum_own[s + 1]
        into[...] = sum_own[s][...] + sum_got[s][...]
        if s + 1 < steps:
            hop_copies.append(link.send(sum_own[s + 1], sum_got[s + 1], hops[s + 1]))

    chain = [one.join for one in groups[0]] + [None]
    for s in range(bits):
        chain += [one.advance for one in double] + [None] + [one.advance for one in groups[0]]
        chain += [one.advance if s else one.join for group in groups[1:] for one in group] + [None]
    chain += [one.advance for group in groups[1:] for one in group]

    def put(some, src, dst):
        for one in some:
            for copy in one.cores:
                arrive(copy, place.away)
        stores.keep(src, dst)

    last = len(chain) - 1 - chain[::-1].index(double[1].advance)
    chain.insert(last + 2, lambda: put(double[1:], full_d, out_d))
    chain.insert(last + 2, lambda: put(double[:1], full_u, out_u))
    hop = 0
    for act in chain + [None] * steps:
        if act is not None:
            act()
        elif hop < steps:
            next_hop(hop)
            hop += 1
    put([one for group in groups for one in group], full_a, out_a)
    for copy in swaps:
        arrive(copy, place.away)
    stores.drain()
    link.close()


def any_space():
    return pl.BlockSpec(memory_space=pl.ANY)


SEMS = 160


def sems(local=24):
    return [
        pltpu.SemaphoreType.DMA((SEMS,)),
        pltpu.SemaphoreType.DMA((SEMS,)),
        pltpu.SemaphoreType.DMA((local,)),
    ]


def remote_call(name, kernel, number, outs, in_specs, scratch, away=()):
    return pl.pallas_call(
        kernel,
        out_shape=outs,
        in_specs=in_specs,
        out_specs=tuple(any_space() if j in away else vmem() for j in range(len(outs))),
        scratch_shapes=scratch + sems(),
        compiler_params=pltpu.CompilerParams(
            collective_id=number, has_side_effects=True, vmem_limit_bytes=62 << 20
        ),
        name=name,
    )


def held_like(arrays):
    return [pltpu.VMEM(x.shape, x.dtype) for x in arrays]


def shaped(shape, dtype):
    return jax.ShapeDtypeStruct(shape, dtype)


def like(x):
    return shaped(x.shape, x.dtype)


def enter(columns, hid, cot, ids, qv, ub, wq, wo, *vecs):
    shard, model = hid.shape
    outs = (like(hid), shaped((4 * shard, model), BF), like(cot), like(ids), like(qv), like(ub), like(wq), like(wo))
    call = remote_call(
        "enter", functools.partial(enter_kernel, columns, shard), 0, outs, [any_space()] * 7 + [vmem()] * 2, []
    )
    return call(hid, cot, ids, qv, ub, wq, wo, *vecs)


def make_mid(columns, att, wo, own, vecs, wu, wd, pieces, cot_own, cot_near):
    shard, model = own.shape
    whole = shaped((4 * shard, model), BF)
    outs = (shaped((shard, model), F32), whole, whole, like(wu), like(wd))
    call = remote_call(
        "mid", functools.partial(mid_kernel, columns, shard), 1, outs, [vmem()] * 6 + [any_space()] * 5,
        held_like(outs[1:]) + scatter_scratch(shard, model),
        away=(1, 2, 3, 4),
    )
    return call(att, wo, own, *vecs, wu, wd, pieces, cot_own, cot_near)


def make_back(columns, size, gi, wu, act, wd, grads_u, grads_d, mid, cot, *vecs):
    shard, model = mid.shape
    bits = columns.bit_length() - 1
    outs = (
        shaped((shard, model), F32),
        shaped((4 * shard, model), BF),
        shaped((shard, model), F32),
        shaped((shard, model), BF),
        shaped((2 * (size // columns), model), BF),
        shaped((8, model), F32),
    )
    per_side = halving_scratch(size, bits, model)
    halves = per_side[: bits - 1] + per_side
    call = remote_call(
        "back", functools.partial(back_kernel, columns, shard), 2, outs,
        [vmem()] * 4 + [any_space()] * 2 + [vmem(), any_space(), vmem(), vmem()],
        scatter_scratch(shard, model)
        + scatter_scratch(shard, model)[:2]
        + [pltpu.VMEM((shard, model), BF)]
        + [pltpu.VMEM((size, model), BF)] * 2
        + halves
        + halves,
    )
    return call(gi, wu, act, wd, grads_u, grads_d, mid, cot, *vecs)


def make_exit(columns, size, dq, dk, dv, wq, own, gmid, slices, far, res, res_near, grads, small, vec):
    shard, model = own.shape
    given = (res, res_near, dq, dk, dv, wq, slices, far, gmid, own)
    bits = columns.bit_length() - 1
    outs = (
        shaped((shard, model), BF),
        shaped((shard, model), BF),
        shaped((size, model), BF),
        shaped((size, model), BF),
        shaped((size, model), BF),
        shaped(small.shape, F32),
    )
    halves = []
    for count in groups_of(size // 2, 16 * columns):
        per_side = halving_scratch(count, bits, model)
        halves += (per_side + per_side + [per_side[-1]]) * 2
    steps = bits + 3
    call = remote_call(
        "exit", functools.partial(exit_kernel, columns, shard), 3, outs,
        [any_space()] * 14 + [vmem()] * 2,
        held_like(given)
        + [pltpu.VMEM((size, model), BF)] * 3
        + scatter_scratch(shard, model)
        + [
            pltpu.VMEM((shard, model), BF),
            pltpu.VMEM((shard, model), BF),
            pltpu.VMEM((size, model), BF),
        ]
        + [pltpu.VMEM(small.shape, F32)] * (2 * steps)
        + halves,
        away=(2, 3, 4),
    )
    return call(*given, *grads, small, vec)


def body(
    hidden,
    segment_ids,
    lengths,
    norm1_gain,
    norm1_shift,
    qkv_weight,
    qv_bias,
    out_weight,
    out_bias,
    norm2_gain,
    norm2_shift,
    up_weight,
    up_bias,
    down_weight,
    down_bias,
    cotangent,
):
    _, shard, model = hidden.shape
    seq = segment_ids.shape[1]
    width = qkv_weight.shape[2]
    d, t = lax.axis_index("dp"), lax.axis_index("tensor")
    columns = lax.axis_size("dp") // 2
    rank = 2 * (d & 1) + (t & 1)

    places = jnp.arange(seq, dtype=jnp.int32)
    ids = jnp.where(places < lengths[0], segment_ids[0], 16 + places)
    start = jnp.sum((ids[None, :] < ids[:, None]).astype(jnp.int32), axis=1)
    blocks = seq // BLK
    start = jnp.concatenate([start, start[::BLK] // BLK, jnp.zeros((LANES - blocks,), jnp.int32)])
    start = start[None]

    own, normed1, cot_own, start, b_qv, b_up, w_qkv, w_out = enter(
        columns, hidden[0], cotangent[0], start, qv_bias, up_bias, jnp.swapaxes(qkv_weight, 1, 2), out_weight,
        norm1_gain, norm1_shift,
    )
    everywhere = [(i, j) for i in range(2 * columns) for j in range(4)]
    to_near = [(4 * i + j, 4 * i + (j ^ 1)) for i, j in everywhere]
    to_away = [(4 * i + j, 4 * i + (j ^ 2)) for i, j in everywhere if i % 2 == j // 2]
    to_home = [(4 * i + j, 4 * i + (j ^ 2)) for i, j in everywhere if i % 2 != j // 2]
    axes = ("dp", "tensor")
    unit, rest = pieces_of(up_weight, columns)
    pieces = [lax.dynamic_slice_in_dim(w, (d // 2) * unit, unit, 0) for w in (up_weight, down_weight)]
    pieces += [w[unit * columns :] for w in (up_weight, down_weight)]
    cot_own, pieces, normed1 = lax.optimization_barrier((cot_own, jnp.concatenate(pieces), normed1))
    cot_near = lax.ppermute(cot_own, axes, to_near)
    pieces = lax.ppermute(pieces, axes, to_away)

    meta = jnp.concatenate([rank[None].astype(jnp.int32), start[0, seq : seq + blocks]])

    attended, lse, q, k, v = attn_fwd(meta, start, normed1, w_qkv, b_qv, shard)

    mid, normed2, cot_full, w_up, w_down = make_mid(
        columns,
        attended,
        w_out,
        own,
        (out_bias, norm2_gain, norm2_shift),
        up_weight,
        down_weight,
        pieces,
        cot_own,
        cot_near,
    )
    inner = mm(normed2, w_up) + b_up
    c0 = math.sqrt(2.0 / math.pi)
    tanh = jnp.tanh(c0 * (inner + 0.044715 * inner * inner * inner))
    active = (0.5 * inner * (1.0 + tanh)).astype(BF)
    slope = 0.5 * (1.0 + tanh) + 0.5 * inner * (1.0 - tanh * tanh) * c0 * (
        1.0 + 3 * 0.044715 * inner * inner
    )
    grad_inner = (mm_nt(cot_full, w_down) * slope).astype(BF)
    unit = 32 * columns
    size = -(-model // unit) * unit
    grad_mid, gm_full, res, res_near, slices, sums = make_back(
        columns,
        size,
        grad_inner,
        w_up,
        active,
        w_down,
        mm_tn(normed2, grad_inner).astype(BF),
        mm_tn(active, cot_full).astype(BF),
        mid,
        cot_full,
        norm2_gain,
        down_bias,
    )
    far = lax.ppermute(slices, axes, to_home)
    res_near = lax.ppermute(res_near, axes, to_near)
    dq, dk, dv = attn_bwd(meta, start, q, k, v, attended, gm_full, w_out, lse, shard)
    far, dk, dv = lax.optimization_barrier((far, dk, dv))
    res_near, dq = lax.optimization_barrier((res_near, dq))
    att_grads = [
        mm_tn(dq, normed1).astype(BF),
        mm_tn(dk, normed1).astype(BF),
        mm_tn(dv, normed1).astype(BF),
        mm_tn(attended, gm_full).astype(BF),
    ]

    qv_grad = jnp.concatenate([jnp.sum(dq, axis=0, dtype=F32), jnp.sum(dv, axis=0, dtype=F32)])
    qv_grad = jnp.pad(qv_grad, (0, model - 2 * width))
    up_b_grad = jnp.sum(grad_inner, axis=0, dtype=F32)
    slots = lax.broadcasted_iota(jnp.int32, (4, 1), 0) == rank
    small = jnp.concatenate(
        [
            jnp.zeros((2, model), F32),
            sums[:4],
            jnp.zeros((2, model), F32),
            jnp.where(slots, up_b_grad[None], 0.0),
            jnp.where(slots, qv_grad[None], 0.0),
        ]
    )
    input_grad, output, up_grad, down_grad, att_grad, small = make_exit(
        columns,
        size,
        dq,
        dk,
        dv,
        w_qkv,
        own,
        grad_mid,
        slices,
        far,
        res,
        res_near,
        att_grads,
        small,
        norm1_gain,
    )
    quarter = lax.dynamic_slice_in_dim(small, 12 + t, 1, 0)[0, : 2 * width].reshape(2, width)
    att_grad = att_grad.reshape(4, size // 4, model)
    qkv_grad = att_grad[:3, :width].astype(F32)
    return (
        output[None],
        input_grad[None],
        small[0],
        small[1],
        jnp.swapaxes(qkv_grad, 1, 2),
        quarter,
        att_grad[3, :width].astype(F32),
        small[2],
        small[3],
        small[4],
        up_grad[:model].astype(F32),
        lax.dynamic_slice_in_dim(small, 8 + t, 1, 0)[0],
        down_grad[:model].astype(F32),
        small[5],
    )


def solution(mesh):
    in_specs = (
        P("dp", "tensor", None),
        P("dp", None),
        P("dp"),
        P(),
        P(),
        P(None, None, "tensor"),
        P(None, "tensor"),
        P("tensor", None),
        P(),
        P(),
        P(),
        P(None, "tensor"),
        P("tensor"),
        P("tensor", None),
        P(),
        P("dp", "tensor", None),
    )
    out_specs = (
        P("dp", "tensor", None),
        P("dp", "tensor", None),
        P(),
        P(),
        P(None, None, "tensor"),
        P(None, "tensor"),
        P("tensor", None),
        P(),
        P(),
        P(),
        P(None, "tensor"),
        P("tensor"),
        P("tensor", None),
        P(),
    )
    return jax.shard_map(body, mesh=mesh, in_specs=in_specs, out_specs=out_specs, check_vma=False)
```

```python
import functools
import math

import jax
import jax.numpy as jnp
from jax import lax
from jax.experimental import pallas as pl
from jax.experimental.pallas import tpu as pltpu
from jax.sharding import PartitionSpec as P

HEAD = 56
EPS = 1e-05
LANES = 128
BLK = 256
BF = jnp.bfloat16
F32 = jnp.float32


def mm(a, b):
    return jnp.dot(a, b, preferred_element_type=F32)


def mm_nt(a, b):
    return lax.dot_general(a, b, (((1,), (1,)), ((), ())), preferred_element_type=F32)


def mm_tn(a, b):
    return lax.dot_general(a, b, (((0,), (0,)), ((), ())), preferred_element_type=F32)


def head_window(h):
    lo, hi = h * HEAD, (h + 1) * HEAD
    first = lo // LANES * LANES
    last = -(-hi // LANES) * LANES
    return first, last


def head_mask(h, rows):
    first, last = head_window(h)
    lane = lax.broadcasted_iota(jnp.int32, (rows, last - first), 1) + first
    return (lane >= h * HEAD) & (lane < (h + 1) * HEAD)


def stage_in(rank, src, dst, shard, width):
    wide = dst.shape[1]
    for s in range(src.shape[0] // shard):
        rel = pl.multiple_of((rank ^ s) * shard, 16)
        dst[s * shard : (s + 1) * shard, :width] = src[pl.ds(rel, shard), :]
    if wide > width:
        dst[:, width:] = jnp.zeros((dst.shape[0], wide - width), dst.dtype)


def project(rank, src, shard, width, products):
    @pl.loop(0, src.shape[0] // shard)
    def _(s):
        rel = pl.multiple_of((rank ^ s) * shard, 16)
        rows = pl.ds(pl.multiple_of(s * shard, 16), shard)
        x = src[pl.ds(rel, shard), :]
        for dst, weight, bias in products:
            value = dot_nt(x, weight[...])
            if bias is not None:
                value = value + bias
            dst[rows, :width] = value.astype(BF)

    for dst, _, _ in products:
        if dst.shape[1] > width:
            dst[:, width:] = jnp.zeros((dst.shape[0], dst.shape[1] - width), BF)


def stage_out(rank, src, dst, shard, width):
    for s in range(dst.shape[0] // shard):
        rel = pl.multiple_of((rank ^ s) * shard, 16)
        dst[pl.ds(rel, shard), :] = src[s * shard : (s + 1) * shard, :width]


def tile_mask(start_row, qb, kb):
    kpos = kb * BLK + lax.broadcasted_iota(jnp.int32, (BLK, BLK), 0)
    qpos = qb * BLK + lax.broadcasted_iota(jnp.int32, (BLK, BLK), 1)
    return (kpos <= qpos) & (kpos >= start_row)


def dot_nt(a, b):
    return lax.dot_general(a, b, (((1,), (1,)), ((), ())), preferred_element_type=F32)


def attn_fwd_kernel(heads, shard, meta, start, normed, wq, bias, out, lse, qs, ks, vs, vt, os, ot, ms, ls, acc):
    seq, width = out.shape
    scale2 = HEAD ** (-0.5) * math.log2(math.e)
    rank = meta[0]
    b_q, b_v = bias[0:1, :], bias[1:2, :]
    project(
        rank, normed, shard, width, [(qs, wq.at[0], b_q), (ks, wq.at[1], None), (vs, wq.at[2], b_v)]
    )
    blocks = seq // BLK

    @pl.loop(0, blocks)
    def _(b):
        rows = pl.ds(pl.multiple_of(b * BLK, BLK), BLK)
        flipped = vs[rows, :].astype(F32).T
        for h in range(heads):
            vt[h, :, rows] = flipped[h * HEAD : (h + 1) * HEAD, :].astype(BF)

    lse[...] = jnp.zeros_like(lse)

    @pl.loop(0, blocks)
    def _(b):
        rows = pl.ds(pl.multiple_of(b * BLK, BLK), BLK)
        start_row = start[0:1, rows]
        ms[...] = jnp.full_like(ms, -1e30)
        ls[...] = jnp.zeros_like(ls)
        acc[...] = jnp.zeros_like(acc)

        def tile(kb, carry):
            krows = pl.ds(pl.multiple_of(kb * BLK, BLK), BLK)
            mask = tile_mask(start_row, b, kb)
            for h in range(heads):
                first, last = head_window(h)
                qm = jnp.where(head_mask(h, BLK), qs[rows, first:last], 0)
                s = dot_nt(ks[krows, first:last], qm) * scale2
                s = jnp.where(mask, s, -1e30)
                old = ms[h : h + 1, :]
                new = jnp.maximum(old, jnp.max(s, axis=0, keepdims=True))
                p = jnp.exp2(s - new)
                p = jnp.where(mask, p, 0.0)
                fade = jnp.exp2(old - new)
                ms[h : h + 1, :] = new
                ls[h : h + 1, :] = ls[h : h + 1, :] * fade + jnp.sum(p, axis=0, keepdims=True)
                acc[h] = acc[h] * fade + jnp.dot(
                    vt[h, :, krows], p.astype(BF), preferred_element_type=F32
                )
            return carry

        lax.fori_loop(meta[1 + b], b + 1, tile, 0)
        for h in range(heads):
            total = ls[h : h + 1, :]
            lse[h : h + 1, rows] = ms[h : h + 1, :] + jnp.log(total) * math.log2(math.e)
            ot[h * HEAD : (h + 1) * HEAD, :] = acc[h] / total
        os[rows, :] = ot[...].T.astype(BF)

    stage_out(rank, os, out, shard, width)


def attn_bwd_kernel(
    heads, shard, meta, start, qs, ks, vs, o, gm, wo, lse, dq, dk, dv,
    os, dos, kt, delta, dqs, dks, dvs, dqt, qm, dm,
):
    seq, width = o.shape
    scale = HEAD ** (-0.5)
    scale2 = scale * math.log2(math.e)
    rank = meta[0]
    blocks = seq // BLK
    stage_in(rank, o, os, shard, width)
    project(rank, gm, shard, width, [(dos, wo, None)])

    @pl.loop(0, blocks)
    def _(b):
        rows = pl.ds(pl.multiple_of(b * BLK, BLK), BLK)
        flipped = (os[rows, :].astype(F32) * dos[rows, :].astype(F32)).T
        for h in range(heads):
            delta[h : h + 1, rows] = jnp.sum(
                flipped[h * HEAD : (h + 1) * HEAD, :], axis=0, keepdims=True
            )

    @pl.loop(0, blocks)
    def _(b):
        rows = pl.ds(pl.multiple_of(b * BLK, BLK), BLK)
        flipped = ks[rows, :].astype(F32).T
        for h in range(heads):
            kt[h, :, rows] = flipped[h * HEAD : (h + 1) * HEAD, :].astype(BF)

    dks[...] = jnp.zeros_like(dks)
    dvs[...] = jnp.zeros_like(dvs)
    dqt[...] = jnp.zeros_like(dqt)

    @pl.loop(0, blocks)
    def _(b):
        rows = pl.ds(pl.multiple_of(b * BLK, BLK), BLK)
        start_row = start[0:1, rows]
        dqt[...] = jnp.zeros_like(dqt)
        for h in range(heads):
            first, last = head_window(h)
            keep = head_mask(h, BLK)
            qm[h, :, : last - first] = jnp.where(keep, qs[rows, first:last], 0)
            dm[h, :, : last - first] = jnp.where(keep, dos[rows, first:last], 0)

        def tile(kb, carry):
            krows = pl.ds(pl.multiple_of(kb * BLK, BLK), BLK)
            mask = tile_mask(start_row, b, kb)
            for h in range(heads):
                first, last = head_window(h)
                qh = qm[h, :, : last - first]
                dh = dm[h, :, : last - first]
                s = dot_nt(ks[krows, first:last], qh) * scale2
                p = jnp.where(mask, jnp.exp2(s - lse[h : h + 1, rows]), 0.0)
                dp = dot_nt(vs[krows, first:last], dh)
                ds = (p * (dp - delta[h : h + 1, rows])).astype(BF)
                dvs[krows, first:last] += jnp.dot(p.astype(BF), dh, preferred_element_type=F32)
                dks[krows, first:last] += jnp.dot(ds, qh, preferred_element_type=F32)
                dqt[h * HEAD : (h + 1) * HEAD, :] += jnp.dot(
                    kt[h, :, krows], ds, preferred_element_type=F32
                )
            return carry

        lax.fori_loop(meta[1 + b], b + 1, tile, 0)
        dqs[rows, :] = (dqt[...].T * scale).astype(BF)

    stage_out(rank, dqs, dq, shard, width)
    for s in range(seq // shard):
        rel = pl.multiple_of((rank ^ s) * shard, 16)
        here = slice(s * shard, (s + 1) * shard)
        dk[pl.ds(rel, shard), :] = (dks[here, :width] * scale).astype(BF)
        dv[pl.ds(rel, shard), :] = dvs[here, :width].astype(BF)


def vmem():
    return pl.BlockSpec(memory_space=pltpu.VMEM)


def smem():
    return pl.BlockSpec(memory_space=pltpu.SMEM)


def attn_cost(seq, width, products):
    return pl.CostEstimate(
        flops=products * seq * seq * width,
        bytes_accessed=8 * seq * width * 2,
        transcendentals=seq * seq * width // (2 * HEAD),
    )


def attn_fwd(meta, start, normed, wq, bias, shard):
    seq, (_, width, _) = normed.shape[0], wq.shape
    heads = width // HEAD
    wide = -(-width // LANES) * LANES
    staged = jax.ShapeDtypeStruct((seq, wide), BF)
    return pl.pallas_call(
        functools.partial(attn_fwd_kernel, heads, shard),
        out_shape=(
            jax.ShapeDtypeStruct((seq, width), BF),
            jax.ShapeDtypeStruct((8, seq), F32),
            staged,
            staged,
            staged,
        ),
        in_specs=[smem()] + [vmem()] * 4,
        out_specs=(vmem(),) * 5,
        scratch_shapes=[
            pltpu.VMEM((heads, HEAD, seq), BF),
            pltpu.VMEM((seq, wide), BF),
            pltpu.VMEM((wide, BLK), F32),
            pltpu.VMEM((8, BLK), F32),
            pltpu.VMEM((8, BLK), F32),
            pltpu.VMEM((heads, HEAD, BLK), F32),
        ],
        cost_estimate=attn_cost(seq, width, 3),
        name="attn_fwd",
    )(meta, start, normed, wq, bias)


def attn_bwd(meta, start, q, k, v, o, gm, wo, lse, shard):
    seq, width = o.shape
    heads = width // HEAD
    wide = q.shape[1]
    grad = jax.ShapeDtypeStruct((seq, width), BF)
    return pl.pallas_call(
        functools.partial(attn_bwd_kernel, heads, shard),
        out_shape=(grad, grad, grad),
        in_specs=[smem()] + [vmem()] * 8,
        out_specs=(vmem(), vmem(), vmem()),
        scratch_shapes=[
            pltpu.VMEM((seq, wide), BF),
            pltpu.VMEM((seq, wide), BF),
            pltpu.VMEM((heads, HEAD, seq), BF),
            pltpu.VMEM((8, seq), F32),
            pltpu.VMEM((seq, wide), BF),
            pltpu.VMEM((seq, wide), F32),
            pltpu.VMEM((seq, wide), F32),
            pltpu.VMEM((wide, BLK), F32),
            pltpu.VMEM((heads, BLK, 2 * LANES), BF),
            pltpu.VMEM((heads, BLK, 2 * LANES), BF),
        ],
        cost_estimate=attn_cost(seq, width, 8),
        name="attn_bwd",
    )(meta, start, q, k, v, o, gm, wo, lse)


MESH = pl.DeviceIdType.MESH
CHUNKS = 2
STEP = 32


class Place:
    def __init__(self, columns):
        d, t = lax.axis_index("dp"), lax.axis_index("tensor")
        core, low, high = lax.rem(d, 2), lax.rem(t, 2), lax.div(t, 2)
        self.d, self.t, self.columns = d, t, columns
        self.bits = columns.bit_length() - 1
        self.core = (d + 1 - 2 * core, t)
        self.near = (d, t + 1 - 2 * low)
        self.far = (d, t + 2 - 4 * high)
        self.swap = (d + 1 - 2 * core, t + 2 - 4 * high)
        self.home = core == high
        self.away = core != high

    def bit(self, b):
        return lax.rem(lax.div(self.d, 2 << b), 2)

    def column(self, m):
        d = self.d
        for b in range(self.bits):
            if (m >> b) & 1:
                d = d + (2 << b) * (1 - 2 * self.bit(b))
        return (d, self.t)


class Link:
    def __init__(self, send_sems, recv_sems):
        self.send_sems, self.recv_sems = send_sems, recv_sems
        self.count = 0
        self.open, self.kept, self.number = [], [], {}

    def make(self, src, dst, to, like=None):
        if like is None:
            i = self.count
            self.count += 1
        else:
            i = self.number[id(like)]
        copy = pltpu.make_async_remote_copy(
            src_ref=src,
            dst_ref=dst,
            send_sem=self.send_sems.at[i],
            recv_sem=self.recv_sems.at[i],
            device_id=to,
            device_id_type=MESH,
        )
        self.number[id(copy)] = i
        self.kept.append(copy)
        return copy

    def start(self, copy, when=None):
        if when is None:
            copy.start()
        else:
            pl.when(when)(copy.start)
        self.open.append((copy, when))

    def send(self, src, dst, to, when=None):
        copy = self.make(src, dst, to)
        self.start(copy, when)
        return copy

    def close(self):
        for copy, when in self.open:
            if when is None:
                copy.wait_send()
            else:
                pl.when(when)(copy.wait_send)


def arrive(copy, when=None):
    if when is None:
        copy.wait_recv()
    else:
        pl.when(when)(copy.wait_recv)


def meet(partners):
    barrier = pltpu.get_barrier_semaphore()
    for to in partners:
        pl.semaphore_signal(barrier, inc=1, device_id=to, device_id_type=MESH)
    pl.semaphore_wait(barrier, len(partners))


def row_of(ref):
    return ref[...][None, :]


def rows_of(ref, first, count):
    return ref.at[pl.ds(first, count)]


def gather_start(link, place, full, shard, i):
    n = shard // CHUNKS
    near = link.send(rows_of(full, i * n, n), rows_of(full, shard + i * n, n), place.near)
    core = link.send(rows_of(full, i * n, n), rows_of(full, 2 * shard + i * n, n), place.core)
    return near, core


def gather_relay(link, place, full, shard, i, near):
    n = shard // CHUNKS
    near.wait_recv()
    return link.send(
        rows_of(full, shard + i * n, n), rows_of(full, 3 * shard + i * n, n), place.core
    )


class Scatter:
    def __init__(self, link, place, make, part, core_buf, out_buf, near_buf, shard):
        self.link, self.place, self.make, self.part = link, place, make, part
        self.core_buf, self.out_buf, self.near_buf = core_buf, out_buf, near_buf
        self.shard, self.n = shard, shard // CHUNKS
        self.core, self.near = {}, {}

    def fill(self, block):
        rows = pl.ds(pl.multiple_of(block * self.shard, 16), self.shard)
        self.part[rows, :] = self.make(rows).astype(BF)

    def to_core(self, block):
        for i in range(CHUNKS):
            at = (block - 2) * self.shard + i * self.n
            self.core[block - 2, i] = self.link.send(
                rows_of(self.part, 2 * self.shard + at, self.n),
                rows_of(self.core_buf, at, self.n),
                self.place.core,
            )

    def start(self):
        self.fill(3)
        self.to_core(3)
        self.fill(1)

    def rest(self):
        @pl.loop(0, 2)
        def _(b):
            self.fill(2 - 2 * b)

        self.to_core(2)

    def pass_on(self, i):
        at = self.shard + i * self.n
        self.core[1, i].wait_recv()

        @pl.loop(0, self.n // STEP)
        def _(r):
            here = pl.multiple_of(at + r * STEP, STEP)
            there = pl.multiple_of(i * self.n + r * STEP, STEP)
            total = self.part[pl.ds(here, STEP), :].astype(F32) + self.core_buf[
                pl.ds(here, STEP), :
            ].astype(F32)
            self.out_buf[pl.ds(there, STEP), :] = total.astype(BF)

        self.near[i] = self.link.send(
            rows_of(self.out_buf, i * self.n, self.n),
            rows_of(self.near_buf, i * self.n, self.n),
            self.place.near,
        )

    def pair(self, rows):
        return self.part[rows, :].astype(F32) + self.core_buf[rows, :].astype(F32)

    def ready(self, i):
        self.core[0, i].wait_recv()
        self.near[i].wait_recv()

    def rows(self, rows):
        return (
            self.part[rows, :].astype(F32)
            + self.core_buf[rows, :].astype(F32)
            + self.near_buf[rows, :].astype(F32)
        )


class Spread:
    def __init__(self, link, place, src, dst):
        self.link, self.place, self.src, self.dst = link, place, src, dst
        rows = src.shape[-2]
        self.unit = rows // (16 * place.columns) * 16
        self.rest = rows - self.unit * place.columns
        self.at = pl.multiple_of(lax.div(place.d, 2) * self.unit, 16)
        self.pieces, self.shared = [], []

    def move(self, src, at, count, to, when):
        return self.link.send(rows_of(src, at, count), rows_of(self.dst, at, count), to, when)

    def open(self):
        far, home = self.place.far, self.place.home
        if self.unit:
            self.first = self.move(self.src, self.at, self.unit, far, home)
        if self.rest:
            at = self.unit * self.place.columns
            self.pieces.append(self.move(self.src, at, self.rest, far, home))

    def share(self):
        away = self.place.away
        if self.unit:
            arrive(self.first, away)
            for m in range(1, self.place.columns):
                to = self.place.column(m)
                self.pieces.append(self.move(self.dst, self.at, self.unit, to, away))

    def drain(self):
        for copy in self.pieces:
            arrive(copy, self.place.away)


class Local:
    def __init__(self, sems, when=None, base=0):
        self.sems, self.when, self.base, self.copies = sems, when, base, []

    def keep(self, src, dst):
        copy = pltpu.make_async_copy(src, dst, self.sems.at[self.base + len(self.copies)])
        self.copies.append(copy)
        self.run(copy.start)
        return copy

    def run(self, act):
        if self.when is None:
            act()
        else:
            pl.when(self.when)(act)

    def drain(self, first=0):
        for copy in self.copies[first:]:
            self.run(copy.wait)


def pack(local, sources, buf):
    block = buf.shape[0] // len(sources)
    for j, src in enumerate(sources):
        count = src.shape[0]
        local.keep(src, rows_of(buf, j * block, count))
        if count < block:
            buf[j * block + count : (j + 1) * block, :] = jnp.zeros((block - count, buf.shape[1]), buf.dtype)


def scatter_scratch(shard, model):
    return [
        pltpu.VMEM((4 * shard, model), BF),
        pltpu.VMEM((2 * shard, model), BF),
        pltpu.VMEM((shard, model), BF),
        pltpu.VMEM((shard, model), BF),
    ]


def over_rows(first, count, step, fn):
    @pl.loop(0, count // step)
    def _(r):
        fn(pl.ds(pl.multiple_of(first + r * step, 16), step))


class Halving:
    def __init__(self, link, place, source, first, size, turn, work, got):
        self.link, self.place = link, place
        self.source, self.first, self.size = source, first, size
        self.order = [(b + turn) % place.bits for b in range(place.bits)]
        self.work, self.got = work, got
        self.copies = []

    def start(self, s):
        n = self.size >> (s + 1)
        bit = self.place.bit(self.order[s])
        src, base = (self.source, self.first) if s == 0 else (self.work[s - 1], 0)
        at = pl.multiple_of(base + (1 - bit) * n, 16)
        self.copies.append(
            self.link.send(
                rows_of(src, at, n), self.got[s], self.place.column(1 << self.order[s])
            )
        )

    def finish(self, s):
        n = self.size >> (s + 1)
        bit = self.place.bit(self.order[s])
        src, base = (self.source, self.first) if s == 0 else (self.work[s - 1], 0)
        self.copies[s].wait_recv()

        step = step_of(n)

        @pl.loop(0, n // step)
        def _(r):
            here = pl.multiple_of(base + bit * n + r * step, 16)
            to = pl.ds(pl.multiple_of(r * step, 16), step)
            total = src[pl.ds(here, step), :].astype(F32) + self.got[s][to, :].astype(F32)
            self.work[s][to, :] = total.astype(BF)

    def offset(self):
        at, n = 0, self.size
        for b in self.order:
            n //= 2
            at = at + self.place.bit(b) * n
        return self.first + at


def step_of(n):
    return next(step for step in (48, 32, 16) if n % step == 0)


def groups_of(side, unit):
    units = side // unit
    first = max(1, min(units - 1, 2 * units // 3))
    return [count * unit for count in (first, units - first) if count]


def halving_scratch(size, bits, model):
    return [pltpu.VMEM((size >> (s + 1), model), BF) for s in range(bits)]


class Doubling:
    def __init__(self, link, place, half, full, slice_ref, far_buf):
        self.link, self.place, self.half, self.full = link, place, half, full
        self.far = None
        self.slice_ref, self.far_buf = slice_ref, far_buf
        self.n = half.size >> place.bits
        self.at = half.offset()
        self.cores, self.waits = [], []

    def start(self):
        self.far = self.link.send(
            self.slice_ref, self.far_buf, self.place.far, self.place.away
        )

    def to_core(self, at, n):
        self.link.send(
            rows_of(self.full, at, n), rows_of(self.full, at, n), self.place.core, self.place.home
        )

    def join(self):
        if self.far is not None:
            arrive(self.far, self.place.home)

        @pl.when(self.place.home)
        def _():
            step = step_of(self.n)

            @pl.loop(0, self.n // step)
            def _(r):
                here = pl.ds(pl.multiple_of(r * step, 16), step)
                to = pl.ds(pl.multiple_of(self.at + r * step, 16), step)
                total = self.slice_ref[here, :].astype(F32) + self.far_buf[here, :].astype(F32)
                self.full[to, :] = total.astype(BF)

        self.block, self.count = pl.multiple_of(self.at, 16), self.n
        self.stage = 0
        self.push(self.block)

    def push(self, fresh):
        if self.stage < self.place.bits:
            b = self.half.order[self.place.bits - 1 - self.stage]
            self.copy = self.link.send(
                rows_of(self.full, self.block, self.count),
                rows_of(self.full, self.block, self.count),
                self.place.column(1 << b),
                self.place.home,
            )
        copy = self.link.send(
            rows_of(self.full, fresh, self.count if self.stage == 0 else self.count // 2),
            rows_of(self.full, fresh, self.count if self.stage == 0 else self.count // 2),
            self.place.core,
            self.place.home,
        )
        self.cores.append(copy)

    def advance(self):
        b = self.half.order[self.place.bits - 1 - self.stage]
        bit = self.place.bit(b)
        fresh = pl.multiple_of(self.block + (1 - 2 * bit) * self.count, 16)
        arrive(self.copy, self.place.home)
        self.block = pl.multiple_of(self.block - bit * self.count, 16)
        self.count *= 2
        self.stage += 1
        self.push(fresh)


def norm_stats(values):
    center = values - jnp.mean(values, axis=-1, keepdims=True)
    rstd = lax.rsqrt(jnp.mean(center * center, axis=-1, keepdims=True) + EPS)
    return center * rstd, rstd


def norm_pull(grad, hat, rstd, gain):
    gn = grad * gain
    return rstd * (
        gn
        - jnp.mean(gn, axis=-1, keepdims=True)
        - hat * jnp.mean(gn * hat, axis=-1, keepdims=True)
    )


def enter_kernel(
    columns, shard, hid, cot, ids, qv, ub, wq, wo, gain, shift,
    own_out, full_out, cot_out, ids_o, qv_o, ub_o, wq_out, wo_out,
    own, full, cot_own, wq_o, wo_o, send_sems, recv_sems, local_sems,
):
    place, link = Place(columns), Link(send_sems, recv_sems)
    n = shard // CHUNKS
    home, away = place.home, place.away
    meet([place.core, place.near, place.far, place.swap] + [place.column(m) for m in range(1, columns)])
    weights = [Spread(link, place, wq.at[j], wq_o.at[j]) for j in range(wq.shape[0])]
    weights.append(Spread(link, place, wo, wo_o))

    ids_copy = link.send(ids, ids_o, place.swap, away)
    swaps = [
        link.send(rows_of(hid, i * n, n), rows_of(own, i * n, n), place.swap, away) for i in range(CHUNKS)
    ]
    for weight in weights:
        weight.open()
    qv_copy = link.send(qv, qv_o, place.far, home)
    ub_copy = link.send(ub, ub_o, place.far, home)
    local = Local(local_sems, home)
    held = [local.keep(rows_of(hid, i * n, n), rows_of(own, i * n, n)) for i in range(CHUNKS)]
    local.keep(cot, cot_own)
    local.keep(wq, wq_o)
    local.keep(wo, wo_o)
    local.keep(ids, ids_o)
    local.keep(qv, qv_o)
    local.keep(ub, ub_o)

    near, core = {}, []
    for i in range(CHUNKS):
        pl.when(home)(held[i].wait)
        arrive(swaps[i], away)

        def rows(here):
            hat = norm_stats(own[here, :].astype(F32))[0]
            full[here, :] = (hat * row_of(gain) + row_of(shift)).astype(BF)

        over_rows(i * n, n, STEP, rows)
        near[i], copy = gather_start(link, place, full, shard, i)
        core.append(copy)
    cot_copy = link.send(cot, cot_own, place.swap, away)
    for i in range(CHUNKS):
        core.append(gather_relay(link, place, full, shard, i, near[i]))
    for weight in weights:
        weight.share()
    stores = Local(local_sems, None, 8)
    stores.keep(own, own_out)
    for copy in core:
        copy.wait_recv()
    stores.keep(full, full_out)
    for copy in (ids_copy, qv_copy, ub_copy, cot_copy):
        arrive(copy, away)
    local.drain(CHUNKS)
    stores.keep(cot_own, cot_out)
    for weight in weights:
        weight.drain()
    stores.keep(wq_o, wq_out)
    stores.keep(wo_o, wo_out)
    stores.drain()
    link.close()


def mid_kernel(
    columns, shard, att, wo, own, bias, gain, shift, wu, wd, pieces, cot_own, cot_near,
    mid, full_out, cfull_out, wu_out, wd_out, full, cfull, wu_o, wd_o,
    part, core_buf, out_buf, near_buf, send_sems, recv_sems, local_sems
):
    place, link = Place(columns), Link(send_sems, recv_sems)
    n = shard // CHUNKS
    home, away = place.home, place.away
    stores = Local(local_sems, None, 8)
    unit, rest = pieces_of(wu, columns)
    at = pl.multiple_of(lax.div(place.d, 2) * unit, 16)
    mine = Local(local_sems, home, 0)
    mine.keep(wu, wu_o)
    mine.keep(wd, wd_o)
    both = Local(local_sems, None, 2)
    both.keep(cot_own, rows_of(cfull, 0, shard))
    both.keep(cot_near, rows_of(cfull, shard, shard))
    other = Local(local_sems, away, 4)
    for j, out in enumerate((wu_o, wd_o)):
        if unit:
            other.keep(rows_of(pieces, j * unit, unit), rows_of(out, at, unit))
        if rest:
            last = rows_of(pieces, 2 * unit + j * rest, rest)
            other.keep(last, rows_of(out, unit * columns, rest))
    meet([place.core, place.near, place.far] + [place.column(m) for m in range(1, columns)])
    shared = []
    if unit:
        for j, out in enumerate((wu_o, wd_o)):
            for m in range(1, columns):
                src = rows_of(pieces, j * unit, unit)
                shared.append(link.send(src, rows_of(out, at, unit), place.column(m), away))

    def make(rows):
        return mm(att[rows, :], wo[...])

    total = Scatter(link, place, make, part, core_buf, out_buf, near_buf, shard)
    total.start()
    for i in range(CHUNKS):
        total.pass_on(i)
    total.rest()
    core = [
        link.send(cot_own, rows_of(cfull, 2 * shard, shard), place.core),
        link.send(cot_near, rows_of(cfull, 3 * shard, shard), place.core),
    ]
    near = {}
    for i in range(CHUNKS):
        total.ready(i)

        def rows(here):
            value = own[here, :].astype(F32) + total.rows(here) + row_of(bias)
            mid[here, :] = value
            full[here, :] = (norm_stats(value)[0] * row_of(gain) + row_of(shift)).astype(BF)

        over_rows(i * n, n, STEP, rows)
        near[i], copy = gather_start(link, place, full, shard, i)
        core.append(copy)
    for copy in shared:
        arrive(copy, away)
    for local in (mine, both, other):
        local.drain()
    for copy in core[:2]:
        copy.wait_recv()
    stores.keep(wu_o, wu_out)
    stores.keep(wd_o, wd_out)
    stores.keep(cfull, cfull_out)
    for i in range(CHUNKS):
        core.append(gather_relay(link, place, full, shard, i, near[i]))
    stores.keep(rows_of(full, 0, 2 * shard), rows_of(full_out, 0, 2 * shard))
    for copy in core[2:]:
        copy.wait_recv()
    stores.keep(rows_of(full, 2 * shard, 2 * shard), rows_of(full_out, 2 * shard, 2 * shard))
    stores.drain()
    link.close()


def pieces_of(weight, columns):
    rows = weight.shape[0]
    unit = rows // (16 * columns) * 16
    return unit, rows - unit * columns


def back_kernel(
    columns, shard, *refs
):
    place, link = Place(columns), Link(*refs[-3:-1])
    bits = place.bits
    given, (raw_u, raw_d, cot_full, gain, bias), refs = refs[:5], refs[5:10], refs[10:]
    (res_o, near_o, gmid_o, full_o, slices_o), sums = refs[:5], refs[5]
    held, (res, res_near, gmid, full, slices), scratch = refs[6:11], refs[11:16], list(refs[16:-3])
    gi, wu, act, wd, mid = held
    a_bufs, b_bufs = scratch[:4], scratch[4:6]
    cot, grads_u, grads_d = scratch[6:9]
    halves = scratch[9:]
    n = shard // CHUNKS
    local = Local(refs[-1])
    pack(local, [raw_u], grads_u)
    pack(local, [raw_d], grads_d)
    local.keep(rows_of(cot_full, 0, shard), cot)
    loads = Local(refs[-1], None, 3)
    for src, dst in zip(given, held):
        loads.keep(src, dst)
    stores = Local(refs[-1], None, 8)
    meet([place.core, place.near] + [place.column(1 << b) for b in range(bits)])

    def make(rows):
        return mm_nt(gi[rows, :], wu[...])

    def make2(rows):
        return mm(act[rows, :], wd[...])

    total = Scatter(link, place, make, *a_bufs, shard)
    total2 = Scatter(link, place, make2, *b_bufs, None, None, shard)
    size = grads_u.shape[0]
    slice_u, slice_d = (rows_of(slices, j * (size // columns), size // columns) for j in range(2))
    half_u = Halving(
        link, place, grads_u, 0, size, 0, halves[: bits - 1] + [slice_u], halves[bits - 1 : 2 * bits - 1]
    )
    halves = halves[2 * bits - 1 :]
    half_d = Halving(
        link, place, grads_d, 0, size, 1, halves[: bits - 1] + [slice_d], halves[bits - 1 : 2 * bits - 1]
    )
    local.drain()
    half_u.start(0)
    half_d.start(0)
    for copy in loads.copies[:2]:
        copy.wait()
    total.start()
    for i in range(CHUNKS):
        total.pass_on(i)
    total.rest()
    for copy in loads.copies[2:]:
        copy.wait()
    total2.start()
    total2.rest()
    for copy in total2.core.values():
        copy.wait_recv()

    def rows2(here):
        res[here, :] = mid[here, :] + total2.pair(here) + row_of(bias)

    def rows3(here):
        there = pl.ds(pl.multiple_of(here.start - shard, STEP), STEP)
        res_near[there, :] = total2.pair(here).astype(BF)

    over_rows(0, shard, STEP, rows2)
    over_rows(shard, shard, STEP, rows3)
    sums[...] = jnp.zeros_like(sums)
    near, core = {}, []
    for i in range(CHUNKS):
        total.ready(i)

        def rows(here):
            grad = total.rows(here)
            out_grad = cot[here, :].astype(F32)
            hat, rstd = norm_stats(mid[here, :])
            value = out_grad + norm_pull(grad, hat, rstd, row_of(gain))
            gmid[here, :] = value
            full[here, :] = value.astype(BF)
            for row, term in enumerate((value, grad * hat, grad, out_grad)):
                sums[row : row + 1, :] += jnp.sum(term, axis=0, keepdims=True)

        over_rows(i * n, n, STEP, rows)
        near[i], copy = gather_start(link, place, full, shard, i)
        core.append(copy)
    half_u.finish(0)
    half_d.finish(0)
    if bits > 1:
        half_u.start(1)
        half_d.start(1)
    stores.keep(res, res_o)
    stores.keep(res_near, near_o)
    stores.keep(gmid, gmid_o)
    for i in range(CHUNKS):
        core.append(gather_relay(link, place, full, shard, i, near[i]))
    for s in range(1, bits):
        half_u.finish(s)
        if s + 1 < bits:
            half_u.start(s + 1)
        half_d.finish(s)
        if s + 1 < bits:
            half_d.start(s + 1)
    for copy in core:
        copy.wait_recv()
    stores.keep(full, full_o)
    stores.keep(slices, slices_o)
    stores.drain()
    link.close()


def exit_kernel(
    columns, shard, *refs
):
    place, link = Place(columns), Link(*refs[-3:-1])
    bits = place.bits
    given, (gq, gk, gv, go, small_in, gain), refs = refs[:10], refs[10:16], refs[16:]
    inp, out, out_u, out_d, out_a, small = refs[:6]
    held, (full_u, full_d, full_a), scratch = refs[6:16], refs[16:19], list(refs[19:-3])
    res, res_near, dq, dk, dv, wq, slices, far, gmid, own = held
    a_bufs = scratch[:4]
    swap_buf, out_buf, grads_a = scratch[4:7]
    steps = bits + 3
    sum_own, sum_got = scratch[7 : 7 + steps], scratch[7 + steps : 7 + 2 * steps]
    halves = scratch[7 + 2 * steps :]
    n = shard // CHUNKS
    local = Local(refs[-1])
    pack(local, [gq, gk, gv, go], grads_a)
    loads = Local(refs[-1], None, 4)
    for src, dst in zip(given, held):
        loads.keep(src, dst)
    stores = Local(refs[-1], None, 14)
    hops = [place.core] + [place.column(1 << b) for b in range(bits)] + [place.near, place.far]
    meet(hops + [place.swap])
    size = full_u.shape[0]

    def make(rows):
        return mm(dq[rows, :], wq[0]) + mm(dk[rows, :], wq[1]) + mm(dv[rows, :], wq[2])

    total = Scatter(link, place, make, *a_bufs, shard)
    groups, at = [], 0
    for count in groups_of(size // 2, 16 * columns):
        group = []
        for side in range(2):
            half = Halving(
                link, place, grads_a, side * (size // 2) + at, count, side,
                halves[:bits], halves[bits : 2 * bits],
            )
            group.append(Doubling(link, place, half, full_a, half.work[bits - 1], halves[2 * bits]))
            halves = halves[2 * bits + 1 :]
        groups.append(group)
        at += count
    half_u = Halving(link, place, None, 0, size, 0, [], [])
    half_d = Halving(link, place, None, 0, size, 1, [], [])
    part = size // columns
    double = [
        Doubling(link, place, half_u, full_u, rows_of(slices, 0, part), rows_of(far, 0, part)),
        Doubling(link, place, half_d, full_d, rows_of(slices, part, part), rows_of(far, part, part)),
    ]
    local.drain()
    for group in groups:
        for one in group:
            one.half.start(0)

    def finish_out(here):
        value = (res[here, :] + res_near[here, :].astype(F32)).astype(BF)
        out_buf[here, :] = value

        @pl.when(place.home)
        def _():
            out[here, :] = value

    for copy in loads.copies[:2]:
        copy.wait()
    over_rows(0, shard, STEP, finish_out)
    swaps = [link.send(out_buf, out, place.swap, place.away)]
    for copy in loads.copies[2:6]:
        copy.wait()
    total.start()
    for i in range(CHUNKS):
        total.pass_on(i)
    total.rest()
    sum_own[0][...] = small_in[...]
    for s in range(bits):
        for group in groups:
            for one in group:
                one.half.finish(s)
                if s + 1 < bits:
                    one.half.start(s + 1)
                else:
                    one.start()
    for copy in loads.copies[6:]:
        copy.wait()
    for one in double:
        one.join()
    for i in range(CHUNKS):
        total.ready(i)

        def rows(here):
            grad = total.rows(here)
            hat, rstd = norm_stats(own[here, :].astype(F32))
            value = (gmid[here, :] + norm_pull(grad, hat, rstd, row_of(gain))).astype(BF)
            swap_buf[here, :] = value
            for row, term in enumerate((grad * hat, grad)):
                sum_own[0][row : row + 1, :] += jnp.sum(term, axis=0, keepdims=True)

            @pl.when(place.home)
            def _():
                inp[here, :] = value

        over_rows(i * n, n, STEP, rows)
        swaps.append(
            link.send(rows_of(swap_buf, i * n, n), rows_of(inp, i * n, n), place.swap, place.away)
        )
    hop_copies = [link.send(sum_own[0], sum_got[0], hops[0])]

    def next_hop(s):
        hop_copies[s].wait_recv()
        into = small if s + 1 == steps else sum_own[s + 1]
        into[...] = sum_own[s][...] + sum_got[s][...]
        if s + 1 < steps:
            hop_copies.append(link.send(sum_own[s + 1], sum_got[s + 1], hops[s + 1]))

    chain = [one.join for one in groups[0]] + [None]
    for s in range(bits):
        chain += [one.advance for one in double] + [None] + [one.advance for one in groups[0]]
        chain += [one.advance if s else one.join for group in groups[1:] for one in group] + [None]
    chain += [one.advance for group in groups[1:] for one in group]

    def put(some, src, dst):
        for one in some:
            for copy in one.cores:
                arrive(copy, place.away)
        stores.keep(src, dst)

    last = len(chain) - 1 - chain[::-1].index(double[1].advance)
    chain.insert(last + 2, lambda: put(double[1:], full_d, out_d))
    chain.insert(last + 2, lambda: put(double[:1], full_u, out_u))
    hop = 0
    for act in chain + [None] * steps:
        if act is not None:
            act()
        elif hop < steps:
            next_hop(hop)
            hop += 1
    put([one for group in groups for one in group], full_a, out_a)
    for copy in swaps:
        arrive(copy, place.away)
    stores.drain()
    link.close()


def any_space():
    return pl.BlockSpec(memory_space=pl.ANY)


SEMS = 160


def sems(local=24):
    return [
        pltpu.SemaphoreType.DMA((SEMS,)),
        pltpu.SemaphoreType.DMA((SEMS,)),
        pltpu.SemaphoreType.DMA((local,)),
    ]


def remote_call(name, kernel, number, outs, in_specs, scratch, away=()):
    return pl.pallas_call(
        kernel,
        out_shape=outs,
        in_specs=in_specs,
        out_specs=tuple(any_space() if j in away else vmem() for j in range(len(outs))),
        scratch_shapes=scratch + sems(),
        compiler_params=pltpu.CompilerParams(
            collective_id=number, has_side_effects=True, vmem_limit_bytes=62 << 20
        ),
        name=name,
    )


def held_like(arrays):
    return [pltpu.VMEM(x.shape, x.dtype) for x in arrays]


def shaped(shape, dtype):
    return jax.ShapeDtypeStruct(shape, dtype)


def like(x):
    return shaped(x.shape, x.dtype)


def enter(columns, hid, cot, ids, qv, ub, wq, wo, *vecs):
    shard, model = hid.shape
    outs = (like(hid), shaped((4 * shard, model), BF), like(cot), like(ids), like(qv), like(ub), like(wq), like(wo))
    call = remote_call(
        "enter", functools.partial(enter_kernel, columns, shard), 0, outs, [any_space()] * 7 + [vmem()] * 2,
        held_like([outs[j] for j in (0, 1, 2, 6, 7)]), away=(0, 1, 2, 6, 7),
    )
    return call(hid, cot, ids, qv, ub, wq, wo, *vecs)


def make_mid(columns, att, wo, own, vecs, wu, wd, pieces, cot_own, cot_near):
    shard, model = own.shape
    whole = shaped((4 * shard, model), BF)
    outs = (shaped((shard, model), F32), whole, whole, like(wu), like(wd))
    call = remote_call(
        "mid", functools.partial(mid_kernel, columns, shard), 1, outs, [vmem()] * 6 + [any_space()] * 5,
        held_like(outs[1:]) + scatter_scratch(shard, model),
        away=(1, 2, 3, 4),
    )
    return call(att, wo, own, *vecs, wu, wd, pieces, cot_own, cot_near)


def make_back(columns, size, gi, wu, act, wd, grads_u, grads_d, mid, cot, *vecs):
    shard, model = mid.shape
    bits = columns.bit_length() - 1
    given = (gi, wu, act, wd, mid)
    outs = (
        shaped((shard, model), F32),
        shaped((shard, model), BF),
        shaped((shard, model), F32),
        shaped((4 * shard, model), BF),
        shaped((2 * (size // columns), model), BF),
        shaped((8, model), F32),
    )
    per_side = halving_scratch(size, bits, model)
    halves = per_side[: bits - 1] + per_side
    call = remote_call(
        "back", functools.partial(back_kernel, columns, shard), 2, outs,
        [any_space()] * 8 + [vmem()] * 2,
        held_like(given)
        + held_like(outs[:5])
        + scatter_scratch(shard, model)
        + scatter_scratch(shard, model)[:2]
        + [pltpu.VMEM((shard, model), BF)]
        + [pltpu.VMEM((size, model), BF)] * 2
        + halves
        + halves,
        away=range(5),
    )
    return call(*given, grads_u, grads_d, cot, *vecs)


def make_exit(columns, size, dq, dk, dv, wq, own, gmid, slices, far, res, res_near, grads, small, vec):
    shard, model = own.shape
    given = (res, res_near, dq, dk, dv, wq, slices, far, gmid, own)
    bits = columns.bit_length() - 1
    outs = (
        shaped((shard, model), BF),
        shaped((shard, model), BF),
        shaped((size, model), BF),
        shaped((size, model), BF),
        shaped((size, model), BF),
        shaped(small.shape, F32),
    )
    halves = []
    for count in groups_of(size // 2, 16 * columns):
        per_side = halving_scratch(count, bits, model)
        halves += (per_side + per_side + [per_side[-1]]) * 2
    steps = bits + 3
    call = remote_call(
        "exit", functools.partial(exit_kernel, columns, shard), 3, outs,
        [any_space()] * 14 + [vmem()] * 2,
        held_like(given)
        + [pltpu.VMEM((size, model), BF)] * 3
        + scatter_scratch(shard, model)
        + [
            pltpu.VMEM((shard, model), BF),
            pltpu.VMEM((shard, model), BF),
            pltpu.VMEM((size, model), BF),
        ]
        + [pltpu.VMEM(small.shape, F32)] * (2 * steps)
        + halves,
        away=(2, 3, 4),
    )
    return call(*given, *grads, small, vec)


def body(
    hidden,
    segment_ids,
    lengths,
    norm1_gain,
    norm1_shift,
    qkv_weight,
    qv_bias,
    out_weight,
    out_bias,
    norm2_gain,
    norm2_shift,
    up_weight,
    up_bias,
    down_weight,
    down_bias,
    cotangent,
):
    _, shard, model = hidden.shape
    seq = segment_ids.shape[1]
    width = qkv_weight.shape[2]
    d, t = lax.axis_index("dp"), lax.axis_index("tensor")
    columns = lax.axis_size("dp") // 2
    rank = 2 * (d & 1) + (t & 1)

    places = jnp.arange(seq, dtype=jnp.int32)
    ids = jnp.where(places < lengths[0], segment_ids[0], 16 + places)
    start = jnp.sum((ids[None, :] < ids[:, None]).astype(jnp.int32), axis=1)
    blocks = seq // BLK
    start = jnp.concatenate([start, start[::BLK] // BLK, jnp.zeros((LANES - blocks,), jnp.int32)])
    start = start[None]

    own, normed1, cot_own, start, b_qv, b_up, w_qkv, w_out = enter(
        columns, hidden[0], cotangent[0], start, qv_bias, up_bias, jnp.swapaxes(qkv_weight, 1, 2), out_weight,
        norm1_gain, norm1_shift,
    )
    everywhere = [(i, j) for i in range(2 * columns) for j in range(4)]
    to_near = [(4 * i + j, 4 * i + (j ^ 1)) for i, j in everywhere]
    to_away = [(4 * i + j, 4 * i + (j ^ 2)) for i, j in everywhere if i % 2 == j // 2]
    to_home = [(4 * i + j, 4 * i + (j ^ 2)) for i, j in everywhere if i % 2 != j // 2]
    axes = ("dp", "tensor")
    unit, rest = pieces_of(up_weight, columns)
    pieces = [lax.dynamic_slice_in_dim(w, (d // 2) * unit, unit, 0) for w in (up_weight, down_weight)]
    pieces += [w[unit * columns :] for w in (up_weight, down_weight)]
    cot_own, pieces, normed1 = lax.optimization_barrier((cot_own, jnp.concatenate(pieces), normed1))
    cot_near = lax.ppermute(cot_own, axes, to_near)
    pieces = lax.ppermute(pieces, axes, to_away)

    meta = jnp.concatenate([rank[None].astype(jnp.int32), start[0, seq : seq + blocks]])

    attended, lse, q, k, v = attn_fwd(meta, start, normed1, w_qkv, b_qv, shard)

    mid, normed2, cot_full, w_up, w_down = make_mid(
        columns,
        attended,
        w_out,
        own,
        (out_bias, norm2_gain, norm2_shift),
        up_weight,
        down_weight,
        pieces,
        cot_own,
        cot_near,
    )
    inner = mm(normed2, w_up) + b_up
    c0 = math.sqrt(2.0 / math.pi)
    tanh = jnp.tanh(c0 * (inner + 0.044715 * inner * inner * inner))
    active = (0.5 * inner * (1.0 + tanh)).astype(BF)
    slope = 0.5 * (1.0 + tanh) + 0.5 * inner * (1.0 - tanh * tanh) * c0 * (
        1.0 + 3 * 0.044715 * inner * inner
    )
    grad_inner = (mm_nt(cot_full, w_down) * slope).astype(BF)
    unit = 32 * columns
    size = -(-model // unit) * unit
    res, res_near, grad_mid, gm_full, slices, sums = make_back(
        columns,
        size,
        grad_inner,
        w_up,
        active,
        w_down,
        mm_tn(normed2, grad_inner).astype(BF),
        mm_tn(active, cot_full).astype(BF),
        mid,
        cot_full,
        norm2_gain,
        down_bias,
    )
    far = lax.ppermute(slices, axes, to_home)
    res_near = lax.ppermute(res_near, axes, to_near)
    dq, dk, dv = attn_bwd(meta, start, q, k, v, attended, gm_full, w_out, lse, shard)
    far, dk, dv = lax.optimization_barrier((far, dk, dv))
    res_near, dq = lax.optimization_barrier((res_near, dq))
    att_grads = [
        mm_tn(dq, normed1).astype(BF),
        mm_tn(dk, normed1).astype(BF),
        mm_tn(dv, normed1).astype(BF),
        mm_tn(attended, gm_full).astype(BF),
    ]

    qv_grad = jnp.concatenate([jnp.sum(dq, axis=0, dtype=F32), jnp.sum(dv, axis=0, dtype=F32)])
    qv_grad = jnp.pad(qv_grad, (0, model - 2 * width))
    up_b_grad = jnp.sum(grad_inner, axis=0, dtype=F32)
    slots = lax.broadcasted_iota(jnp.int32, (4, 1), 0) == rank
    small = jnp.concatenate(
        [
            jnp.zeros((2, model), F32),
            sums[:4],
            jnp.zeros((2, model), F32),
            jnp.where(slots, up_b_grad[None], 0.0),
            jnp.where(slots, qv_grad[None], 0.0),
        ]
    )
    input_grad, output, up_grad, down_grad, att_grad, small = make_exit(
        columns,
        size,
        dq,
        dk,
        dv,
        w_qkv,
        own,
        grad_mid,
        slices,
        far,
        res,
        res_near,
        att_grads,
        small,
        norm1_gain,
    )
    quarter = lax.dynamic_slice_in_dim(small, 12 + t, 1, 0)[0, : 2 * width].reshape(2, width)
    att_grad = att_grad.reshape(4, size // 4, model)
    qkv_grad = att_grad[:3, :width].astype(F32)
    return (
        output[None],
        input_grad[None],
        small[0],
        small[1],
        jnp.swapaxes(qkv_grad, 1, 2),
        quarter,
        att_grad[3, :width].astype(F32),
        small[2],
        small[3],
        small[4],
        up_grad[:model].astype(F32),
        lax.dynamic_slice_in_dim(small, 8 + t, 1, 0)[0],
        down_grad[:model].astype(F32),
        small[5],
    )


def solution(mesh):
    in_specs = (
        P("dp", "tensor", None),
        P("dp", None),
        P("dp"),
        P(),
        P(),
        P(None, None, "tensor"),
        P(None, "tensor"),
        P("tensor", None),
        P(),
        P(),
        P(),
        P(None, "tensor"),
        P("tensor"),
        P("tensor", None),
        P(),
        P("dp", "tensor", None),
    )
    out_specs = (
        P("dp", "tensor", None),
        P("dp", "tensor", None),
        P(),
        P(),
        P(None, None, "tensor"),
        P(None, "tensor"),
        P("tensor", None),
        P(),
        P(),
        P(),
        P(None, "tensor"),
        P("tensor"),
        P("tensor", None),
        P(),
    )
    return jax.shard_map(body, mesh=mesh, in_specs=in_specs, out_specs=out_specs, check_vma=False)
```

```python
import functools
import math

import jax
import jax.numpy as jnp
from jax import lax
from jax.experimental import pallas as pl
from jax.experimental.pallas import tpu as pltpu
from jax.sharding import PartitionSpec as P

HEAD = 56
EPS = 1e-05
LANES = 128
BLK = 256
BF = jnp.bfloat16
F32 = jnp.float32


def mm(a, b):
    return jnp.dot(a, b, preferred_element_type=F32)


def mm_nt(a, b):
    return lax.dot_general(a, b, (((1,), (1,)), ((), ())), preferred_element_type=F32)


def mm_tn(a, b):
    return lax.dot_general(a, b, (((0,), (0,)), ((), ())), preferred_element_type=F32)


def head_window(h):
    lo, hi = h * HEAD, (h + 1) * HEAD
    first = lo // LANES * LANES
    last = -(-hi // LANES) * LANES
    return first, last


def head_mask(h, rows):
    first, last = head_window(h)
    lane = lax.broadcasted_iota(jnp.int32, (rows, last - first), 1) + first
    return (lane >= h * HEAD) & (lane < (h + 1) * HEAD)


def stage_in(rank, src, dst, shard, width):
    wide = dst.shape[1]
    for s in range(src.shape[0] // shard):
        rel = pl.multiple_of((rank ^ s) * shard, 16)
        dst[s * shard : (s + 1) * shard, :width] = src[pl.ds(rel, shard), :]
    if wide > width:
        dst[:, width:] = jnp.zeros((dst.shape[0], wide - width), dst.dtype)


def project(rank, src, shard, width, products):
    @pl.loop(0, src.shape[0] // shard)
    def _(s):
        rel = pl.multiple_of((rank ^ s) * shard, 16)
        rows = pl.ds(pl.multiple_of(s * shard, 16), shard)
        x = src[pl.ds(rel, shard), :]
        for dst, weight, bias in products:
            value = dot_nt(x, weight[...])
            if bias is not None:
                value = value + bias
            dst[rows, :width] = value.astype(BF)

    for dst, _, _ in products:
        if dst.shape[1] > width:
            dst[:, width:] = jnp.zeros((dst.shape[0], dst.shape[1] - width), BF)


def stage_out(rank, src, dst, shard, width):
    for s in range(dst.shape[0] // shard):
        rel = pl.multiple_of((rank ^ s) * shard, 16)
        dst[pl.ds(rel, shard), :] = src[s * shard : (s + 1) * shard, :width]


def tile_mask(start_row, qb, kb):
    kpos = kb * BLK + lax.broadcasted_iota(jnp.int32, (BLK, BLK), 0)
    qpos = qb * BLK + lax.broadcasted_iota(jnp.int32, (BLK, BLK), 1)
    return (kpos <= qpos) & (kpos >= start_row)


def dot_nt(a, b):
    return lax.dot_general(a, b, (((1,), (1,)), ((), ())), preferred_element_type=F32)


def attn_fwd_kernel(heads, shard, meta, start, normed, wq, bias, out, lse, qs, ks, vs, vt, os, ot, ms, ls, acc):
    seq, width = out.shape
    scale2 = HEAD ** (-0.5) * math.log2(math.e)
    rank = meta[0]
    b_q, b_v = bias[0:1, :], bias[1:2, :]
    project(
        rank, normed, shard, width, [(qs, wq.at[0], b_q), (ks, wq.at[1], None), (vs, wq.at[2], b_v)]
    )
    blocks = seq // BLK

    @pl.loop(0, blocks)
    def _(b):
        rows = pl.ds(pl.multiple_of(b * BLK, BLK), BLK)
        flipped = vs[rows, :].astype(F32).T
        for h in range(heads):
            vt[h, :, rows] = flipped[h * HEAD : (h + 1) * HEAD, :].astype(BF)

    lse[...] = jnp.zeros_like(lse)

    @pl.loop(0, blocks)
    def _(b):
        rows = pl.ds(pl.multiple_of(b * BLK, BLK), BLK)
        start_row = start[0:1, rows]
        ms[...] = jnp.full_like(ms, -1e30)
        ls[...] = jnp.zeros_like(ls)
        acc[...] = jnp.zeros_like(acc)

        def tile(kb, carry):
            krows = pl.ds(pl.multiple_of(kb * BLK, BLK), BLK)
            mask = tile_mask(start_row, b, kb)
            for h in range(heads):
                first, last = head_window(h)
                qm = jnp.where(head_mask(h, BLK), qs[rows, first:last], 0)
                s = dot_nt(ks[krows, first:last], qm) * scale2
                s = jnp.where(mask, s, -1e30)
                old = ms[h : h + 1, :]
                new = jnp.maximum(old, jnp.max(s, axis=0, keepdims=True))
                p = jnp.exp2(s - new)
                p = jnp.where(mask, p, 0.0)
                fade = jnp.exp2(old - new)
                ms[h : h + 1, :] = new
                ls[h : h + 1, :] = ls[h : h + 1, :] * fade + jnp.sum(p, axis=0, keepdims=True)
                acc[h] = acc[h] * fade + jnp.dot(
                    vt[h, :, krows], p.astype(BF), preferred_element_type=F32
                )
            return carry

        lax.fori_loop(meta[1 + b], b + 1, tile, 0)
        for h in range(heads):
            total = ls[h : h + 1, :]
            lse[h : h + 1, rows] = ms[h : h + 1, :] + jnp.log(total) * math.log2(math.e)
            ot[h * HEAD : (h + 1) * HEAD, :] = acc[h] / total
        os[rows, :] = ot[...].T.astype(BF)

    stage_out(rank, os, out, shard, width)


def attn_bwd_kernel(
    heads, shard, meta, start, qs, ks, vs, o, gm, wo, lse, dq, dk, dv,
    os, dos, kt, delta, dqs, dks, dvs, dqt, qm, dm,
):
    seq, width = o.shape
    scale = HEAD ** (-0.5)
    scale2 = scale * math.log2(math.e)
    rank = meta[0]
    blocks = seq // BLK
    stage_in(rank, o, os, shard, width)
    project(rank, gm, shard, width, [(dos, wo, None)])

    @pl.loop(0, blocks)
    def _(b):
        rows = pl.ds(pl.multiple_of(b * BLK, BLK), BLK)
        flipped = (os[rows, :].astype(F32) * dos[rows, :].astype(F32)).T
        for h in range(heads):
            delta[h : h + 1, rows] = jnp.sum(
                flipped[h * HEAD : (h + 1) * HEAD, :], axis=0, keepdims=True
            )

    @pl.loop(0, blocks)
    def _(b):
        rows = pl.ds(pl.multiple_of(b * BLK, BLK), BLK)
        flipped = ks[rows, :].astype(F32).T
        for h in range(heads):
            kt[h, :, rows] = flipped[h * HEAD : (h + 1) * HEAD, :].astype(BF)

    dks[...] = jnp.zeros_like(dks)
    dvs[...] = jnp.zeros_like(dvs)
    dqt[...] = jnp.zeros_like(dqt)

    @pl.loop(0, blocks)
    def _(b):
        rows = pl.ds(pl.multiple_of(b * BLK, BLK), BLK)
        start_row = start[0:1, rows]
        dqt[...] = jnp.zeros_like(dqt)
        for h in range(heads):
            first, last = head_window(h)
            keep = head_mask(h, BLK)
            qm[h, :, : last - first] = jnp.where(keep, qs[rows, first:last], 0)
            dm[h, :, : last - first] = jnp.where(keep, dos[rows, first:last], 0)

        def tile(kb, carry):
            krows = pl.ds(pl.multiple_of(kb * BLK, BLK), BLK)
            mask = tile_mask(start_row, b, kb)
            for h in range(heads):
                first, last = head_window(h)
                qh = qm[h, :, : last - first]
                dh = dm[h, :, : last - first]
                s = dot_nt(ks[krows, first:last], qh) * scale2
                p = jnp.where(mask, jnp.exp2(s - lse[h : h + 1, rows]), 0.0)
                dp = dot_nt(vs[krows, first:last], dh)
                ds = (p * (dp - delta[h : h + 1, rows])).astype(BF)
                dvs[krows, first:last] += jnp.dot(p.astype(BF), dh, preferred_element_type=F32)
                dks[krows, first:last] += jnp.dot(ds, qh, preferred_element_type=F32)
                dqt[h * HEAD : (h + 1) * HEAD, :] += jnp.dot(
                    kt[h, :, krows], ds, preferred_element_type=F32
                )
            return carry

        lax.fori_loop(meta[1 + b], b + 1, tile, 0)
        dqs[rows, :] = (dqt[...].T * scale).astype(BF)

    stage_out(rank, dqs, dq, shard, width)
    for s in range(seq // shard):
        rel = pl.multiple_of((rank ^ s) * shard, 16)
        here = slice(s * shard, (s + 1) * shard)
        dk[pl.ds(rel, shard), :] = (dks[here, :width] * scale).astype(BF)
        dv[pl.ds(rel, shard), :] = dvs[here, :width].astype(BF)


def vmem():
    return pl.BlockSpec(memory_space=pltpu.VMEM)


def smem():
    return pl.BlockSpec(memory_space=pltpu.SMEM)


def attn_cost(seq, width, products):
    return pl.CostEstimate(
        flops=products * seq * seq * width,
        bytes_accessed=8 * seq * width * 2,
        transcendentals=seq * seq * width // (2 * HEAD),
    )


def attn_fwd(meta, start, normed, wq, bias, shard):
    seq, (_, width, _) = normed.shape[0], wq.shape
    heads = width // HEAD
    wide = -(-width // LANES) * LANES
    staged = jax.ShapeDtypeStruct((seq, wide), BF)
    return pl.pallas_call(
        functools.partial(attn_fwd_kernel, heads, shard),
        out_shape=(
            jax.ShapeDtypeStruct((seq, width), BF),
            jax.ShapeDtypeStruct((8, seq), F32),
            staged,
            staged,
            staged,
        ),
        in_specs=[smem()] + [vmem()] * 4,
        out_specs=(vmem(),) * 5,
        scratch_shapes=[
            pltpu.VMEM((heads, HEAD, seq), BF),
            pltpu.VMEM((seq, wide), BF),
            pltpu.VMEM((wide, BLK), F32),
            pltpu.VMEM((8, BLK), F32),
            pltpu.VMEM((8, BLK), F32),
            pltpu.VMEM((heads, HEAD, BLK), F32),
        ],
        cost_estimate=attn_cost(seq, width, 3),
        name="attn_fwd",
    )(meta, start, normed, wq, bias)


def attn_bwd(meta, start, q, k, v, o, gm, wo, lse, shard):
    seq, width = o.shape
    heads = width // HEAD
    wide = q.shape[1]
    grad = jax.ShapeDtypeStruct((seq, width), BF)
    return pl.pallas_call(
        functools.partial(attn_bwd_kernel, heads, shard),
        out_shape=(grad, grad, grad),
        in_specs=[smem()] + [vmem()] * 8,
        out_specs=(vmem(), vmem(), vmem()),
        scratch_shapes=[
            pltpu.VMEM((seq, wide), BF),
            pltpu.VMEM((seq, wide), BF),
            pltpu.VMEM((heads, HEAD, seq), BF),
            pltpu.VMEM((8, seq), F32),
            pltpu.VMEM((seq, wide), BF),
            pltpu.VMEM((seq, wide), F32),
            pltpu.VMEM((seq, wide), F32),
            pltpu.VMEM((wide, BLK), F32),
            pltpu.VMEM((heads, BLK, 2 * LANES), BF),
            pltpu.VMEM((heads, BLK, 2 * LANES), BF),
        ],
        cost_estimate=attn_cost(seq, width, 8),
        name="attn_bwd",
    )(meta, start, q, k, v, o, gm, wo, lse)


MESH = pl.DeviceIdType.MESH
CHUNKS = 2
STEP = 32


class Place:
    def __init__(self, columns):
        d, t = lax.axis_index("dp"), lax.axis_index("tensor")
        core, low, high = lax.rem(d, 2), lax.rem(t, 2), lax.div(t, 2)
        self.d, self.t, self.columns = d, t, columns
        self.bits = columns.bit_length() - 1
        self.core = (d + 1 - 2 * core, t)
        self.near = (d, t + 1 - 2 * low)
        self.far = (d, t + 2 - 4 * high)
        self.swap = (d + 1 - 2 * core, t + 2 - 4 * high)
        self.home = core == high
        self.away = core != high

    def bit(self, b):
        return lax.rem(lax.div(self.d, 2 << b), 2)

    def column(self, m):
        d = self.d
        for b in range(self.bits):
            if (m >> b) & 1:
                d = d + (2 << b) * (1 - 2 * self.bit(b))
        return (d, self.t)


class Link:
    def __init__(self, send_sems, recv_sems):
        self.send_sems, self.recv_sems = send_sems, recv_sems
        self.count = 0
        self.open, self.kept, self.number = [], [], {}

    def make(self, src, dst, to, like=None):
        if like is None:
            i = self.count
            self.count += 1
        else:
            i = self.number[id(like)]
        copy = pltpu.make_async_remote_copy(
            src_ref=src,
            dst_ref=dst,
            send_sem=self.send_sems.at[i],
            recv_sem=self.recv_sems.at[i],
            device_id=to,
            device_id_type=MESH,
        )
        self.number[id(copy)] = i
        self.kept.append(copy)
        return copy

    def start(self, copy, when=None):
        if when is None:
            copy.start()
        else:
            pl.when(when)(copy.start)
        self.open.append((copy, when))

    def send(self, src, dst, to, when=None):
        copy = self.make(src, dst, to)
        self.start(copy, when)
        return copy

    def close(self):
        for copy, when in self.open:
            if when is None:
                copy.wait_send()
            else:
                pl.when(when)(copy.wait_send)


def arrive(copy, when=None):
    if when is None:
        copy.wait_recv()
    else:
        pl.when(when)(copy.wait_recv)


def meet(partners):
    barrier = pltpu.get_barrier_semaphore()
    for to in partners:
        pl.semaphore_signal(barrier, inc=1, device_id=to, device_id_type=MESH)
    pl.semaphore_wait(barrier, len(partners))


def row_of(ref):
    return ref[...][None, :]


def rows_of(ref, first, count):
    return ref.at[pl.ds(first, count)]


def gather_start(link, place, full, shard, i):
    n = shard // CHUNKS
    near = link.send(rows_of(full, i * n, n), rows_of(full, shard + i * n, n), place.near)
    core = link.send(rows_of(full, i * n, n), rows_of(full, 2 * shard + i * n, n), place.core)
    return near, core


def gather_relay(link, place, full, shard, i, near):
    n = shard // CHUNKS
    near.wait_recv()
    return link.send(
        rows_of(full, shard + i * n, n), rows_of(full, 3 * shard + i * n, n), place.core
    )


class Scatter:
    def __init__(self, link, place, make, part, core_buf, out_buf, near_buf, shard):
        self.link, self.place, self.make, self.part = link, place, make, part
        self.core_buf, self.out_buf, self.near_buf = core_buf, out_buf, near_buf
        self.shard, self.n = shard, shard // CHUNKS
        self.core, self.near = {}, {}

    def fill(self, block):
        rows = pl.ds(pl.multiple_of(block * self.shard, 16), self.shard)
        self.part[rows, :] = self.make(rows).astype(BF)

    def to_core(self, block):
        for i in range(CHUNKS):
            at = (block - 2) * self.shard + i * self.n
            self.core[block - 2, i] = self.link.send(
                rows_of(self.part, 2 * self.shard + at, self.n),
                rows_of(self.core_buf, at, self.n),
                self.place.core,
            )

    def start(self):
        self.fill(3)
        self.to_core(3)
        self.fill(1)

    def rest(self):
        @pl.loop(0, 2)
        def _(b):
            self.fill(2 - 2 * b)

        self.to_core(2)

    def pass_on(self, i):
        at = self.shard + i * self.n
        self.core[1, i].wait_recv()

        @pl.loop(0, self.n // STEP)
        def _(r):
            here = pl.multiple_of(at + r * STEP, STEP)
            there = pl.multiple_of(i * self.n + r * STEP, STEP)
            total = self.part[pl.ds(here, STEP), :].astype(F32) + self.core_buf[
                pl.ds(here, STEP), :
            ].astype(F32)
            self.out_buf[pl.ds(there, STEP), :] = total.astype(BF)

        self.near[i] = self.link.send(
            rows_of(self.out_buf, i * self.n, self.n),
            rows_of(self.near_buf, i * self.n, self.n),
            self.place.near,
        )

    def pair(self, rows):
        return self.part[rows, :].astype(F32) + self.core_buf[rows, :].astype(F32)

    def ready(self, i):
        self.core[0, i].wait_recv()
        self.near[i].wait_recv()

    def rows(self, rows):
        return (
            self.part[rows, :].astype(F32)
            + self.core_buf[rows, :].astype(F32)
            + self.near_buf[rows, :].astype(F32)
        )


class Spread:
    def __init__(self, link, place, src, dst):
        self.link, self.place, self.src, self.dst = link, place, src, dst
        rows = src.shape[-2]
        self.unit = rows // (16 * place.columns) * 16
        self.rest = rows - self.unit * place.columns
        self.at = pl.multiple_of(lax.div(place.d, 2) * self.unit, 16)
        self.pieces, self.shared = [], []

    def move(self, src, at, count, to, when):
        return self.link.send(rows_of(src, at, count), rows_of(self.dst, at, count), to, when)

    def open(self):
        far, home = self.place.far, self.place.home
        if self.unit:
            self.first = self.move(self.src, self.at, self.unit, far, home)
        if self.rest:
            at = self.unit * self.place.columns
            self.pieces.append(self.move(self.src, at, self.rest, far, home))

    def share(self):
        away = self.place.away
        if self.unit:
            arrive(self.first, away)
            for m in range(1, self.place.columns):
                to = self.place.column(m)
                self.pieces.append(self.move(self.dst, self.at, self.unit, to, away))

    def drain(self):
        for copy in self.pieces:
            arrive(copy, self.place.away)


class Local:
    def __init__(self, sems, when=None, base=0):
        self.sems, self.when, self.base, self.copies = sems, when, base, []

    def keep(self, src, dst):
        copy = pltpu.make_async_copy(src, dst, self.sems.at[self.base + len(self.copies)])
        self.copies.append(copy)
        self.run(copy.start)
        return copy

    def run(self, act):
        if self.when is None:
            act()
        else:
            pl.when(self.when)(act)

    def drain(self, first=0):
        for copy in self.copies[first:]:
            self.run(copy.wait)


def pack(local, sources, buf):
    block = buf.shape[0] // len(sources)
    for j, src in enumerate(sources):
        count = src.shape[0]
        local.keep(src, rows_of(buf, j * block, count))
        if count < block:
            buf[j * block + count : (j + 1) * block, :] = jnp.zeros((block - count, buf.shape[1]), buf.dtype)


def scatter_scratch(shard, model):
    return [
        pltpu.VMEM((4 * shard, model), BF),
        pltpu.VMEM((2 * shard, model), BF),
        pltpu.VMEM((shard, model), BF),
        pltpu.VMEM((shard, model), BF),
    ]


def over_rows(first, count, step, fn):
    @pl.loop(0, count // step)
    def _(r):
        fn(pl.ds(pl.multiple_of(first + r * step, 16), step))


class Halving:
    def __init__(self, link, place, source, first, size, turn, work, got):
        self.link, self.place = link, place
        self.source, self.first, self.size = source, first, size
        self.order = [(b + turn) % place.bits for b in range(place.bits)]
        self.work, self.got = work, got
        self.copies = []

    def start(self, s):
        n = self.size >> (s + 1)
        bit = self.place.bit(self.order[s])
        src, base = (self.source, self.first) if s == 0 else (self.work[s - 1], 0)
        at = pl.multiple_of(base + (1 - bit) * n, 16)
        self.copies.append(
            self.link.send(
                rows_of(src, at, n), self.got[s], self.place.column(1 << self.order[s])
            )
        )

    def finish(self, s):
        n = self.size >> (s + 1)
        bit = self.place.bit(self.order[s])
        src, base = (self.source, self.first) if s == 0 else (self.work[s - 1], 0)
        self.copies[s].wait_recv()

        step = step_of(n)

        @pl.loop(0, n // step)
        def _(r):
            here = pl.multiple_of(base + bit * n + r * step, 16)
            to = pl.ds(pl.multiple_of(r * step, 16), step)
            total = src[pl.ds(here, step), :].astype(F32) + self.got[s][to, :].astype(F32)
            self.work[s][to, :] = total.astype(BF)

    def offset(self):
        at, n = 0, self.size
        for b in self.order:
            n //= 2
            at = at + self.place.bit(b) * n
        return self.first + at


def step_of(n):
    return next(step for step in (48, 32, 16) if n % step == 0)


def groups_of(side, unit):
    units = side // unit
    first = max(1, min(units - 1, 2 * units // 3))
    return [count * unit for count in (first, units - first) if count]


def halving_scratch(size, bits, model):
    return [pltpu.VMEM((size >> (s + 1), model), BF) for s in range(bits)]


class Doubling:
    def __init__(self, link, place, half, full, slice_ref, far_buf):
        self.link, self.place, self.half, self.full = link, place, half, full
        self.far = None
        self.slice_ref, self.far_buf = slice_ref, far_buf
        self.n = half.size >> place.bits
        self.at = half.offset()
        self.cores, self.waits = [], []

    def start(self):
        self.far = self.link.send(
            self.slice_ref, self.far_buf, self.place.far, self.place.away
        )

    def to_core(self, at, n):
        self.link.send(
            rows_of(self.full, at, n), rows_of(self.full, at, n), self.place.core, self.place.home
        )

    def join(self):
        if self.far is not None:
            arrive(self.far, self.place.home)

        @pl.when(self.place.home)
        def _():
            step = step_of(self.n)

            @pl.loop(0, self.n // step)
            def _(r):
                here = pl.ds(pl.multiple_of(r * step, 16), step)
                to = pl.ds(pl.multiple_of(self.at + r * step, 16), step)
                total = self.slice_ref[here, :].astype(F32) + self.far_buf[here, :].astype(F32)
                self.full[to, :] = total.astype(BF)

        self.block, self.count = pl.multiple_of(self.at, 16), self.n
        self.stage = 0
        self.push(self.block)

    def push(self, fresh):
        if self.stage < self.place.bits:
            b = self.half.order[self.place.bits - 1 - self.stage]
            self.copy = self.link.send(
                rows_of(self.full, self.block, self.count),
                rows_of(self.full, self.block, self.count),
                self.place.column(1 << b),
                self.place.home,
            )
        copy = self.link.send(
            rows_of(self.full, fresh, self.count if self.stage == 0 else self.count // 2),
            rows_of(self.full, fresh, self.count if self.stage == 0 else self.count // 2),
            self.place.core,
            self.place.home,
        )
        self.cores.append(copy)

    def advance(self):
        b = self.half.order[self.place.bits - 1 - self.stage]
        bit = self.place.bit(b)
        fresh = pl.multiple_of(self.block + (1 - 2 * bit) * self.count, 16)
        arrive(self.copy, self.place.home)
        self.block = pl.multiple_of(self.block - bit * self.count, 16)
        self.count *= 2
        self.stage += 1
        self.push(fresh)


def norm_stats(values):
    center = values - jnp.mean(values, axis=-1, keepdims=True)
    rstd = lax.rsqrt(jnp.mean(center * center, axis=-1, keepdims=True) + EPS)
    return center * rstd, rstd


def norm_pull(grad, hat, rstd, gain):
    gn = grad * gain
    return rstd * (
        gn
        - jnp.mean(gn, axis=-1, keepdims=True)
        - hat * jnp.mean(gn * hat, axis=-1, keepdims=True)
    )


def enter_kernel(
    columns, shard, hid, cot, ids, qv, ub, wq, wo, gain, shift,
    own_out, full_out, cot_out, ids_o, qv_o, ub_o, wq_out, wo_out,
    own, full, cot_own, wq_o, wo_o, send_sems, recv_sems, local_sems,
):
    place, link = Place(columns), Link(send_sems, recv_sems)
    n = shard // CHUNKS
    home, away = place.home, place.away
    meet([place.core, place.near, place.far, place.swap] + [place.column(m) for m in range(1, columns)])
    weights = [Spread(link, place, wq.at[j], wq_o.at[j]) for j in range(wq.shape[0])]
    weights.append(Spread(link, place, wo, wo_o))

    ids_copy = link.send(ids, ids_o, place.swap, away)
    swaps = [
        link.send(rows_of(hid, i * n, n), rows_of(own, i * n, n), place.swap, away) for i in range(CHUNKS)
    ]
    local = Local(local_sems, home)
    held = [local.keep(rows_of(hid, i * n, n), rows_of(own, i * n, n)) for i in range(CHUNKS)]
    local.keep(cot, cot_own)
    local.keep(wq, wq_o)
    local.keep(wo, wo_o)
    local.keep(ids, ids_o)
    local.keep(qv, qv_o)
    local.keep(ub, ub_o)

    near, core = {}, []
    for i in range(CHUNKS):
        pl.when(home)(held[i].wait)
        arrive(swaps[i], away)

        def rows(here):
            hat = norm_stats(own[here, :].astype(F32))[0]
            full[here, :] = (hat * row_of(gain) + row_of(shift)).astype(BF)

        over_rows(i * n, n, STEP, rows)
        near[i], copy = gather_start(link, place, full, shard, i)
        core.append(copy)
    for weight in weights:
        weight.open()
    qv_copy = link.send(qv, qv_o, place.far, home)
    ub_copy = link.send(ub, ub_o, place.far, home)
    cot_copy = link.send(cot, cot_own, place.swap, away)
    for i in range(CHUNKS):
        core.append(gather_relay(link, place, full, shard, i, near[i]))
    for weight in weights:
        weight.share()
    stores = Local(local_sems, None, 8)
    stores.keep(own, own_out)
    for copy in core:
        copy.wait_recv()
    stores.keep(full, full_out)
    for copy in (ids_copy, qv_copy, ub_copy, cot_copy):
        arrive(copy, away)
    local.drain(CHUNKS)
    stores.keep(cot_own, cot_out)
    for weight in weights:
        weight.drain()
    stores.keep(wq_o, wq_out)
    stores.keep(wo_o, wo_out)
    stores.drain()
    link.close()


def mid_kernel(
    columns, shard, att, wo, own, bias, gain, shift, wu, wd, pieces, cot_own, cot_near,
    mid, full_out, cfull_out, wu_out, wd_out, full, cfull, wu_o, wd_o,
    part, core_buf, out_buf, near_buf, send_sems, recv_sems, local_sems
):
    place, link = Place(columns), Link(send_sems, recv_sems)
    n = shard // CHUNKS
    home, away = place.home, place.away
    stores = Local(local_sems, None, 8)
    unit, rest = pieces_of(wu, columns)
    at = pl.multiple_of(lax.div(place.d, 2) * unit, 16)
    mine = Local(local_sems, home, 0)
    mine.keep(wu, wu_o)
    mine.keep(wd, wd_o)
    both = Local(local_sems, None, 2)
    both.keep(cot_own, rows_of(cfull, 0, shard))
    both.keep(cot_near, rows_of(cfull, shard, shard))
    other = Local(local_sems, away, 4)
    for j, out in enumerate((wu_o, wd_o)):
        if unit:
            other.keep(rows_of(pieces, j * unit, unit), rows_of(out, at, unit))
        if rest:
            last = rows_of(pieces, 2 * unit + j * rest, rest)
            other.keep(last, rows_of(out, unit * columns, rest))
    meet([place.core, place.near, place.far] + [place.column(m) for m in range(1, columns)])
    shared = []
    if unit:
        for j, out in enumerate((wu_o, wd_o)):
            for m in range(1, columns):
                src = rows_of(pieces, j * unit, unit)
                shared.append(link.send(src, rows_of(out, at, unit), place.column(m), away))

    def make(rows):
        return mm(att[rows, :], wo[...])

    total = Scatter(link, place, make, part, core_buf, out_buf, near_buf, shard)
    total.start()
    for i in range(CHUNKS):
        total.pass_on(i)
    total.rest()
    core = [
        link.send(cot_own, rows_of(cfull, 2 * shard, shard), place.core),
        link.send(cot_near, rows_of(cfull, 3 * shard, shard), place.core),
    ]
    near = {}
    for i in range(CHUNKS):
        total.ready(i)

        def rows(here):
            value = own[here, :].astype(F32) + total.rows(here) + row_of(bias)
            mid[here, :] = value
            full[here, :] = (norm_stats(value)[0] * row_of(gain) + row_of(shift)).astype(BF)

        over_rows(i * n, n, STEP, rows)
        near[i], copy = gather_start(link, place, full, shard, i)
        core.append(copy)
    for copy in shared:
        arrive(copy, away)
    for local in (mine, both, other):
        local.drain()
    for copy in core[:2]:
        copy.wait_recv()
    stores.keep(wu_o, wu_out)
    stores.keep(wd_o, wd_out)
    stores.keep(cfull, cfull_out)
    for i in range(CHUNKS):
        core.append(gather_relay(link, place, full, shard, i, near[i]))
    stores.keep(rows_of(full, 0, 2 * shard), rows_of(full_out, 0, 2 * shard))
    for copy in core[2:]:
        copy.wait_recv()
    stores.keep(rows_of(full, 2 * shard, 2 * shard), rows_of(full_out, 2 * shard, 2 * shard))
    stores.drain()
    link.close()


def pieces_of(weight, columns):
    rows = weight.shape[0]
    unit = rows // (16 * columns) * 16
    return unit, rows - unit * columns


def back_kernel(
    columns, shard, *refs
):
    place, link = Place(columns), Link(*refs[-3:-1])
    bits = place.bits
    given, (raw_u, raw_d, cot_full, gain, bias), refs = refs[:5], refs[5:10], refs[10:]
    (res_o, near_o, gmid_o, full_o, slices_o), sums = refs[:5], refs[5]
    held, (res, res_near, gmid, full, slices), scratch = refs[6:11], refs[11:16], list(refs[16:-3])
    gi, wu, act, wd, mid = held
    a_bufs, b_bufs = scratch[:4], scratch[4:6]
    cot, grads_u, grads_d = scratch[6:9]
    halves = scratch[9:]
    n = shard // CHUNKS
    local = Local(refs[-1])
    pack(local, [raw_u], grads_u)
    pack(local, [raw_d], grads_d)
    local.keep(rows_of(cot_full, 0, shard), cot)
    loads = Local(refs[-1], None, 3)
    for src, dst in zip(given, held):
        loads.keep(src, dst)
    stores = Local(refs[-1], None, 8)
    meet([place.core, place.near] + [place.column(1 << b) for b in range(bits)])

    def make(rows):
        return mm_nt(gi[rows, :], wu[...])

    def make2(rows):
        return mm(act[rows, :], wd[...])

    total = Scatter(link, place, make, *a_bufs, shard)
    total2 = Scatter(link, place, make2, *b_bufs, None, None, shard)
    size = grads_u.shape[0]
    slice_u, slice_d = (rows_of(slices, j * (size // columns), size // columns) for j in range(2))
    half_u = Halving(
        link, place, grads_u, 0, size, 0, halves[: bits - 1] + [slice_u], halves[bits - 1 : 2 * bits - 1]
    )
    halves = halves[2 * bits - 1 :]
    half_d = Halving(
        link, place, grads_d, 0, size, 1, halves[: bits - 1] + [slice_d], halves[bits - 1 : 2 * bits - 1]
    )
    local.drain()
    half_u.start(0)
    half_d.start(0)
    for copy in loads.copies[:2]:
        copy.wait()
    total.start()
    for i in range(CHUNKS):
        total.pass_on(i)
    total.rest()
    for copy in loads.copies[2:]:
        copy.wait()
    total2.start()
    total2.rest()
    for copy in total2.core.values():
        copy.wait_recv()

    def rows2(here):
        res[here, :] = mid[here, :] + total2.pair(here) + row_of(bias)

    def rows3(here):
        there = pl.ds(pl.multiple_of(here.start - shard, STEP), STEP)
        res_near[there, :] = total2.pair(here).astype(BF)

    over_rows(0, shard, STEP, rows2)
    over_rows(shard, shard, STEP, rows3)
    sums[...] = jnp.zeros_like(sums)
    near, core = {}, []
    for i in range(CHUNKS):
        total.ready(i)

        def rows(here):
            grad = total.rows(here)
            out_grad = cot[here, :].astype(F32)
            hat, rstd = norm_stats(mid[here, :])
            value = out_grad + norm_pull(grad, hat, rstd, row_of(gain))
            gmid[here, :] = value
            full[here, :] = value.astype(BF)
            for row, term in enumerate((value, grad * hat, grad, out_grad)):
                sums[row : row + 1, :] += jnp.sum(term, axis=0, keepdims=True)

        over_rows(i * n, n, STEP, rows)
        near[i], copy = gather_start(link, place, full, shard, i)
        core.append(copy)
    half_u.finish(0)
    half_d.finish(0)
    if bits > 1:
        half_u.start(1)
        half_d.start(1)
    stores.keep(res, res_o)
    stores.keep(res_near, near_o)
    stores.keep(gmid, gmid_o)
    for i in range(CHUNKS):
        core.append(gather_relay(link, place, full, shard, i, near[i]))
    for s in range(1, bits):
        half_u.finish(s)
        if s + 1 < bits:
            half_u.start(s + 1)
        half_d.finish(s)
        if s + 1 < bits:
            half_d.start(s + 1)
    for copy in core:
        copy.wait_recv()
    stores.keep(full, full_o)
    stores.keep(slices, slices_o)
    stores.drain()
    link.close()


def exit_kernel(
    columns, shard, *refs
):
    place, link = Place(columns), Link(*refs[-3:-1])
    bits = place.bits
    given, (gq, gk, gv, go, small_in, gain), refs = refs[:10], refs[10:16], refs[16:]
    inp, out, out_u, out_d, out_a, small = refs[:6]
    held, (full_u, full_d, full_a), scratch = refs[6:16], refs[16:19], list(refs[19:-3])
    res, res_near, dq, dk, dv, wq, slices, far, gmid, own = held
    a_bufs = scratch[:4]
    swap_buf, out_buf, grads_a = scratch[4:7]
    steps = bits + 3
    sum_own, sum_got = scratch[7 : 7 + steps], scratch[7 + steps : 7 + 2 * steps]
    halves = scratch[7 + 2 * steps :]
    n = shard // CHUNKS
    local = Local(refs[-1])
    pack(local, [gq, gk, gv, go], grads_a)
    loads = Local(refs[-1], None, 4)
    for src, dst in zip(given, held):
        loads.keep(src, dst)
    stores = Local(refs[-1], None, 14)
    hops = [place.core] + [place.column(1 << b) for b in range(bits)] + [place.near, place.far]
    meet(hops + [place.swap])
    size = full_u.shape[0]

    def make(rows):
        return mm(dq[rows, :], wq[0]) + mm(dk[rows, :], wq[1]) + mm(dv[rows, :], wq[2])

    total = Scatter(link, place, make, *a_bufs, shard)
    groups, at = [], 0
    for count in groups_of(size // 2, 16 * columns):
        group = []
        for side in range(2):
            half = Halving(
                link, place, grads_a, side * (size // 2) + at, count, side,
                halves[:bits], halves[bits : 2 * bits],
            )
            group.append(Doubling(link, place, half, full_a, half.work[bits - 1], halves[2 * bits]))
            halves = halves[2 * bits + 1 :]
        groups.append(group)
        at += count
    half_u = Halving(link, place, None, 0, size, 0, [], [])
    half_d = Halving(link, place, None, 0, size, 1, [], [])
    part = size // columns
    double = [
        Doubling(link, place, half_u, full_u, rows_of(slices, 0, part), rows_of(far, 0, part)),
        Doubling(link, place, half_d, full_d, rows_of(slices, part, part), rows_of(far, part, part)),
    ]
    local.drain()
    for group in groups:
        for one in group:
            one.half.start(0)

    def finish_out(here):
        value = (res[here, :] + res_near[here, :].astype(F32)).astype(BF)
        out_buf[here, :] = value

        @pl.when(place.home)
        def _():
            out[here, :] = value

    for copy in loads.copies[:2]:
        copy.wait()
    over_rows(0, shard, STEP, finish_out)
    swaps = [link.send(out_buf, out, place.swap, place.away)]
    for copy in loads.copies[2:6]:
        copy.wait()
    total.start()
    for i in range(CHUNKS):
        total.pass_on(i)
    total.rest()
    sum_own[0][...] = small_in[...]
    for s in range(bits):
        for group in groups:
            for one in group:
                one.half.finish(s)
                if s + 1 < bits:
                    one.half.start(s + 1)
                else:
                    one.start()
    for copy in loads.copies[6:]:
        copy.wait()
    for one in double:
        one.join()
    for i in range(CHUNKS):
        total.ready(i)

        def rows(here):
            grad = total.rows(here)
            hat, rstd = norm_stats(own[here, :].astype(F32))
            value = (gmid[here, :] + norm_pull(grad, hat, rstd, row_of(gain))).astype(BF)
            swap_buf[here, :] = value
            for row, term in enumerate((grad * hat, grad)):
                sum_own[0][row : row + 1, :] += jnp.sum(term, axis=0, keepdims=True)

            @pl.when(place.home)
            def _():
                inp[here, :] = value

        over_rows(i * n, n, STEP, rows)
        swaps.append(
            link.send(rows_of(swap_buf, i * n, n), rows_of(inp, i * n, n), place.swap, place.away)
        )
    hop_copies = [link.send(sum_own[0], sum_got[0], hops[0])]

    def next_hop(s):
        hop_copies[s].wait_recv()
        into = small if s + 1 == steps else sum_own[s + 1]
        into[...] = sum_own[s][...] + sum_got[s][...]
        if s + 1 < steps:
            hop_copies.append(link.send(sum_own[s + 1], sum_got[s + 1], hops[s + 1]))

    chain = [one.join for one in groups[0]] + [None]
    for s in range(bits):
        chain += [one.advance for one in double] + [None] + [one.advance for one in groups[0]]
        chain += [one.advance if s else one.join for group in groups[1:] for one in group] + [None]
    chain += [one.advance for group in groups[1:] for one in group]

    def put(some, src, dst):
        for one in some:
            for copy in one.cores:
                arrive(copy, place.away)
        stores.keep(src, dst)

    last = len(chain) - 1 - chain[::-1].index(double[1].advance)
    chain.insert(last + 2, lambda: put(double[1:], full_d, out_d))
    chain.insert(last + 2, lambda: put(double[:1], full_u, out_u))
    hop = 0
    for act in chain + [None] * steps:
        if act is not None:
            act()
        elif hop < steps:
            next_hop(hop)
            hop += 1
    put([one for group in groups for one in group], full_a, out_a)
    for copy in swaps:
        arrive(copy, place.away)
    stores.drain()
    link.close()


def any_space():
    return pl.BlockSpec(memory_space=pl.ANY)


SEMS = 160


def sems(local=24):
    return [
        pltpu.SemaphoreType.DMA((SEMS,)),
        pltpu.SemaphoreType.DMA((SEMS,)),
        pltpu.SemaphoreType.DMA((local,)),
    ]


def remote_call(name, kernel, number, outs, in_specs, scratch, away=()):
    return pl.pallas_call(
        kernel,
        out_shape=outs,
        in_specs=in_specs,
        out_specs=tuple(any_space() if j in away else vmem() for j in range(len(outs))),
        scratch_shapes=scratch + sems(),
        compiler_params=pltpu.CompilerParams(
            collective_id=number, has_side_effects=True, vmem_limit_bytes=62 << 20
        ),
        name=name,
    )


def held_like(arrays):
    return [pltpu.VMEM(x.shape, x.dtype) for x in arrays]


def shaped(shape, dtype):
    return jax.ShapeDtypeStruct(shape, dtype)


def like(x):
    return shaped(x.shape, x.dtype)


def enter(columns, hid, cot, ids, qv, ub, wq, wo, *vecs):
    shard, model = hid.shape
    outs = (like(hid), shaped((4 * shard, model), BF), like(cot), like(ids), like(qv), like(ub), like(wq), like(wo))
    call = remote_call(
        "enter", functools.partial(enter_kernel, columns, shard), 0, outs, [any_space()] * 7 + [vmem()] * 2,
        held_like([outs[j] for j in (0, 1, 2, 6, 7)]), away=(0, 1, 2, 6, 7),
    )
    return call(hid, cot, ids, qv, ub, wq, wo, *vecs)


def make_mid(columns, att, wo, own, vecs, wu, wd, pieces, cot_own, cot_near):
    shard, model = own.shape
    whole = shaped((4 * shard, model), BF)
    outs = (shaped((shard, model), F32), whole, whole, like(wu), like(wd))
    call = remote_call(
        "mid", functools.partial(mid_kernel, columns, shard), 1, outs, [vmem()] * 6 + [any_space()] * 5,
        held_like(outs[1:]) + scatter_scratch(shard, model),
        away=(1, 2, 3, 4),
    )
    return call(att, wo, own, *vecs, wu, wd, pieces, cot_own, cot_near)


def make_back(columns, size, gi, wu, act, wd, grads_u, grads_d, mid, cot, *vecs):
    shard, model = mid.shape
    bits = columns.bit_length() - 1
    given = (gi, wu, act, wd, mid)
    outs = (
        shaped((shard, model), F32),
        shaped((shard, model), BF),
        shaped((shard, model), F32),
        shaped((4 * shard, model), BF),
        shaped((2 * (size // columns), model), BF),
        shaped((8, model), F32),
    )
    per_side = halving_scratch(size, bits, model)
    halves = per_side[: bits - 1] + per_side
    call = remote_call(
        "back", functools.partial(back_kernel, columns, shard), 2, outs,
        [any_space()] * 8 + [vmem()] * 2,
        held_like(given)
        + held_like(outs[:5])
        + scatter_scratch(shard, model)
        + scatter_scratch(shard, model)[:2]
        + [pltpu.VMEM((shard, model), BF)]
        + [pltpu.VMEM((size, model), BF)] * 2
        + halves
        + halves,
        away=range(5),
    )
    return call(*given, grads_u, grads_d, cot, *vecs)


def make_exit(columns, size, dq, dk, dv, wq, own, gmid, slices, far, res, res_near, grads, small, vec):
    shard, model = own.shape
    given = (res, res_near, dq, dk, dv, wq, slices, far, gmid, own)
    bits = columns.bit_length() - 1
    outs = (
        shaped((shard, model), BF),
        shaped((shard, model), BF),
        shaped((size, model), BF),
        shaped((size, model), BF),
        shaped((size, model), BF),
        shaped(small.shape, F32),
    )
    halves = []
    for count in groups_of(size // 2, 16 * columns):
        per_side = halving_scratch(count, bits, model)
        halves += (per_side + per_side + [per_side[-1]]) * 2
    steps = bits + 3
    call = remote_call(
        "exit", functools.partial(exit_kernel, columns, shard), 3, outs,
        [any_space()] * 14 + [vmem()] * 2,
        held_like(given)
        + [pltpu.VMEM((size, model), BF)] * 3
        + scatter_scratch(shard, model)
        + [
            pltpu.VMEM((shard, model), BF),
            pltpu.VMEM((shard, model), BF),
            pltpu.VMEM((size, model), BF),
        ]
        + [pltpu.VMEM(small.shape, F32)] * (2 * steps)
        + halves,
        away=(2, 3, 4),
    )
    return call(*given, *grads, small, vec)


def body(
    hidden,
    segment_ids,
    lengths,
    norm1_gain,
    norm1_shift,
    qkv_weight,
    qv_bias,
    out_weight,
    out_bias,
    norm2_gain,
    norm2_shift,
    up_weight,
    up_bias,
    down_weight,
    down_bias,
    cotangent,
):
    _, shard, model = hidden.shape
    seq = segment_ids.shape[1]
    width = qkv_weight.shape[2]
    d, t = lax.axis_index("dp"), lax.axis_index("tensor")
    columns = lax.axis_size("dp") // 2
    rank = 2 * (d & 1) + (t & 1)

    places = jnp.arange(seq, dtype=jnp.int32)
    ids = jnp.where(places < lengths[0], segment_ids[0], 16 + places)
    start = jnp.sum((ids[None, :] < ids[:, None]).astype(jnp.int32), axis=1)
    blocks = seq // BLK
    start = jnp.concatenate([start, start[::BLK] // BLK, jnp.zeros((LANES - blocks,), jnp.int32)])
    start = start[None]

    own, normed1, cot_own, start, b_qv, b_up, w_qkv, w_out = enter(
        columns, hidden[0], cotangent[0], start, qv_bias, up_bias, jnp.swapaxes(qkv_weight, 1, 2), out_weight,
        norm1_gain, norm1_shift,
    )
    everywhere = [(i, j) for i in range(2 * columns) for j in range(4)]
    to_near = [(4 * i + j, 4 * i + (j ^ 1)) for i, j in everywhere]
    to_away = [(4 * i + j, 4 * i + (j ^ 2)) for i, j in everywhere if i % 2 == j // 2]
    to_home = [(4 * i + j, 4 * i + (j ^ 2)) for i, j in everywhere if i % 2 != j // 2]
    axes = ("dp", "tensor")
    unit, rest = pieces_of(up_weight, columns)
    pieces = [lax.dynamic_slice_in_dim(w, (d // 2) * unit, unit, 0) for w in (up_weight, down_weight)]
    pieces += [w[unit * columns :] for w in (up_weight, down_weight)]
    cot_own, pieces, normed1 = lax.optimization_barrier((cot_own, jnp.concatenate(pieces), normed1))
    cot_near = lax.ppermute(cot_own, axes, to_near)
    pieces = lax.ppermute(pieces, axes, to_away)

    meta = jnp.concatenate([rank[None].astype(jnp.int32), start[0, seq : seq + blocks]])

    attended, lse, q, k, v = attn_fwd(meta, start, normed1, w_qkv, b_qv, shard)

    mid, normed2, cot_full, w_up, w_down = make_mid(
        columns,
        attended,
        w_out,
        own,
        (out_bias, norm2_gain, norm2_shift),
        up_weight,
        down_weight,
        pieces,
        cot_own,
        cot_near,
    )
    inner = mm(normed2, w_up) + b_up
    c0 = math.sqrt(2.0 / math.pi)
    tanh = jnp.tanh(c0 * (inner + 0.044715 * inner * inner * inner))
    active = (0.5 * inner * (1.0 + tanh)).astype(BF)
    slope = 0.5 * (1.0 + tanh) + 0.5 * inner * (1.0 - tanh * tanh) * c0 * (
        1.0 + 3 * 0.044715 * inner * inner
    )
    grad_inner = (mm_nt(cot_full, w_down) * slope).astype(BF)
    unit = 32 * columns
    size = -(-model // unit) * unit
    res, res_near, grad_mid, gm_full, slices, sums = make_back(
        columns,
        size,
        grad_inner,
        w_up,
        active,
        w_down,
        mm_tn(normed2, grad_inner).astype(BF),
        mm_tn(active, cot_full).astype(BF),
        mid,
        cot_full,
        norm2_gain,
        down_bias,
    )
    far = lax.ppermute(slices, axes, to_home)
    res_near = lax.ppermute(res_near, axes, to_near)
    dq, dk, dv = attn_bwd(meta, start, q, k, v, attended, gm_full, w_out, lse, shard)
    far, dk, dv = lax.optimization_barrier((far, dk, dv))
    res_near, dq = lax.optimization_barrier((res_near, dq))
    att_grads = [
        mm_tn(dq, normed1).astype(BF),
        mm_tn(dk, normed1).astype(BF),
        mm_tn(dv, normed1).astype(BF),
        mm_tn(attended, gm_full).astype(BF),
    ]

    qv_grad = jnp.concatenate([jnp.sum(dq, axis=0, dtype=F32), jnp.sum(dv, axis=0, dtype=F32)])
    qv_grad = jnp.pad(qv_grad, (0, model - 2 * width))
    up_b_grad = jnp.sum(grad_inner, axis=0, dtype=F32)
    slots = lax.broadcasted_iota(jnp.int32, (4, 1), 0) == rank
    small = jnp.concatenate(
        [
            jnp.zeros((2, model), F32),
            sums[:4],
            jnp.zeros((2, model), F32),
            jnp.where(slots, up_b_grad[None], 0.0),
            jnp.where(slots, qv_grad[None], 0.0),
        ]
    )
    input_grad, output, up_grad, down_grad, att_grad, small = make_exit(
        columns,
        size,
        dq,
        dk,
        dv,
        w_qkv,
        own,
        grad_mid,
        slices,
        far,
        res,
        res_near,
        att_grads,
        small,
        norm1_gain,
    )
    quarter = lax.dynamic_slice_in_dim(small, 12 + t, 1, 0)[0, : 2 * width].reshape(2, width)
    att_grad = att_grad.reshape(4, size // 4, model)
    qkv_grad = att_grad[:3, :width].astype(F32)
    return (
        output[None],
        input_grad[None],
        small[0],
        small[1],
        jnp.swapaxes(qkv_grad, 1, 2),
        quarter,
        att_grad[3, :width].astype(F32),
        small[2],
        small[3],
        small[4],
        up_grad[:model].astype(F32),
        lax.dynamic_slice_in_dim(small, 8 + t, 1, 0)[0],
        down_grad[:model].astype(F32),
        small[5],
    )


def solution(mesh):
    in_specs = (
        P("dp", "tensor", None),
        P("dp", None),
        P("dp"),
        P(),
        P(),
        P(None, None, "tensor"),
        P(None, "tensor"),
        P("tensor", None),
        P(),
        P(),
        P(),
        P(None, "tensor"),
        P("tensor"),
        P("tensor", None),
        P(),
        P("dp", "tensor", None),
    )
    out_specs = (
        P("dp", "tensor", None),
        P("dp", "tensor", None),
        P(),
        P(),
        P(None, None, "tensor"),
        P(None, "tensor"),
        P("tensor", None),
        P(),
        P(),
        P(),
        P(None, "tensor"),
        P("tensor"),
        P("tensor", None),
        P(),
    )
    return jax.shard_map(body, mesh=mesh, in_specs=in_specs, out_specs=out_specs, check_vma=False)
```
